32 devices in a mesh: rep: 4 (over x, core), shard: 8 (over z, y).
Axes of the slice: x: 2, y: 2, z: 4, core: 2. Of those that a mesh axis runs over, the one named last changes fastest.
Arguments:
- tokens: bfloat16 [16384, 1024], P(('rep', 'shard')), may hold values from -6 to 6
- lengths: int32 [32], P(('rep', 'shard')), may hold values from 1 to 512, 12288 in all
- cotangent: bfloat16 [16384, 1024], P(('rep', 'shard')), may hold values from -6 to 6
- norm_gain: bfloat16 [6, 1024], P(None, 'shard'), may hold values from 0.25 to 1.75
- norm_shift: bfloat16 [6, 1024], P(None, 'shard'), may hold values from -2.5 to 2.5
- feed_in: bfloat16 [2, 1024, 4096], P(None, 'shard'), may hold values from -0.1875 to 0.1875
- feed_in_bias: bfloat16 [2, 4096], P(None, 'shard'), may hold values from -2.5 to 2.5
- feed_out: bfloat16 [2, 4096, 1024], P(None, 'shard'), may hold values from -0.09375 to 0.09375
- feed_out_bias: bfloat16 [2, 1024], P(None, 'shard'), may hold values from -2.5 to 2.5
- attention_in: bfloat16 [1024, 3072], P('shard'), may hold values from -0.1875 to 0.1875
- attention_in_bias: bfloat16 [2, 1024], P(None, 'shard'), may hold values from -2.5 to 2.5
- attention_out: bfloat16 [1024, 1024], P('shard'), may hold values from -0.75 to 0.75
- attention_out_bias: bfloat16 [1024], P('shard'), may hold values from -2.5 to 2.5
- relative_table: bfloat16 [73, 64], replicated, may hold values from -6 to 6
- pointwise_in: bfloat16 [1024, 2048], P('shard'), may hold values from -0.1875 to 0.1875
- depthwise: bfloat16 [31, 1024], P(None, 'shard'), may hold values from -1 to 1
- pointwise_out: bfloat16 [1024, 1024], P('shard'), may hold values from -0.1875 to 0.1875
Outputs:
- activations: bfloat16 [16384, 1024], P(('rep', 'shard'))
- tokens_grad: bfloat16 [16384, 1024], P(('rep', 'shard'))
- norm_gain_grad: float32 [6, 1024], P(None, 'shard')
- norm_shift_grad: float32 [6, 1024], P(None, 'shard')
- feed_in_grad: float32 [2, 1024, 4096], P(None, 'shard')
- feed_in_bias_grad: float32 [2, 4096], P(None, 'shard')
- feed_out_grad: float32 [2, 4096, 1024], P(None, 'shard')
- feed_out_bias_grad: float32 [2, 1024], P(None, 'shard')
- attention_in_grad: float32 [1024, 3072], P('shard')
- attention_in_bias_grad: float32 [2, 1024], P(None, 'shard')
- attention_out_grad: float32 [1024, 1024], P('shard')
- attention_out_bias_grad: float32 [1024], P('shard')
- relative_table_grad: float32 [73, 64], replicated
- pointwise_in_grad: float32 [1024, 2048], P('shard')
- depthwise_grad: float32 [31, 1024], P(None, 'shard')
- pointwise_out_grad: float32 [1024, 1024], P('shard')
The draws below stay inside these ranges and needn't reach their ends.
Inputs may be any that keep to these rules, and one draw needn't show every extreme that they name: `lengths`: each device's block holds one clip; its length is the number of live rows at the block's start.
All inputs are finite; a program needn't handle non-finite values.
Results may differ from the reference program's by a relative error of at most 0.02.
Values may be sent and summed in bfloat16 or wider, within the bound.
A program may use at most 320 MiB of HBM per device.

```python
import math
import jax
import jax.numpy as jnp
import numpy as np
from jax import lax

D = 1024
HEADS = 16
HD = 64
FF = 4096
KERNEL = 31
LEFT = 64
RIGHT = 8
TOK_DEV = 512
POS = 73
TOKENS = 16384
DEVICES = 32


def block_levels(own_key, shape, pieces, smallest, largest):
    loudness, own = 1.0, jax.random.fold_in(own_key, 6)
    for axis_at, blocks in pieces:
        steps = jnp.exp(jax.random.uniform(jax.random.fold_in(own, axis_at), (blocks,), jnp.float32, smallest / len(pieces), largest / len(pieces)))
        loudness = loudness * jnp.repeat(steps, shape[axis_at] // blocks).reshape([-1 if axis == axis_at else 1 for axis in range(len(shape))])
    return loudness


def length_profile(amount, total, reach, slope):
    weights = [(1 << 20) // math.isqrt(rank ** slope) + 1 for rank in range(2, amount + 1)]
    rest, given = total - reach - (amount - 1), [1] * (amount - 1)
    while rest > 0:
        free = [i for i in range(amount - 1) if given[i] < reach]
        mass, remaining = sum([weights[i] for i in free]), rest
        for i in free:
            more = min(reach - given[i], max(1, remaining * weights[i] // mass), rest)
            given[i] = given[i] + more
            rest = rest - more
    return np.array([reach] + given)


def uneven(stream_key, count, total, reach, slope):
    if count == 2:
        one = jax.random.randint(stream_key, (), max(1, total - reach), min(reach, total - 1) + 1)
        return jnp.stack([one, total - one])
    sizes = jnp.asarray(length_profile(count, total, reach, slope), jnp.int32)
    twos = (count - 1) // 2
    giver, taker = sizes[1:1 + 2 * twos:2], sizes[2:2 + 2 * twos:2]
    slack = jnp.minimum(giver - 1, reach - taker)
    passed = jax.random.randint(jax.random.fold_in(stream_key, 1), (twos,), 0, 1 << 20) % (slack + 1)
    sizes = sizes.at[1:1 + 2 * twos:2].set(giver - passed).at[2:2 + 2 * twos:2].set(taker + passed)
    return sizes[jax.random.permutation(jax.random.fold_in(stream_key, 2), count)]


def gaussian(stream_key, shape, deviation, reach, shards=(), kind=jnp.bfloat16):
    drawn = jax.random.normal(stream_key, shape, jnp.float32) * deviation
    if len(shards) > 0:
        drawn = block_levels(stream_key, shape, shards, -0.22, 0.18) * drawn
    return jnp.clip(drawn, min=-reach, max=reach).astype(kind)


def setup_inputs(seed: int = 0) -> dict:
    key_list = jax.random.split(jax.random.key(seed), 18)
    return {
        "tokens": gaussian(key_list[0], (TOKENS, D), 1.0, 6.0, ((0, 32),)),
        "lengths": uneven(key_list[1], DEVICES, TOKENS * 3 // 4, TOK_DEV, 2).astype(jnp.int32),
        "cotangent": gaussian(key_list[2], (TOKENS, D), 1.0, 6.0, ((0, 32),)),
        "norm_gain": jnp.clip(1.0 + 0.15 * jax.random.normal(key_list[3], (6, D), jnp.float32), 0.25, 1.75).astype(jnp.bfloat16),
        "norm_shift": gaussian(key_list[4], (6, D), 0.3, 2.5, ((1, 8),)),
        "feed_in": gaussian(key_list[5], (2, D, FF), D ** -0.5, 0.1875, ((1, 8),)),
        "feed_in_bias": gaussian(key_list[6], (2, FF), 0.3, 2.5, ((1, 8),)),
        "feed_out": gaussian(key_list[7], (2, FF, D), FF ** -0.5, 0.09375, ((1, 8),)),
        "feed_out_bias": gaussian(key_list[8], (2, D), 0.3, 2.5, ((1, 8),)),
        "attention_in": gaussian(key_list[9], (D, 3 * D), D ** -0.5, 0.1875, ((0, 8),)),
        "attention_in_bias": gaussian(key_list[10], (2, D), 0.3, 2.5, ((1, 8),)),
        "attention_out": gaussian(key_list[11], (D, D), (D // 16) ** -0.5, 0.75, ((0, 8),)),
        "attention_out_bias": gaussian(key_list[12], (D,), 0.3, 2.5, ((0, 8),)),
        "relative_table": gaussian(key_list[13], (POS, HD), 1.0, 6.0),
        "pointwise_in": gaussian(key_list[14], (D, 2 * D), D ** -0.5, 0.1875, ((0, 8),)),
        "depthwise": gaussian(key_list[15], (KERNEL, D), KERNEL ** -0.5, 1.0, ((1, 8),)),
        "pointwise_out": gaussian(key_list[16], (D, D), D ** -0.5, 0.1875, ((0, 8),)),
    }


@jax.custom_vjp
def low(v):
    return lax.optimization_barrier(v.astype(jnp.bfloat16)).astype(jnp.float32)

@jax.custom_vjp
def low_back(v):
    return v

def low_keep(v):
    return (low(v), None)

def low_pass(kept, grad):
    return (grad,)

def back_keep(v):
    return (v, None)

def back_low(kept, grad):
    return (low(grad),)
low.defvjp(low_keep, low_pass)
low_back.defvjp(back_keep, back_low)

def layer_norm(state, gain, shift):
    center = state - lax.optimization_barrier(jnp.mean(state, axis=-1, keepdims=True))
    spread = lax.optimization_barrier(jnp.mean(center * center, axis=-1, keepdims=True))
    return center * lax.rsqrt(spread + 1e-05) * gain + shift

def product(left, right):
    return jnp.dot(left, right, precision=lax.Precision.HIGHEST)

def causal(signal, kernel):
    steps = signal.shape[0]
    taps = kernel.shape[0]
    padded = jnp.pad(signal, ((taps - 1, 0), (0, 0)))
    total = kernel[0] * padded[0:steps]
    for offset in range(1, taps):
        total = total + kernel[offset] * padded[offset:offset + steps]
    return total

def clip_layer(state, length, params):
    norm_gain, norm_shift, feed_in, feed_in_bias, feed_out, feed_out_bias, attention_in, attention_in_bias, attention_out, attention_out_bias, relative_table, pointwise_in, depthwise, pointwise_out = params
    steps, width = state.shape
    places = jnp.arange(steps, dtype=jnp.int32)
    valid = (places < length).astype(jnp.float32)

    def feed(inputs, norm, layer):
        hidden = low(layer_norm(inputs, norm_gain[norm], norm_shift[norm]))
        pre = low_back(product(hidden, feed_in[layer]) + feed_in_bias[layer])
        active = low(jax.nn.silu(pre))
        return low_back(product(active, feed_out[layer]) + feed_out_bias[layer])
    first = state + 0.5 * feed(state, 0, 0)
    hidden = low(layer_norm(first, norm_gain[1], norm_shift[1]))
    zeros = jnp.zeros((width,), jnp.float32)
    bias_full = jnp.concatenate([attention_in_bias[0], zeros, attention_in_bias[1]])
    packed = low(low_back(product(hidden, attention_in) + bias_full))
    split = packed.reshape(steps, 3, HEADS, HD).transpose(1, 2, 0, 3)
    query, keys, values = (split[0], split[1], split[2])
    index = jnp.clip(places[None, :] - places[:, None], -LEFT, RIGHT) + LEFT
    index = jnp.broadcast_to(index.astype(jnp.int32), (HEADS, steps, steps))
    rel = low_back(jnp.einsum('hqd,rd->hqr', query, relative_table, precision=lax.Precision.HIGHEST))
    rel_full = jnp.take_along_axis(rel, index, axis=2)
    pairs = jnp.einsum('hqd,hkd->hqk', query, keys, precision=lax.Precision.HIGHEST)
    scores = low_back((pairs + rel_full) * (1.0 / math.sqrt(HD)))
    scores = jnp.where(valid[None, None, :] > 0, scores, -1e+30)
    probs = low(jax.nn.softmax(scores, axis=-1))
    mixed = low(low_back(jnp.einsum('hqk,hkd->hqd', probs, values, precision=lax.Precision.HIGHEST)))
    mixed = mixed.transpose(1, 0, 2).reshape(steps, width)
    second = first + low_back(product(mixed, attention_out) + attention_out_bias)
    chid = low(layer_norm(second, norm_gain[2], norm_shift[2]))
    upward = low_back(product(chid, pointwise_in))
    glu = upward[:, :width] * jax.nn.sigmoid(upward[:, width:]) * valid[:, None]
    depth = causal(glu, depthwise)
    cact = low(jax.nn.silu(layer_norm(depth, norm_gain[3], norm_shift[3])))
    third = second + low_back(product(cact, pointwise_out))
    fourth = third + 0.5 * feed(third, 4, 1)
    return layer_norm(fourth, norm_gain[5], norm_shift[5]) * valid[:, None]

def reference(tokens, lengths, cotangent, norm_gain, norm_shift, feed_in, feed_in_bias, feed_out, feed_out_bias, attention_in, attention_in_bias, attention_out, attention_out_bias, relative_table, pointwise_in, depthwise, pointwise_out):
    params = tuple((item.astype(jnp.float32) for item in (norm_gain, norm_shift, feed_in, feed_in_bias, feed_out, feed_out_bias, attention_in, attention_in_bias, attention_out, attention_out_bias, relative_table, pointwise_in, depthwise, pointwise_out)))
    per_step = 4
    clips = tokens.astype(jnp.float32).reshape(DEVICES // per_step, per_step, TOK_DEV, D)
    spans = lengths.astype(jnp.int32).reshape(DEVICES // per_step, per_step)
    seeds = cotangent.astype(jnp.float32).reshape(DEVICES // per_step, per_step, TOK_DEV, D)

    def whole(clip_rows, weights):

        def group(inputs, weight_set):
            rows, spans_here = inputs
            return jax.vmap(clip_layer, in_axes=(0, 0, None))(rows, spans_here, weight_set)
        saved = jax.checkpoint(group)

        def advance(carry, inputs):
            return (carry, saved(inputs, weights))
        final, results = lax.scan(advance, jnp.float32(0.0), (clip_rows, spans))
        return results
    results, pullback = jax.vjp(whole, clips, params)
    clip_grad, grads = pullback(seeds)
    return (results.reshape(TOKENS, D).astype(jnp.bfloat16), clip_grad.reshape(TOKENS, D).astype(jnp.bfloat16), grads[0], grads[1], grads[2], grads[3], grads[4], grads[5], grads[6], grads[7], grads[8], grads[9], grads[10], grads[11], grads[12], grads[13])
```

```python
import functools, math
import numpy as np
import jax, jax.numpy as jnp
from jax import lax
from jax.experimental import pallas as pl
from jax.experimental.pallas import tpu as pltpu
from jax.sharding import PartitionSpec as P
LEFT=64; RIGHT=8
BF=jnp.bfloat16; F32=jnp.float32

def nn(a,b): return lax.dot_general(a,b,(((1,),(0,)),((),())),preferred_element_type=F32)
def nt(a,b): return lax.dot_general(a,b,(((1,),(1,)),((),())),preferred_element_type=F32)
def tn(a,b): return lax.dot_general(a,b,(((0,),(0,)),((),())),preferred_element_type=F32)

def picker_table(steps, block):
    span=steps+block
    n=np.arange(span)
    rows=[]
    for i in range(steps//block):
        off=np.where(n<steps, n, n-span)-block*i
        row=np.clip(off,-LEFT,RIGHT)+LEFT
        rows.append(np.arange(128)[:,None]==row[None,:])
    return np.stack(rows)

QB=128

MESH=pl.DeviceIdType.MESH
def al(v,m): return pl.multiple_of(v,m)
def during(lo,hi,body):
    def run(i,c):
        body(i); return c
    lax.fori_loop(lo,hi,run,0)

class Place:
    def __init__(self,S):
        self.S=S; self.Z=S//2
        r=lax.axis_index('rep'); s=lax.axis_index('shard')
        self.r,self.s=r,s
        self.c=lax.rem(r,2); self.x=lax.rem(r//2,2); self.y=lax.rem(s,2); self.z=s//2
        base=r-2*self.x-self.c
        self.d=1-2*self.c
        self.next=(r,2*self.zat(1)+self.y); self.prev=(r,2*self.zat(-1)+self.y)
        self.over_y=(r,2*self.z+1-self.y); self.over_x=(base+2*(1-self.x)+self.c,s); self.twin=(base+2*self.x+1-self.c,s)
    def zat(self,k): return lax.rem(self.z+self.d*k+2*self.Z,self.Z)
    def greet(self):
        bar=pltpu.get_barrier_semaphore()
        for dev in (self.next,self.prev,self.over_y,self.over_x,self.twin):
            pl.semaphore_signal(bar,inc=1,device_id=dev,device_id_type=MESH)
        pl.semaphore_wait(bar,5)

SUB=(128,512)
class Scatter:
    OWN=18; RING=6; GAP=2
    def __init__(self,S,sources,common=None):
        self.common=common
        self.S=S; Z=S//2
        counts=[a if isinstance(a,int) else a.shape[0] for a in sources]
        n=self.n=sum(counts)
        (rows,wide)=SUB
        h,q=rows//2,rows//4
        self.h,self.q,self.Z=h,q,Z
        self.made=[isinstance(a,int) for a in sources]
        self.at=np.cumsum([0]+counts).tolist(); self.counts=counts
        self.inputs=[a.reshape(a.shape[0],Z,2,2,h,wide) for a in sources if not isinstance(a,int)]
        self.out_shapes=[jax.ShapeDtypeStruct((n,rows,wide),BF)]+[jax.ShapeDtypeStruct((k,Z,2,2,h,wide),BF) for k,m in zip(counts,self.made) if m]
        G=self.GAP
        self.lag=[0]+[G*k for k in range(1,5+Z)]
        self.lag[4+Z]=self.lag[3+Z]+1
        self.lag.append(self.lag[4+Z]+1)
        self.ticks=n+self.lag[-1]
        own,ring=min(n,self.OWN),min(n,self.RING)
        self.slots=own; self.ring=ring
        assert own>=self.lag[-1] or own==n
        V=lambda *d: pltpu.VMEM(d,BF)
        self.scratch=[V(n,rows,wide),V(own,Z,2,h,wide),V(ring,Z,2,h,wide),V(ring,Z,q,wide),V(ring,Z,q,wide),V(ring,Z-1,h,wide),V(ring,h,wide),
            pltpu.SemaphoreType.DMA((n,)),pltpu.SemaphoreType.DMA((n,5+Z)),pltpu.SemaphoreType.DMA((n,5+Z)),pltpu.SemaphoreType.DMA((n,2)),pltpu.SemaphoreType.REGULAR((4+Z,))]
        if common:
            self.out_shapes.append(jax.ShapeDtypeStruct((Z,2,common[2],wide),BF))
            self.scratch+=[V(Z,2,common[2],wide),pltpu.SemaphoreType.DMA((Z,)),pltpu.SemaphoreType.DMA((Z,)),pltpu.SemaphoreType.DMA((1,))]
            self.begin_common=common[0]+self.lag[-1]+1
            self.ticks=max(self.ticks,self.begin_common+Z+1)
        self.out_specs=[pl.BlockSpec(memory_space=pl.ANY)]*len(self.out_shapes)
    def bind(self,ins,outs,scr):
        self.out=outs[0]; ins,made=list(ins),list(outs[1:1+sum(self.made)])
        self.makes=list(made)
        self.g=[made.pop(0) if m else ins.pop(0) for m in self.made]
        if self.common: self.all,self.cs,self.ct,self.co=scr[-4:]; self.all_out=outs[-1]; scr=scr[:-4]
        self.o,self.own,self.cr,self.xr,self.yr,self.zr,self.fr,self.os,self.ss,self.rs,self.ls,self.free=scr
        self.p=Place(self.S); return self
    def slot(self,i): return i if self.slots==self.n else lax.rem(i,self.slots)
    def land(self,i): return i if self.ring==self.n else lax.rem(i,self.ring)
    def remote(self,i,k,src,dst,dev):
        return pltpu.make_async_remote_copy(src,dst,self.ss.at[i,k],self.rs.at[i,k],device_id=dev,device_id_type=MESH)
    def column(self,yy): return 1-self.p.y if yy else self.p.y
    def first(self,ref,i,yy):
        return self.remote(i,yy,ref.at[:,self.column(yy),1-self.p.c],self.cr.at[self.land(i),:,self.column(yy)],self.p.twin)
    def load(self,ref,i,yy):
        return pltpu.make_async_copy(ref.at[:,self.column(yy),self.p.c],self.own.at[self.slot(i),:,self.column(yy)],self.ls.at[i,yy])
    def part(self,i,col,x): return self.own.at[self.slot(i),:,col,pl.ds(al(x*self.q,self.q),self.q)]
    def cross(self,i): return self.remote(i,2,self.part(i,1-self.p.y,1-self.p.x),self.xr.at[self.land(i)],self.p.over_x)
    def side(self,i): return self.remote(i,3,self.part(i,1-self.p.y,self.p.x),self.yr.at[self.land(i)],self.p.over_y)
    def hop(self,i,s): return self.remote(i,3+s,self.own.at[self.slot(i),self.p.zat(-s),self.p.y],self.zr.at[self.land(i),s-1],self.p.next)
    def swap(self,i): return self.remote(i,3+self.Z,self.own.at[self.slot(i),self.p.z,self.p.y],self.fr.at[self.land(i)],self.p.over_x)
    def half(self,i): return self.o.at[i,pl.ds(al(self.p.c*self.h,self.h),self.h)]
    def share(self,i): return self.remote(i,4+self.Z,self.half(i),self.half(i),self.p.twin)
    def save(self,i): return pltpu.make_async_copy(self.o.at[i],self.out.at[i],self.os.at[i])
    def ask(self,i,k):
        if self.ring<self.n:
            @pl.when(i>=self.ring)
            def _(): pl.semaphore_wait(self.free.at[k],1)
    def tell(self,i,k,dev):
        if self.ring<self.n:
            @pl.when(i<self.n-self.ring)
            def _(): pl.semaphore_signal(self.free.at[k],inc=1,device_id=dev,device_id_type=MESH)
    def begin(self): self.p.greet()
    def phase(self,k,i):
        p=self.p; Z=self.Z; some=self.g[0].at[0]; here=self.slot(i); land=self.land(i)
        if k==0:
            self.ask(i,0)
            for at,count,ref in zip(self.at,self.counts,self.g):
                @pl.when((i>=at)&(i<at+count))
                def _(at=at,ref=ref):
                    for yy in (1,0): self.first(ref.at[i-at],i,yy).start(); self.load(ref.at[i-at],i,yy).start()
        elif k==1:
            for yy in (1,0):
                col=self.column(yy)
                self.load(some,i,yy).wait(); self.first(some,i,yy).wait_recv()
                self.own[here,:,col]=self.own[here,:,col]+self.cr[land,:,col]
                if yy: self.ask(i,1); self.cross(i).start()
            self.tell(i,0,p.twin)
        elif k==2:
            self.cross(i).wait_recv()
            ref=self.part(i,1-p.y,p.x); ref[...]=ref[...]+self.xr[land]
            self.tell(i,1,p.over_x)
            self.ask(i,2); self.side(i).start()
        elif k==3:
            self.side(i).wait_recv()
            ref=self.part(i,p.y,p.x); ref[...]=ref[...]+self.yr[land]
            self.tell(i,2,p.over_y)
            self.ask(i,3); self.hop(i,1).start()
        elif k<3+Z:
            s=k-3
            self.hop(i,s).wait_recv()
            ref=self.own.at[here,p.zat(-1-s),p.y]; ref[...]=ref[...]+self.zr[land,s-1]
            self.tell(i,2+s,p.prev)
            self.ask(i,3+s)
            (self.hop(i,s+1) if s+1<Z else self.swap(i)).start()
        elif k==3+Z:
            self.swap(i).wait_recv()
            ref=self.half(i); ref[...]=self.own[here,p.z,p.y]+self.fr[land]
            self.tell(i,2+Z,p.over_x)
            self.share(i).start()
        elif k==4+Z:
            for yy in (0,1): self.first(some,i,yy).wait_send()
            self.cross(i).wait_send(); self.side(i).wait_send()
            for s in range(1,Z): self.hop(i,s).wait_send()
            self.swap(i).wait_send(); self.share(i).wait()
            self.save(i).start()
        else: self.save(i).wait()
    def relay(self,s):
        p=self.p
        ref=self.all.at[p.z,p.y] if s==0 else self.all.at[p.zat(1-s)]
        return pltpu.make_async_remote_copy(ref,ref,self.cs.at[s],self.ct.at[s],device_id=p.over_y if s==0 else p.next,device_id_type=MESH)
    def spread_common(self,k):
        p=self.p; unit,at,count=self.common
        if k==0: self.all[p.z,p.y]=self.o[unit,at:at+count]
        else: self.relay(k-1).wait()
        if k<self.Z: self.relay(k).start()
        else:
            cp=pltpu.make_async_copy(self.all,self.all_out,self.co.at[0]); cp.start(); cp.wait()
    def run(self,lo,count):
        def tick(u):
            for k in reversed(range(len(self.lag))):
                i=u-self.lag[k]
                @pl.when((i>=0)&(i<self.n))
                def _(k=k,i=i): self.phase(k,i)
            if self.common:
                for k in range(self.Z+1):
                    @pl.when(u==self.begin_common+k)
                    def _(k=k): self.spread_common(k)
        during(0,count,lambda v:tick(lo+v))
    def spread(self,step,steps):
        per=-(-self.ticks//steps)
        self.run(step*per,per)

class Gather:
    def __init__(self,S,shards,cuts=None,modes=None,lag=1,ahead=None):
        self.S=S; self.Z=S//2
        pick=lambda a: a if isinstance(a,tuple) else (a,None)
        self.local=[isinstance(a,tuple) and isinstance(a[0],int) for a in shards]
        pairs=[pick(a) for a,m in zip(shards,self.local) if not m]
        self.inputs=[]; self.source=[]
        for a,layer in pairs:
            k=next((k for k,v in enumerate(self.inputs) if v is a),None)
            if k is None: k=len(self.inputs); self.inputs.append(a)
            self.source.append((k,layer))
        self.shapes=[a if m else pick(a)[0].shape[-2:] for a,m in zip(shards,self.local)]
        self.cuts=cuts or [1]*len(shards)
        self.units=[(w,a) for w,k in enumerate(self.cuts) for a in range(k)]
        self.modes=[m for k,ms in zip(self.cuts,modes or ['h']*len(shards)) for m in (ms*k)[:k]]
        self.lag=lag; Z=self.Z
        n=len(self.units); k=6*Z-2+2*(Z-1)
        self.out_shapes=[jax.ShapeDtypeStruct((a*S,b),BF) for a,b in self.shapes]
        self.out_specs=[pl.BlockSpec(memory_space=pl.ANY)]*len(shards)
        self.scratch=[pltpu.VMEM(a,BF) for a,m in zip(self.shapes,self.local) if m]+[pltpu.SemaphoreType.DMA((n,k)),pltpu.SemaphoreType.DMA((n,k)),pltpu.SemaphoreType.DMA((n,))]
        D=lag
        self.plan={}
        add=lambda at,*stage: self.plan.setdefault(at,[]).append(stage)
        for t in range(1,Z): add(D*t,'z',t)
        for t in range(Z): add(D*(t+1),'y',t)
        for t in range(1,Z): add(D*(t+1),'u',t)
        for t in range(Z): add(D*(t+2),'x',t)
        add(D*(Z+2),'end',0)
        self.last=D*(Z+2)
        self.ahead=n if ahead is None else ahead
        self.ticks=n+self.last
    def bind(self,ins,outs,scr):
        mine=list(scr[:-3]); source=list(self.source); self.i=[]
        for m in self.local:
            if m: self.i.append(mine.pop(0))
            else:
                k,layer=source.pop(0)
                self.i.append(ins[k] if layer is None else ins[k].at[layer])
        self.o=outs; self.ss,self.rs,self.ls=scr[-3:]; self.p=Place(self.S); return self
    def cols(self,u):
        w,a=self.units[u]; wide=self.shapes[w][1]//self.cuts[w]
        return pl.ds(a*wide,wide)
    def rows(self,u,zo,yy,off,ln):
        w=self.units[u][0]; n=self.shapes[w][0]; q=n//4
        return self.o[w].at[pl.ds(al((2*zo+yy)*n+off*q,q),ln*q),self.cols(u)]
    def half(self,u,t): return self.rows(u,self.p.zat(-t),self.p.y,2*self.p.c,2)
    def quarter(self,u,t,yy,x): return self.rows(u,self.p.zat(-t),yy,2*self.p.c+x,1)
    def mine(self,u,off,ln):
        w=self.units[u][0]; q=self.shapes[w][0]//4
        return self.i[w].at[pl.ds(al(off*q,q),ln*q),self.cols(u)]
    def cp(self,u,kind,t):
        p=self.p; Z=self.Z; h=self.modes[u]=='h'
        k={'z':t-1,'y':Z-1+t,'x':2*Z-1+t,'cz':3*Z-1+t-1,'cy':4*Z-2+t,'cx':5*Z-2+t,'u':6*Z-2+t-1,'cu':7*Z-3+t-1}[kind]
        if kind=='z':
            dst=self.half(u,t-1) if h else self.quarter(u,t-1,p.y,p.x); src=dst; dev=p.next
            if t==1: src=self.mine(u,2*p.c,2) if h else self.mine(u,2*p.c+p.x,1)
        elif kind=='y': dst=self.quarter(u,t,p.y,p.x); src=self.mine(u,2*p.c+p.x,1) if t==0 else dst; dev=p.over_y
        elif kind=='x': src=dst=self.quarter(u,t,1-p.y,p.x); dev=p.over_x
        elif kind=='u': src=dst=self.quarter(u,t,p.y,p.x); dev=p.over_x
        elif kind=='cz': src=dst=self.half(u,t) if h else self.quarter(u,t,p.y,p.x); dev=p.twin
        elif kind=='cu': src=dst=self.quarter(u,t,p.y,1-p.x); dev=p.twin
        elif kind=='cy': src=dst=self.quarter(u,t,1-p.y,p.x); dev=p.twin
        else: src=dst=self.quarter(u,t,1-p.y,1-p.x); dev=p.twin
        return pltpu.make_async_remote_copy(src,dst,self.ss.at[u,k],self.rs.at[u,k],device_id=dev,device_id_type=MESH)
    def own(self,u):
        w=self.units[u][0]; n=self.shapes[w][0]
        return pltpu.make_async_copy(self.i[w].at[:,self.cols(u)],self.o[w].at[pl.ds(al(self.p.s*n,n),n),self.cols(u)],self.ls.at[u])
    def open(self,u):
        self.cp(u,'z',1).start(); self.cp(u,'y',0).start(); self.own(u).start()
    def begin(self):
        self.p.greet()
        for u in range(min(self.ahead,len(self.units))): self.open(u)
    def stage(self,u,kind,t):
        Z=self.Z; q=self.modes[u]=='q'
        if kind=='z':
            self.cp(u,'z',t).wait_recv()
            if t+1<Z: self.cp(u,'z',t+1).start()
            self.cp(u,'y',t).start()
            if q: self.cp(u,'u',t).start()
            self.cp(u,'cz',t).start()
        elif kind=='y':
            self.cp(u,'y',t).wait_recv()
            self.cp(u,'x',t).start(); self.cp(u,'cy',t).start()
        elif kind=='u':
            if q: self.cp(u,'u',t).wait_recv(); self.cp(u,'cu',t).start()
        elif kind=='x':
            self.cp(u,'x',t).wait_recv(); self.cp(u,'cx',t).start()
        else:
            for t in range(1,Z):
                self.cp(u,'z',t).wait_send(); self.cp(u,'cz',t).wait()
                if q: self.cp(u,'u',t).wait_send(); self.cp(u,'cu',t).wait()
            for t in range(Z):
                self.cp(u,'y',t).wait_send(); self.cp(u,'x',t).wait_send(); self.cp(u,'cy',t).wait(); self.cp(u,'cx',t).wait()
            self.own(u).wait()
    def run(self,lo,count):
        for i in range(lo,min(lo+count,self.ticks)):
            for u in range(len(self.units)):
                if u>=self.ahead and i==u-self.ahead: self.open(u)
            for u in range(len(self.units)):
                for s in self.plan.get(i-u,[]): self.stage(u,*s)
    def done(self,w):
        return max(u for u,(a,_) in enumerate(self.units) if a==w)+self.last+1
    def spread(self,step,steps):
        per=-(-self.ticks//steps)
        for g in range(steps):
            if g*per>=self.ticks: break
            @pl.when(step==g)
            def _(g=g): self.run(g*per,per)

VM=60<<20
def call(body,name,grid,ins,in_specs,outs,out_specs,scratch,side=None,cid=None):
    any_=pl.BlockSpec(memory_space=pl.ANY)
    extra=side.inputs if side else []
    a,b,c,d,e=len(ins),len(extra),len(outs),len(side.out_shapes) if side else 0,len(scratch)
    def kernel(*refs):
        comm=None
        cut=np.cumsum([0,a,b,c,d,e]).tolist()
        part=[refs[x:y] for x,y in zip(cut,cut[1:]+[len(refs)])]
        if side:
            comm=side.bind(part[1],part[3],part[5])
        body(comm,*part[0],*part[2],*part[4])
    out=pl.pallas_call(kernel,grid=grid,out_shape=list(outs)+(side.out_shapes if side else []),in_specs=list(in_specs)+[any_]*b,
        out_specs=list(out_specs)+(side.out_specs if side else []),scratch_shapes=list(scratch)+(side.scratch if side else []),
        compiler_params=pltpu.CompilerParams(vmem_limit_bytes=VM,**(dict(collective_id=cid,has_side_effects=True) if side else {})),name=name)(*ins,*extra)
    return out[:c],out[c:]

def alone(comm):
    comm.begin(); comm.run(0,comm.ticks)
def gather(S,shards,cid,**kw):
    return call(alone,'gather_weights',(),[],[],[],[],[],Gather(S,shards,**kw),cid)[1]
def scatter(S,grads,cid):
    return call(alone,'sum_gradients',(),[],[],[],[],[],Scatter(S,grads),cid)[1][0]


CH=64

def aside(body):
    def run(comm,*refs):
        if comm:
            @pl.when(pl.program_id(0)==0)
            def _(): comm.begin()
        body(*refs)
        if comm: comm.spread(pl.program_id(0),pl.num_programs(0))
    return run
def whole(shape):
    return pl.BlockSpec(shape,lambda *i:(0,)*len(shape),pipeline_mode=pl.Buffered(1))
def chunks(steps,body):
    def run(i,c):
        body(pl.ds(pl.multiple_of(i*CH,CH),CH)); return c
    lax.fori_loop(0,steps//CH,run,0)
def stats(v):
    center=v-jnp.mean(v,axis=-1,keepdims=True)
    rstd=lax.rsqrt(jnp.mean(center*center,axis=-1,keepdims=True)+1e-5)
    return center*rstd,rstd
def norm_back(dy,gain,xhat,rstd):
    g=dy*gain
    return rstd*(g-jnp.mean(g,axis=-1,keepdims=True)-xhat*jnp.mean(g*xhat,axis=-1,keepdims=True))
def sigmoid(v): return 0.5*jnp.tanh(0.5*v)+0.5
def fold(v): return jnp.sum(v.reshape(v.shape[0]//8,8,v.shape[1]),axis=0)

PAD=32
RC=128
def over_columns(width,body):
    def run(i,c):
        body(pl.ds(pl.multiple_of(i*128,128),128)); return c
    lax.fori_loop(0,width//128,run,0)
def taps_of(taps,lead,residue):
    return [(a,k) for k in range(taps) for a in [lead(k)//8] if lead(k)%8==residue]
def slide(pad_ref,w_ref,lead,taps,t0,cols):
    acc=jnp.zeros((RC,128),F32)
    for b in range(8):
        use=taps_of(taps,lead,b)
        if not use: continue
        top=max(a for a,_ in use)
        slab=pad_ref[t0+b:t0+b+RC+8*top,cols]
        for a,k in use: acc=acc+w_ref[k:k+1,cols]*slab[8*a:8*a+RC]
    return acc

def points(comm,count):
    at=[-1]
    def point():
        if not comm: return
        if at[0]<0: comm.begin()
        else:
            per=-(-comm.ticks//count)
            comm.run(at[0]*per,per)
        at[0]+=1
    return point

def into_units(ref,rows):
    n,w=SUB; across=rows.shape[1]//w
    for a in range(rows.shape[0]//n):
        for b in range(across): ref[a*across+b,0]=rows[a*n:a*n+n,b*w:b*w+w]

def feed_back_kernel(norm,d_ref,x_ref,gain_ref,hid_ref,act_ref,dsl_ref,fi_ref,fo_ref,
        out_ref,dfi_ref,dfo_ref,dbin_ref,sums_ref,df_ref,acc_ref,turn_ref):
    steps=x_ref.shape[0]; j=pl.program_id(0)
    @pl.when(j==0)
    def _():
        sums_ref[...]=jnp.zeros_like(sums_ref)
        def body(r):
            df=(0.5*d_ref[r,:]).astype(BF)
            df_ref[r,:]=df
            sums_ref[2]+=fold(df.astype(F32))
        chunks(steps,body)
        turn_ref[...]=hid_ref[...].T
        acc_ref[...]=jnp.zeros_like(acc_ref)
    dpre=(nt(df_ref[...],fo_ref[...])*dsl_ref[...].astype(F32)).astype(BF)
    dbin_ref[...]=fold(dpre.astype(F32))
    acc_ref[...]+=nt(dpre,fi_ref[...])
    dfi_ref[0]=nn(turn_ref[...],dpre).astype(BF)
    into_units(dfo_ref,tn(act_ref[...],df_ref[...]).astype(BF))
    @pl.when(j==pl.num_programs(0)-1)
    def _():
        def body(r):
            xhat,rstd=stats(x_ref[r,:].astype(F32))
            dy=acc_ref[r,:]
            sums_ref[0]+=fold(dy*xhat); sums_ref[1]+=fold(dy)
            out_ref[r,:]=(d_ref[r,:]+norm_back(dy,gain_ref[norm:norm+1,:],xhat,rstd)).astype(out_ref.dtype)
        chunks(steps,body)

def feed_back(d,x,gains,hid,act,dsl,fi,fo,norm,out_type,side=None,cid=None):
    steps,width=x.shape; hidden=fi.shape[1]; tn_=SUB[1]; tiles=hidden//tn_; S=width//SUB[0]
    assert hidden//S==tn_
    units=tn_*width//(SUB[0]*SUB[1])
    ins=[d,x,gains,hid,act,dsl,fi,fo]
    return call(aside(functools.partial(feed_back_kernel,norm)),'feed_forward_back',(tiles,),ins,
        [whole(d.shape),whole(x.shape),whole(gains.shape),whole(hid.shape),pl.BlockSpec((steps,tn_),lambda j:(0,j)),pl.BlockSpec((steps,tn_),lambda j:(0,j)),pl.BlockSpec((width,tn_),lambda j:(0,j)),pl.BlockSpec((tn_,width),lambda j:(j,0))],
        [jax.ShapeDtypeStruct((steps,width),out_type),jax.ShapeDtypeStruct((tiles,width,tn_),BF),jax.ShapeDtypeStruct((units,S)+SUB,BF),jax.ShapeDtypeStruct((8,hidden),F32),jax.ShapeDtypeStruct((3,8,width),F32)],
        [whole((steps,width)),pl.BlockSpec((1,width,tn_),lambda j:(j,0,0)),pl.BlockSpec((units,1)+SUB,lambda j:(0,j,0,0)),pl.BlockSpec((8,tn_),lambda j:(0,j)),whole((3,8,width))],
        [pltpu.VMEM((steps,width),BF),pltpu.VMEM((steps,width),F32),pltpu.VMEM((width,steps),BF)],side,cid)

def in_units(ref,v):
    for j in range(ref.shape[0]): ref[j]=v[:,j*ref.shape[2]:(j+1)*ref.shape[2]]

def middle_back_kernel(taps,comm,d_ref,depth_ref,up_ref,chid_ref,cact_ref,mixed_ref,x2_ref,vec_ref,valid_ref,ao_ref,pi_ref,po_ref,
        dx2_ref,dpv_ref,dpo_ref,dpi_ref,dao_ref,ddw_ref,sums_ref,low_ref,wide_ref,pad_ref,tail_ref):
    steps,width=d_ref.shape
    gain_ref=vec_ref.at[Rows.gain:Rows.gain+8]; shift_ref=vec_ref.at[Rows.shift:Rows.shift+8]; dw_ref=vec_ref.at[Rows.taps:Rows.taps+32]
    point=points(comm,8)
    point()
    sums_ref[...]=jnp.zeros_like(sums_ref)
    def cast(r): low_ref[r,:width]=d_ref[r,:].astype(BF)
    chunks(steps,cast)
    wide_ref[:,:width]=nt(low_ref[:,:width],po_ref[...])
    point()
    in_units(dpo_ref,tn(cact_ref[...],low_ref[:,:width]).astype(BF))
    point()
    tail_ref[steps:steps+PAD,:]=jnp.zeros((PAD,width),F32)
    pad_ref[0:PAD,:]=jnp.zeros((PAD,width),F32)
    def three(i,c):
        r=pl.ds(pl.multiple_of(i*CH,CH),CH)
        xhat,rstd=stats(depth_ref[r,:])
        gain=gain_ref[3:4,:]
        z=xhat*gain+shift_ref[3:4,:]
        sg=sigmoid(z)
        dz=wide_ref[r,:width]*(sg*(1.0+z*(1.0-sg)))
        sums_ref[0]+=fold(dz*xhat); sums_ref[1]+=fold(dz)
        tail_ref[r,:]=norm_back(dz,gain,xhat,rstd)
        pad_ref[pl.ds(pl.multiple_of(i*CH+PAD,PAD),CH),:]=up_ref[r,:width].astype(F32)*sigmoid(up_ref[r,width:].astype(F32))*valid_ref[r,0:1]
        return c
    lax.fori_loop(0,steps//CH,three,0)
    point()
    def conv(cols):
        for t0 in range(0,steps,RC):
            wide_ref[t0:t0+RC,cols]=slide(tail_ref,dw_ref,lambda k:taps-1-k,taps,t0,cols)
        lead=lambda k:k+PAD-taps+1
        for b in range(8):
            use=taps_of(taps,lead,b)
            if not use: continue
            top=max(a for a,_ in use)
            parts={k:jnp.zeros((8,128),F32) for _,k in use}
            for t0 in range(0,steps,RC):
                slab=pad_ref[t0+b:t0+b+RC+8*top,cols]
                dd=tail_ref[t0:t0+RC,cols]
                for a,k in use: parts[k]=parts[k]+fold(slab[8*a:8*a+RC]*dd)
            for k,v in parts.items(): ddw_ref[k:k+1,cols]=jnp.sum(v,axis=0,keepdims=True)
    over_columns(width,conv)
    point()
    def gate(r):
        a=up_ref[r,:width].astype(F32); sg=sigmoid(up_ref[r,width:].astype(F32))
        dg=wide_ref[r,:width]*valid_ref[r,0:1]*sg
        low_ref[r,:width]=dg.astype(BF)
        low_ref[r,width:]=(dg*a*(1.0-sg)).astype(BF)
    chunks(steps,gate)
    in_units(dpi_ref,tn(chid_ref[...],low_ref[...]).astype(BF))
    point()
    wide_ref[:,:width]=nt(low_ref[...],pi_ref[...])
    point()
    def two(r):
        xhat,rstd=stats(x2_ref[r,:])
        dy=wide_ref[r,:width]
        sums_ref[2]+=fold(dy*xhat); sums_ref[3]+=fold(dy)
        dx=d_ref[r,:]+norm_back(dy,gain_ref[2:3,:],xhat,rstd)
        dx2_ref[r,:]=dx
        da=dx.astype(BF)
        low_ref[r,:width]=da
        sums_ref[4]+=fold(da.astype(F32))
    chunks(steps,two)
    point()
    dpv_ref[...]=nt(low_ref[:,:width],ao_ref[...]).astype(BF)
    in_units(dao_ref,tn(mixed_ref[...],low_ref[:,:width]).astype(BF))
    point()

def middle_back(d,depth,up,chid,cact,mixed,x2,vec,valid,ao,pi,po,taps,side=None,cid=None):
    steps,width=d.shape
    ins=[d,depth,up,chid,cact,mixed,x2,vec,valid,ao,pi,po]
    S=jax.ShapeDtypeStruct
    unit=lambda w: S((w.shape[1]//SUB[1],w.shape[0],SUB[1]),BF)
    outs=[S((steps,width),F32),S((steps,width),BF),unit(po),unit(pi),unit(ao),S((32,width),F32),S((5,8,width),F32)]
    return call(functools.partial(middle_back_kernel,taps),'convolution_module_back',(1,),ins,[whole(a.shape) for a in ins],outs,[whole(o.shape) for o in outs],
        [pltpu.VMEM((steps,2*width),BF),pltpu.VMEM((steps,width),F32),pltpu.VMEM((steps+PAD,width),F32),pltpu.VMEM((steps+PAD,width),F32)],side,cid)


def late_kernel(taps,size,vector_rows,comm,q_ref,k_ref,v_ref,p_ref,g_ref,table_ref,pick_ref,hid1_ref,ai_ref,dx2_ref,x1_ref,gain_ref,
        hid0_ref,act_ref,dsl_ref,fi_ref,fo_ref,x_ref,s5_ref,s4_ref,s23_ref,ddw_ref,dbin1_ref,out_ref,
        ds_ref,dpk_ref,dtab_ref,psum_ref,acc_ref,turn_ref,dx1_ref,df_ref,stage_ref,dbin_ref,sums_ref,vec_ref,stage_sem,left_sem):
    steps,width=x1_ref.shape; wide=SUB[1]; S=comm.S
    A=width//128; B=3*width//wide; C=act_ref.shape[1]//wide; D=C
    j=pl.program_id(0)
    made_ai,made_fi,made_small,made_fo=comm.makes
    @pl.when(j==0)
    def _():
        comm.begin()
        dtab_ref[...]=jnp.zeros_like(dtab_ref)
    def put(q,ref):
        return pltpu.make_async_copy(stage_ref.at[lax.rem(q,2)],ref,stage_sem.at[lax.rem(q,2)])
    def unit(q,value,ref):
        @pl.when(q>=2)
        def _(): put(q,ref).wait()
        stage_ref[lax.rem(q,2)]=value.reshape(stage_ref.shape[1:])
        put(q,ref).start()
    def lefts(a,slot):
        rows=act_ref.shape[1]//S
        return [pltpu.make_async_copy(act_ref.at[:,pl.ds(al(s*rows+a*SUB[0],SUB[0]),SUB[0])],dpk_ref.at[slot,:,pl.ds(s*SUB[0],SUB[0])],left_sem.at[slot,s]) for s in range(S)]
    @pl.when(j<A)
    def _():
        flip=(lax.broadcasted_iota(jnp.int32,(QB,QB),0)+lax.broadcasted_iota(jnp.int32,(QB,QB),1)==QB-1).astype(F32).astype(BF)
        here=pl.ds(al(j*128,128),128)
        parts=[]
        for hh in range(128//size):
            cols=slice(hh*size,(hh+1)*size)
            parts.append(one_head_back(q_ref,k_ref,v_ref,p_ref.at[hh],g_ref,table_ref,pick_ref,dtab_ref,ds_ref,flip,cols))
            comm.run(j*2+hh,1)
        for part in range(3):
            dpk_ref[part,:,here]=jnp.concatenate([a[part] for a in parts],axis=1)
        psum_ref[0:1,here]=jnp.sum(dpk_ref[0,:,here].astype(F32),axis=0,keepdims=True)
        psum_ref[1:2,here]=jnp.sum(dpk_ref[2,:,here].astype(F32),axis=0,keepdims=True)
    @pl.when((j>=A)&(j<A+B))
    def _():
        b=j-A; per=width//wide
        @pl.when(b==0)
        def _():
            turn_ref[...]=hid1_ref[...].T
            acc_ref[...]=jnp.zeros_like(acc_ref)
            sums_ref[...]=jnp.zeros_like(sums_ref)
        g=dpk_ref[b//per,:,pl.ds(al(lax.rem(b,per)*wide,wide),wide)]
        acc_ref[...]+=nt(g,ai_ref[...])
        unit(b,nn(turn_ref[...],g).astype(BF),made_ai.at[b])
        @pl.when(b==B-1)
        def _():
            for a in range(3):
                for cp in lefts(a,a): cp.start()
            turn_ref[...]=hid0_ref[...].T
            def body(r):
                xhat,rstd=stats(x1_ref[r,:])
                dy=acc_ref[r,:]
                sums_ref[0]+=fold(dy*xhat); sums_ref[1]+=fold(dy)
                dx=dx2_ref[r,:]+norm_back(dy,gain_ref[1:2,:],xhat,rstd)
                dx1_ref[r,:]=dx
                df=(0.5*dx).astype(BF)
                df_ref[r,:]=df
                sums_ref[4]+=fold(df.astype(F32))
            chunks(steps,body)
            acc_ref[...]=jnp.zeros_like(acc_ref)
        comm.run(2*A+b,1)
    @pl.when((j>=A+B)&(j<A+B+C))
    def _():
        c=j-A-B
        dpre=(nt(df_ref[...],fo_ref[...])*dsl_ref[...].astype(F32)).astype(BF)
        dbin_ref[:,pl.ds(al(c*wide,wide),wide)]=fold(dpre.astype(F32))
        acc_ref[...]+=nt(dpre,fi_ref[...])
        unit(B+c,nn(turn_ref[...],dpre).astype(BF),made_fi.at[c])
        @pl.when(c==C-1)
        def _():
            def body(r):
                xhat,rstd=stats(x_ref[r,:].astype(F32))
                dy=acc_ref[r,:]
                sums_ref[2]+=fold(dy*xhat); sums_ref[3]+=fold(dy)
                out_ref[r,:]=(dx1_ref[r,:]+norm_back(dy,gain_ref[0:1,:],xhat,rstd)).astype(BF)
            chunks(steps,body)
            vec_ref[...]=jnp.zeros_like(vec_ref)
            total=lambda v: jnp.sum(v,axis=0,keepdims=True)
            rows=[sums_ref[2],sums_ref[0],s23_ref[2],s23_ref[0],s4_ref[0],s5_ref[0],sums_ref[3],sums_ref[1],s23_ref[3],s23_ref[1],s4_ref[1],s5_ref[1],sums_ref[4],s4_ref[2]]
            rows=[total(v) for v in rows]+[psum_ref[0:1,:],psum_ref[1:2,:],total(s23_ref[4])]
            L=width//S
            for i,v in enumerate(rows):
                for s in range(S): vec_ref[s,i:i+1,0:L]=v[:,s*L:s*L+L]
            k=len(rows)
            for i,ref in enumerate((dbin_ref,dbin1_ref)):
                v=total(ref[...])
                for s in range(S): vec_ref[s,k+i:k+i+1,:]=v[:,s*wide:s*wide+wide]
            for s in range(S):
                vec_ref[s,32:32+taps,0:L]=ddw_ref[0:taps,s*L:s*L+L]
                n=dtab_ref.shape[0]//S
                vec_ref[s,vector_rows:vector_rows+n,0:size]=dtab_ref[s*n:s*n+n,:]
        comm.run(2*A+B+c,1)
    @pl.when((j>=A+B+C)&(j<A+B+C+D))
    def _():
        d=j-A-B-C; across=width//wide
        @pl.when(d==0)
        def _(): unit(B+C,vec_ref[...].astype(BF).reshape(S*SUB[0],wide),made_small.at[0])
        a=d//across
        for slot in range(3):
            @pl.when((lax.rem(a,3)==slot)&(lax.rem(d,across)==0))
            def _(slot=slot):
                for cp in lefts(a,slot): cp.wait()
        unit(B+C+1+d,tn(dpk_ref[lax.rem(a,3)],df_ref[:,pl.ds(al(lax.rem(d,across)*wide,wide),wide)]).astype(BF),made_fo.at[d])
        @pl.when(d==across-1)
        def _():
            for a in range(3,D//across):
                for cp in lefts(a,a-3): cp.start()
        comm.run(2*A+B+C+d,1)
    @pl.when(j==A+B+C+D)
    def _():
        for q in (0,1): put(B+C+D+1+q,made_fo.at[0]).wait()
        lo=2*A+B+C+D
        comm.run(lo,comm.ticks-lo)

def one_head_back(q_ref,k_ref,v_ref,p_ref,g_ref,table_ref,pick_ref,dtab_ref,ds_ref,flip,cols):
    steps=q_ref.shape[0]; nb=steps//QB; span=steps+QB; size=cols.stop-cols.start
    scale=1.0/math.sqrt(size)
    k=k_ref[:,cols]; v=v_ref[:,cols]; dqs=[]
    for i in range(nb):
        rows=slice(i*QB,(i+1)*QB)
        q=q_ref[rows,cols]
        p=p_ref[rows,:].astype(F32)
        t=p*nt(g_ref[rows,cols],v)
        ds=(t-p*jnp.sum(t,axis=1,keepdims=True)).astype(BF)
        ds_ref[rows,:]=ds
        wide=jnp.concatenate([nn(flip,ds),jnp.zeros((QB,span-steps),F32)],axis=1)
        back=pltpu.roll(wide,span-QB+1,1,stride=1,stride_axis=0).astype(BF)
        drel=nn(flip,(nt(back,pick_ref[i])*scale).astype(BF)).astype(BF)
        dqs.append((nn(ds,k)*scale+nn(drel,table_ref[...])).astype(BF))
        dtab_ref[...]+=tn(drel,q)
    return jnp.concatenate(dqs,axis=0),(tn(ds_ref[...],q_ref[:,cols])*scale).astype(BF),tn(p_ref[...],g_ref[:,cols]).astype(BF)

VECTOR_ROWS=64
def late(S,packed,p,grad,table,pick,heads,hid1,ai,dx2,x1,gains,hid0,act,dsl,fi,fo,tokens,s5,s4,s23,ddw,dbin1,taps,ready,cid):
    steps,width=x1.shape; size=width//heads; wide=SUB[1]
    A=width//128; B=3*width//wide; C=act.shape[1]//wide; D=C; per=128//size
    assert act.shape[1]//S==wide and width//S==SUB[0] and wide//SUB[0]<=4
    comm=Scatter(S,ready+[B,C,1,D],common=(sum(a.shape[0] for a in ready)+B+C,VECTOR_ROWS,table.shape[0]//S))
    head=lambda o:pl.BlockSpec((steps,128),lambda j:(0,o*A+jnp.minimum(j,A-1)))
    tile=lambda lo,n:(lambda j:jnp.minimum(jnp.maximum(j-lo,0),n-1))
    tb,tc=tile(A,B),tile(A+B,C)
    ins=[packed,packed,packed,p,grad,table,pick,hid1,ai,dx2,x1,gains,hid0,act,dsl,fi,fo,tokens,s5,s4,s23,ddw,dbin1]
    specs=[head(0),head(1),head(2),pl.BlockSpec((per,steps,steps),lambda j:(jnp.minimum(j,A-1),0,0)),head(0),whole(table.shape),whole(pick.shape),
        whole(hid1.shape),pl.BlockSpec((width,wide),lambda j:(0,tb(j))),whole(dx2.shape),whole(x1.shape),whole(gains.shape),whole(hid0.shape),pl.BlockSpec(memory_space=pl.ANY),
        pl.BlockSpec((steps,wide),lambda j:(0,tc(j))),pl.BlockSpec((width,wide),lambda j:(0,tc(j))),pl.BlockSpec((wide,width),lambda j:(tc(j),0)),whole(tokens.shape)]
    specs+=[whole(a.shape) for a in (s5,s4,s23,ddw,dbin1)]
    V=pltpu.VMEM; Z=S//2
    scratch=[V((steps,steps),BF),V((3,steps,width),BF),V((128,size),F32),V((8,width),F32),V((steps,width),F32),V((width,steps),BF),V((steps,width),F32),V((steps,width),BF),
        V((2,Z,2,2,SUB[0]//2,wide),BF),V((8,act.shape[1]),F32),V((5,8,width),F32),V((S,)+SUB,F32),pltpu.SemaphoreType.DMA((2,)),pltpu.SemaphoreType.DMA((3,S))]
    return call(functools.partial(late_kernel,taps,size,VECTOR_ROWS),'attend_back_and_sums',(A+B+C+D+1,),ins,specs,[jax.ShapeDtypeStruct((steps,width),BF)],[whole((steps,width))],scratch,comm,cid)

class Rows:
    gain=0; shift=8; inner=16; outer=24; packed=26; mixed=28; taps=32; count=64

def early_kernel(heads,taps,comm,gain_in,shift_in,inner_in,outer_in,packed_in,mixed_in,taps_in,tok_ref,cot_ref,valid_ref,mask_ref,table_ref,pick_ref,
        hid0_ref,act0_ref,dsl0_ref,x1_ref,hid1_ref,packed_ref,mixed_ref,p_ref,x2_ref,chid_ref,up_ref,depth_ref,cact_ref,x3_ref,hid4_ref,act1_ref,dsl1_ref,dx4_ref,res_ref,s5_ref,vec_ref,
        own_ref,land_ref,land_sem,acc_ref,wa_ref,wb_ref,sem_a,sem_b,rel_ref,qkv_ref,pad_ref,wide_ref):
    steps,width=tok_ref.shape; tile=wa_ref.shape[2]; S=comm.S
    small,fi0,fo0,ai,ao,pi,po,fi1,fo1=comm.o
    F=fi0.shape[1]//tile; B=ai.shape[1]//tile; A=width//128; M0,M1,M2=ao.shape[1]//tile,pi.shape[1]//tile,po.shape[1]//tile
    size=width//heads
    cut=np.cumsum([0,F,B,A,M0,M1,M2,F]).tolist()
    j=pl.program_id(0)
    L=width//S
    def row(i): return vec_ref[i:i+1,:]
    def column(w,i,slot): return pltpu.make_async_copy(w.at[:,pl.ds(al(i*tile,tile),tile)],wa_ref.at[slot],sem_a.at[slot])
    def band(w,i,slot): return pltpu.make_async_copy(w.at[pl.ds(al(i*tile,tile),tile)],wb_ref.at[slot],sem_b.at[slot])
    want=[comm.done(2),comm.done(3),comm.done(4),comm.done(5),comm.done(6),comm.done(8)]
    at={}
    def plan(steps_,lo,hi):
        n=len(steps_)
        for i,st in enumerate(steps_):
            a,b=lo+(hi-lo)*i//n,lo+(hi-lo)*(i+1)//n
            if b>a: at[st]=(a,b-a)
    plan(list(range(F//2-1,cut[1],F//2)),want[0],want[1])
    plan([cut[2]-1],want[1],want[2])
    plan(list(range(cut[2]+A//2-1,cut[3],A//2)),want[2],want[4])
    plan([cut[4]-1,cut[6]-1],want[4],comm.ticks-1)
    def ticks():
        for st,(lo,n) in at.items():
            @pl.when(j==st)
            def _(lo=lo,n=n): comm.run(lo,n)
    @pl.when(j==0)
    def _():
        own_ref[...]=jnp.zeros_like(own_ref)
        for at_,ref in ((Rows.gain,gain_in),(Rows.shift,shift_in),(Rows.outer,outer_in),(Rows.packed,packed_in),(Rows.mixed,mixed_in),(Rows.taps,taps_in)):
            own_ref[at_:at_+ref.shape[0],:]=ref[...].astype(F32)
        k=inner_in.shape[1]//L
        for l in range(2):
            for i in range(k): own_ref[Rows.inner+l*k+i:Rows.inner+l*k+i+1,:]=inner_in[l:l+1,i*L:i*L+L].astype(F32)
        comm.i[0][...]=own_ref[...].astype(BF)
        comm.begin()
        comm.run(0,want[0])
        cp=pltpu.make_async_copy(small,land_ref,land_sem.at[0]); cp.start()
        column(fi0,0,0).start(); band(fo0,0,0).start()
        cp.wait()
        for s in range(S): vec_ref[:,s*L:s*L+L]=land_ref[s*Rows.count:(s+1)*Rows.count,:].astype(F32)
        for i in range(steps//QB): rel_ref[i]=tn(table_ref[...],pick_ref[i]).astype(BF)
        def body(r):
            xhat,_r=stats(tok_ref[r,:].astype(F32))
            hid0_ref[r,:]=(xhat*row(Rows.gain)+row(Rows.shift)).astype(BF)
        chunks(steps,body)
        acc_ref[...]=jnp.zeros_like(acc_ref)
        pad_ref[0:PAD,:]=jnp.zeros((PAD,width),F32)
    def feed_tile(i,tau,l,hid_ref,act_ref,dsl_ref,fi,fo):
        slot=lax.rem(tau,2); k=tile//L
        column(fi,i,slot).wait(); band(fo,i,lax.rem(i,2)).wait()
        @pl.when(i+1<F)
        def _(): column(fi,i+1,lax.rem(tau+1,2)).start(); band(fo,i+1,lax.rem(i+1,2)).start()
        bias=jnp.concatenate([vec_ref[Rows.inner+l*k+a:Rows.inner+l*k+a+1,pl.ds(al(i*L,L),L)] for a in range(k)],axis=1)
        pre=nn(hid_ref[...],wa_ref[slot])+bias
        sg=sigmoid(pre)
        act_ref[...]=(pre*sg).astype(BF)
        dsl_ref[...]=(sg*(1.0+pre*(1.0-sg))).astype(BF)
        acc_ref[...]+=nn(act_ref[...],wb_ref[lax.rem(i,2)])
    @pl.when(j<cut[1])
    def _(): feed_tile(j,j,0,hid0_ref,act0_ref,dsl0_ref,fi0,fo0)
    @pl.when(j==cut[1]-1)
    def _():
        def body(r):
            x=tok_ref[r,:].astype(F32)+0.5*(acc_ref[r,:]+row(Rows.outer))
            x1_ref[r,:]=x
            xhat,_r=stats(x)
            hid1_ref[r,:]=(xhat*row(Rows.gain+1)+row(Rows.shift+1)).astype(BF)
        chunks(steps,body)
    def stream(w,lo,n,tau0,use):
        @pl.when((j>=lo)&(j<lo+n))
        def _():
            i=j-lo; slot=lax.rem(tau0+i,2)
            column(w,i,slot).wait()
            @pl.when(i+1<n)
            def _(): column(w,i+1,lax.rem(tau0+i+1,2)).start()
            use(i,slot)
    def after(step,w,tau):
        @pl.when(j==step)
        def _(): column(w,0,lax.rem(tau,2)).start()
    def here(i): return pl.ds(al(i*tile,tile),tile)
    def pack(i,slot):
        v=nn(hid1_ref[...],wa_ref[slot])
        per=width//tile
        @pl.when(i<per)
        def _(): packed_ref[:,here(i)]=(v+vec_ref[Rows.packed:Rows.packed+1,here(lax.rem(i,per))]).astype(BF)
        @pl.when((i>=per)&(i<2*per))
        def _(): packed_ref[:,here(i)]=v.astype(BF)
        @pl.when(i>=2*per)
        def _(): packed_ref[:,here(i)]=(v+vec_ref[Rows.packed+1:Rows.packed+2,here(lax.rem(i,per))]).astype(BF)
    stream(ai,cut[1],B,F,pack)
    @pl.when((j>=cut[2])&(j<cut[3]))
    def _():
        h=j-cut[2]
        for a in range(3): qkv_ref[a]=packed_ref[:,pl.ds(al(a*width+h*128,128),128)]
        scale=1.0/math.sqrt(size)
        for i in range(steps//QB):
            rows=slice(i*QB,(i+1)*QB); outs=[]
            for hh in range(128//size):
                cols=slice(hh*size,(hh+1)*size)
                q=qkv_ref[0,rows,cols]
                rel=pltpu.roll(nn(q,rel_ref[i]),0,1,stride=1,stride_axis=0)[:,:steps]
                s=(nt(q,qkv_ref[1,:,cols])+rel)*scale+mask_ref[0:1,:]
                e=jnp.exp(s-jnp.max(s,axis=1,keepdims=True))
                p=(e*(1.0/jnp.sum(e,axis=1,keepdims=True))).astype(BF)
                p_ref[hh,rows,:]=p
                outs.append(nn(p,qkv_ref[2,:,cols]).astype(BF))
            mixed_ref[rows,pl.ds(al(h*128,128),128)]=jnp.concatenate(outs,axis=1)
    def join(i,slot):
        x2_ref[:,here(i)]=x1_ref[:,here(i)]+nn(mixed_ref[...],wa_ref[slot])+vec_ref[Rows.mixed:Rows.mixed+1,here(i)]
        @pl.when(i==M0-1)
        def _():
            def body(r):
                xhat,_r=stats(x2_ref[r,:])
                chid_ref[r,:]=(xhat*row(Rows.gain+2)+row(Rows.shift+2)).astype(BF)
            chunks(steps,body)
    stream(ao,cut[3],M0,F+B,join)
    def raise_(i,slot):
        wide_ref[:,here(i)]=nn(chid_ref[...],wa_ref[slot])
        @pl.when(i==M1-1)
        def _():
            def gate(k,c):
                r=pl.ds(pl.multiple_of(k*CH,CH),CH)
                a=wide_ref[r,:width]; b=wide_ref[r,width:]
                up_ref[r,:width]=a.astype(BF); up_ref[r,width:]=b.astype(BF)
                pad_ref[pl.ds(pl.multiple_of(k*CH+PAD,PAD),CH),:]=a*sigmoid(b)*valid_ref[r,0:1]
                return c
            lax.fori_loop(0,steps//CH,gate,0)
            weights=vec_ref.at[Rows.taps:Rows.taps+32]
            def conv(cols):
                for t0 in range(0,steps,RC):
                    depth_ref[t0:t0+RC,cols]=slide(pad_ref,weights,lambda k:k+PAD-taps+1,taps,t0,cols)
            over_columns(width,conv)
            def body(r):
                xhat,_r=stats(depth_ref[r,:])
                z=xhat*row(Rows.gain+3)+row(Rows.shift+3)
                cact_ref[r,:]=(z*sigmoid(z)).astype(BF)
            chunks(steps,body)
    stream(pi,cut[4],M1,F+B+M0,raise_)
    def lower(i,slot):
        x3_ref[:,here(i)]=x2_ref[:,here(i)]+nn(cact_ref[...],wa_ref[slot])
        @pl.when(i==M2-1)
        def _():
            def body(r):
                xhat,_r=stats(x3_ref[r,:])
                hid4_ref[r,:]=(xhat*row(Rows.gain+4)+row(Rows.shift+4)).astype(BF)
            chunks(steps,body)
            acc_ref[...]=jnp.zeros_like(acc_ref)
    stream(po,cut[5],M2,F+B+M0+M1,lower)
    ticks()
    tau=F+B+M0+M1+M2
    after(cut[1]-1,ai,F); after(cut[3]-1,ao,F+B); after(cut[4]-1,pi,F+B+M0); after(cut[5]-1,po,F+B+M0+M1)
    @pl.when(j==cut[6]-1)
    def _():
        comm.run(comm.ticks-1,1)
        column(fi1,0,tau%2).start(); band(fo1,0,0).start()
    @pl.when(j>=cut[6])
    def _(): feed_tile(j-cut[6],tau+j-cut[6],1,hid4_ref,act1_ref,dsl1_ref,fi1,fo1)
    @pl.when(j==cut[7]-1)
    def _():
        s5_ref[...]=jnp.zeros_like(s5_ref)
        def body(r):
            y=x3_ref[r,:]+0.5*(acc_ref[r,:]+row(Rows.outer+1))
            xhat,rstd=stats(y)
            ok=valid_ref[r,0:1]
            gain=row(Rows.gain+5)
            res_ref[r,:]=((xhat*gain+row(Rows.shift+5))*ok).astype(BF)
            dy=cot_ref[r,:].astype(F32)*ok
            dx4_ref[r,:]=norm_back(dy,gain,xhat,rstd)
            s5_ref[0]+=fold(dy*xhat)
            s5_ref[1]+=fold(dy)
        chunks(steps,body)

def early(S,vectors,tokens,cot,valid,mask,table,pick,heads,weights,cid):
    steps,width=tokens.shape; tile=512; taps=vectors[-1].shape[0]; L=vectors[0].shape[1]
    comm=Gather(S,[(Rows.count,L)]+weights,cuts=[1,2,2,2,1,1,1,2,2],modes=['h','hq','hh','qh','h','q','h','hq','hh'],ahead=4)
    hidden=comm.shapes[1][1]; size=width//heads
    F,B,A=hidden//tile,comm.shapes[3][1]//tile,width//128
    M=[comm.shapes[i][1]//tile for i in (4,5,6)]
    assert comm.shapes[2][0]*S==hidden and tile==hidden//S
    cut=np.cumsum([0,F,B,A]+M+[F]).tolist()
    within=lambda lo,n:(lambda j:jnp.minimum(jnp.maximum(j-lo,0),n-1))
    f0,at,f1=within(0,F),within(cut[2],A),within(cut[6],F)
    ins=list(vectors)+[tokens,cot,valid,mask,table,pick]
    D=jax.ShapeDtypeStruct
    b=D((steps,width),BF); f=D((steps,width),F32); hid=D((steps,hidden),BF)
    outs=[b,hid,hid,f,b,D((steps,3*width),BF),b,D((heads,steps,steps),BF),f,b,D((steps,2*width),BF),f,b,f,b,hid,hid,f,b,D((2,8,width),F32),D((Rows.count,width),F32)]
    specs=[whole(o.shape) for o in outs]
    for i,t in ((1,f0),(2,f0),(15,f1),(16,f1)): specs[i]=pl.BlockSpec((steps,tile),lambda j,t=t:(0,t(j)))
    specs[7]=pl.BlockSpec((128//size,steps,steps),lambda j:(at(j),0,0))
    V=pltpu.VMEM; sem=lambda n: pltpu.SemaphoreType.DMA((n,))
    scratch=[V((Rows.count,L),F32),V((S*Rows.count,L),BF),sem(1),V((steps,width),F32),V((2,width,tile),BF),V((2,tile,width),BF),sem(2),sem(2),
        V((steps//QB,size,steps+QB),BF),V((3,steps,128),BF),V((steps+PAD,width),F32),V((steps,2*width),F32)]
    return call(functools.partial(early_kernel,heads,taps),'gather_and_forward',(cut[-1],),ins,[whole(a.shape) for a in ins],outs,specs,scratch,comm,cid)


def local(S,R,tokens,lengths,cotangent,norm_gain,norm_shift,feed_in,feed_in_bias,feed_out,feed_out_bias,attention_in,attention_in_bias,attention_out,attention_out_bias,relative_table,pointwise_in,depthwise,pointwise_out):
    steps,width=tokens.shape; taps=depthwise.shape[0]
    live=jnp.arange(steps,dtype=jnp.int32)<lengths[0]
    valid=jnp.broadcast_to(live.astype(F32)[:,None],(steps,128))
    mask=jnp.broadcast_to(jnp.where(live,0.0,-1e30).astype(F32)[None,:],(8,steps))
    rows=relative_table.shape[0]
    table=jnp.pad(relative_table,((0,128-rows),(0,0)))
    pick=jnp.asarray(picker_table(steps,QB).astype(np.float32)).astype(BF)
    vectors=[norm_gain,norm_shift,feed_in_bias,feed_out_bias,attention_in_bias,attention_out_bias.reshape(1,-1),depthwise]
    weights=[(feed_in,0),(feed_out,0),attention_in,attention_out,pointwise_in,pointwise_out,(feed_in,1),(feed_out,1)]
    outs,full=early(S,vectors,tokens,cotangent,valid,mask,table,pick,HEADS,weights,0)
    hid0,act0,dsl0,x1,hid1,packed,mixed,p,x2,chid,up,depth,cact,x3,hid4,act1,dsl1,dx4,result,s5,vec=outs
    fi0,fo0,ai,ao,pi,po,fi1,fo1=full[1:]
    flat=lambda a:a.reshape(a.shape[0],S*SUB[0],SUB[1])
    (dx3,dfi1,dfo1,dbin1,s4),_=feed_back(dx4,x3,vec,hid4,act1,dsl1,fi1,fo1,4,F32)
    (dx2,dpv,dpo,dpi,dao,ddw,s23),_=middle_back(dx3,depth,up,chid,cact,mixed,x2,vec,valid,ao,pi,po,taps)
    ready=[dfi1,flat(dfo1),dpo,dpi,dao]
    (dtok,),outs=late(S,packed,p,dpv,table,pick,HEADS,hid1,ai,dx2,x1,vec,hid0,act0,dsl0,fi0,fo0,tokens,s5,s4,s23,ddw,dbin1,taps,ready,7)
    sums,common=outs[0],outs[-1]
    if R>4:
        groups=[[g*4+i for g in range(R//4)] for i in range(4)]
        sums,common=[lax.psum(a,'rep',axis_index_groups=groups) for a in (sums,common)]
    at=np.cumsum([0]+[a.shape[0] for a in ready]+[3*width//SUB[1],fi0.shape[1]//SUB[1],1,fi0.shape[1]//SUB[1]]).tolist()
    gfi1,gfo1,gpo,gpi,gao,gai,gfi0,small,gfo0=[sums[a:b] for a,b in zip(at,at[1:])]
    def by_column(u): return u.transpose(1,0,2).reshape(SUB[0],-1).astype(F32)
    def by_row(u): return u.reshape(-1,width//SUB[1],*SUB).transpose(0,2,1,3).reshape(-1,width).astype(F32)
    vec=small[0].astype(F32); L=norm_gain.shape[1]
    ggain,gshift,gbout,gpbias,gmbias=[vec[a:b,:L] for a,b in ((0,6),(6,12),(12,14),(14,16),(16,17))]
    gbin=vec[17:19]; gdw=vec[32:32+taps,:L]
    gtab=common.reshape(-1,SUB[1])[:rows,:relative_table.shape[1]].astype(F32)
    return (result,dtok,ggain,gshift,jnp.stack([by_column(gfi0),by_column(gfi1)]),gbin,jnp.stack([by_row(gfo0),by_row(gfo1)]),gbout,by_column(gai),gpbias,by_column(gao),gmbias[0],gtab,by_column(gpi),gdw,by_column(gpo))

HEADS=16

def solution(mesh):
    R,S=mesh.shape['rep'],mesh.shape['shard']
    rows=P(('rep','shard'),None)
    last,mid,first=P(None,'shard'),P(None,'shard',None),P('shard',None)
    weights=(last,last,mid,last,mid,last,first,last,first,P('shard'),P(),first,last,first)
    return jax.shard_map(functools.partial(local,S,R),mesh=mesh,in_specs=(rows,P(('rep','shard')),rows)+weights,out_specs=(rows,rows)+weights,check_vma=False)
```

```python
import functools, math
import numpy as np
import jax, jax.numpy as jnp
from jax import lax
from jax.experimental import pallas as pl
from jax.experimental.pallas import tpu as pltpu
from jax.sharding import PartitionSpec as P
LEFT=64; RIGHT=8
BF=jnp.bfloat16; F32=jnp.float32

def nn(a,b): return lax.dot_general(a,b,(((1,),(0,)),((),())),preferred_element_type=F32)
def nt(a,b): return lax.dot_general(a,b,(((1,),(1,)),((),())),preferred_element_type=F32)
def tn(a,b): return lax.dot_general(a,b,(((0,),(0,)),((),())),preferred_element_type=F32)

def picker_table(steps, block):
    span=steps+block
    n=np.arange(span)
    rows=[]
    for i in range(steps//block):
        off=np.where(n<steps, n, n-span)-block*i
        row=np.clip(off,-LEFT,RIGHT)+LEFT
        rows.append(np.arange(128)[:,None]==row[None,:])
    return np.stack(rows)

QB=128

MESH=pl.DeviceIdType.MESH
def al(v,m): return pl.multiple_of(v,m)
def during(lo,hi,body):
    def run(i,c):
        body(i); return c
    lax.fori_loop(lo,hi,run,0)

class Place:
    def __init__(self,S):
        self.S=S; self.Z=S//2
        r=lax.axis_index('rep'); s=lax.axis_index('shard')
        self.r,self.s=r,s
        self.c=lax.rem(r,2); self.x=lax.rem(r//2,2); self.y=lax.rem(s,2); self.z=s//2
        base=r-2*self.x-self.c
        self.d=1-2*self.c
        self.next=(r,2*self.zat(1)+self.y); self.prev=(r,2*self.zat(-1)+self.y)
        self.over_y=(r,2*self.z+1-self.y); self.over_x=(base+2*(1-self.x)+self.c,s); self.twin=(base+2*self.x+1-self.c,s)
    def zat(self,k): return lax.rem(self.z+self.d*k+2*self.Z,self.Z)
    def greet(self):
        bar=pltpu.get_barrier_semaphore()
        for dev in (self.next,self.prev,self.over_y,self.over_x,self.twin):
            pl.semaphore_signal(bar,inc=1,device_id=dev,device_id_type=MESH)
        pl.semaphore_wait(bar,5)

SUB=(128,512)
class Scatter:
    OWN=18; RING=6; GAP=2
    def __init__(self,S,sources,places,out_shapes,common=None):
        self.places=places
        self.common=common
        self.S=S; Z=S//2
        counts=[a if isinstance(a,int) else a.shape[0] for a in sources]
        n=self.n=sum(counts)
        (rows,wide)=SUB
        h,q=rows//2,rows//4
        self.h,self.q,self.Z=h,q,Z
        self.made=[isinstance(a,int) for a in sources]
        self.at=np.cumsum([0]+counts).tolist(); self.counts=counts
        self.inputs=[a.reshape(a.shape[0],Z,2,2,h,wide) for a in sources if not isinstance(a,int)]
        self.finals=len(out_shapes)
        self.out_shapes=[jax.ShapeDtypeStruct(a,BF) for a in out_shapes]+[jax.ShapeDtypeStruct((k,Z,2,2,h,wide),BF) for k,m in zip(counts,self.made) if m]
        G=self.GAP
        self.lag=[0]+[G*k for k in range(1,5+Z)]
        self.lag[4+Z]=self.lag[3+Z]+1
        self.lag.append(self.lag[4+Z]+1)
        self.ticks=n+self.lag[-1]
        own,ring=min(n,self.OWN),min(n,self.RING)
        self.slots=own; self.ring=ring
        assert own>=self.lag[-1] or own==n
        V=lambda *d: pltpu.VMEM(d,BF)
        self.scratch=[V(n,rows,wide),V(own,Z,2,h,wide),V(ring,Z,2,h,wide),V(ring,Z,q,wide),V(ring,Z,q,wide),V(ring,Z-1,h,wide),V(ring,h,wide),
            pltpu.SemaphoreType.DMA((n,)),pltpu.SemaphoreType.DMA((n,5+Z)),pltpu.SemaphoreType.DMA((n,5+Z)),pltpu.SemaphoreType.DMA((n,2)),pltpu.SemaphoreType.REGULAR((4+Z,))]
        if common:
            self.out_shapes.append(jax.ShapeDtypeStruct((Z,2,common[2],wide),BF))
            self.scratch+=[V(Z,2,common[2],wide),pltpu.SemaphoreType.DMA((Z,)),pltpu.SemaphoreType.DMA((Z,)),pltpu.SemaphoreType.DMA((1,))]
            self.begin_common=common[0]+self.lag[-1]+1
            self.ticks=max(self.ticks,self.begin_common+Z+1)
        self.out_specs=[pl.BlockSpec(memory_space=pl.ANY)]*len(self.out_shapes)
    def bind(self,ins,outs,scr):
        k=self.finals; self.out=outs[:k]; ins,made=list(ins),list(outs[k:k+sum(self.made)])
        self.makes=list(made)
        self.g=[made.pop(0) if m else ins.pop(0) for m in self.made]
        if self.common: self.all,self.cs,self.ct,self.co=scr[-4:]; self.all_out=outs[-1]; scr=scr[:-4]
        self.o,self.own,self.cr,self.xr,self.yr,self.zr,self.fr,self.os,self.ss,self.rs,self.ls,self.free=scr
        self.p=Place(self.S); return self
    def slot(self,i): return i if self.slots==self.n else lax.rem(i,self.slots)
    def land(self,i): return i if self.ring==self.n else lax.rem(i,self.ring)
    def remote(self,i,k,src,dst,dev):
        return pltpu.make_async_remote_copy(src,dst,self.ss.at[i,k],self.rs.at[i,k],device_id=dev,device_id_type=MESH)
    def column(self,yy): return 1-self.p.y if yy else self.p.y
    def first(self,ref,i,yy):
        return self.remote(i,yy,ref.at[:,self.column(yy),1-self.p.c],self.cr.at[self.land(i),:,self.column(yy)],self.p.twin)
    def load(self,ref,i,yy):
        return pltpu.make_async_copy(ref.at[:,self.column(yy),self.p.c],self.own.at[self.slot(i),:,self.column(yy)],self.ls.at[i,yy])
    def part(self,i,col,x): return self.own.at[self.slot(i),:,col,pl.ds(al(x*self.q,self.q),self.q)]
    def cross(self,i): return self.remote(i,2,self.part(i,1-self.p.y,1-self.p.x),self.xr.at[self.land(i)],self.p.over_x)
    def side(self,i): return self.remote(i,3,self.part(i,1-self.p.y,self.p.x),self.yr.at[self.land(i)],self.p.over_y)
    def hop(self,i,s): return self.remote(i,3+s,self.own.at[self.slot(i),self.p.zat(-s),self.p.y],self.zr.at[self.land(i),s-1],self.p.next)
    def swap(self,i): return self.remote(i,3+self.Z,self.own.at[self.slot(i),self.p.z,self.p.y],self.fr.at[self.land(i)],self.p.over_x)
    def half(self,i): return self.o.at[i,pl.ds(al(self.p.c*self.h,self.h),self.h)]
    def share(self,i): return self.remote(i,4+self.Z,self.half(i),self.half(i),self.p.twin)
    def save(self,i,place,unit):
        index,layer,across=place; rows,wide=SUB
        ref=self.out[index] if layer is None else self.out[index].at[layer]
        return pltpu.make_async_copy(self.o.at[i],ref.at[pl.ds(al(unit//across*rows,rows),rows),pl.ds(al(lax.rem(unit,across)*wide,wide),wide)],self.os.at[i])
    def ask(self,i,k):
        if self.ring<self.n:
            @pl.when(i>=self.ring)
            def _(): pl.semaphore_wait(self.free.at[k],1)
    def tell(self,i,k,dev):
        if self.ring<self.n:
            @pl.when(i<self.n-self.ring)
            def _(): pl.semaphore_signal(self.free.at[k],inc=1,device_id=dev,device_id_type=MESH)
    def begin(self): self.p.greet()
    def phase(self,k,i):
        p=self.p; Z=self.Z; some=self.g[0].at[0]; here=self.slot(i); land=self.land(i)
        if k==0:
            self.ask(i,0)
            for at,count,ref in zip(self.at,self.counts,self.g):
                @pl.when((i>=at)&(i<at+count))
                def _(at=at,ref=ref):
                    for yy in (1,0): self.first(ref.at[i-at],i,yy).start(); self.load(ref.at[i-at],i,yy).start()
        elif k==1:
            for yy in (1,0):
                col=self.column(yy)
                self.load(some,i,yy).wait(); self.first(some,i,yy).wait_recv()
                self.own[here,:,col]=self.own[here,:,col]+self.cr[land,:,col]
                if yy: self.ask(i,1); self.cross(i).start()
            self.tell(i,0,p.twin)
        elif k==2:
            self.cross(i).wait_recv()
            ref=self.part(i,1-p.y,p.x); ref[...]=ref[...]+self.xr[land]
            self.tell(i,1,p.over_x)
            self.ask(i,2); self.side(i).start()
        elif k==3:
            self.side(i).wait_recv()
            ref=self.part(i,p.y,p.x); ref[...]=ref[...]+self.yr[land]
            self.tell(i,2,p.over_y)
            self.ask(i,3); self.hop(i,1).start()
        elif k<3+Z:
            s=k-3
            self.hop(i,s).wait_recv()
            ref=self.own.at[here,p.zat(-1-s),p.y]; ref[...]=ref[...]+self.zr[land,s-1]
            self.tell(i,2+s,p.prev)
            self.ask(i,3+s)
            (self.hop(i,s+1) if s+1<Z else self.swap(i)).start()
        elif k==3+Z:
            self.swap(i).wait_recv()
            ref=self.half(i); ref[...]=self.own[here,p.z,p.y]+self.fr[land]
            self.tell(i,2+Z,p.over_x)
            self.share(i).start()
        elif k==4+Z:
            for yy in (0,1): self.first(some,i,yy).wait_send()
            self.cross(i).wait_send(); self.side(i).wait_send()
            for s in range(1,Z): self.hop(i,s).wait_send()
            self.swap(i).wait_send(); self.share(i).wait()
            for at,count,place in zip(self.at,self.counts,self.places):
                @pl.when((i>=at)&(i<at+count))
                def _(at=at,place=place): self.save(i,place,i-at).start()
        else: self.save(i,self.places[0],0).wait()
    def relay(self,s):
        p=self.p
        ref=self.all.at[p.z,p.y] if s==0 else self.all.at[p.zat(1-s)]
        return pltpu.make_async_remote_copy(ref,ref,self.cs.at[s],self.ct.at[s],device_id=p.over_y if s==0 else p.next,device_id_type=MESH)
    def spread_common(self,k):
        p=self.p; unit,at,count=self.common
        if k==0: self.all[p.z,p.y]=self.o[unit,at:at+count]
        else: self.relay(k-1).wait()
        if k<self.Z: self.relay(k).start()
        else:
            cp=pltpu.make_async_copy(self.all,self.all_out,self.co.at[0]); cp.start(); cp.wait()
    def run(self,lo,count):
        def tick(u):
            for k in reversed(range(len(self.lag))):
                i=u-self.lag[k]
                @pl.when((i>=0)&(i<self.n))
                def _(k=k,i=i): self.phase(k,i)
            if self.common:
                for k in range(self.Z+1):
                    @pl.when(u==self.begin_common+k)
                    def _(k=k): self.spread_common(k)
        during(0,count,lambda v:tick(lo+v))
    def spread(self,step,steps):
        per=-(-self.ticks//steps)
        self.run(step*per,per)

class Gather:
    def __init__(self,S,shards,cuts,modes,lag=2,ahead=1):
        self.S=S; Z=self.Z=S//2
        pick=lambda a: a if isinstance(a,tuple) else (a,None)
        self.local=[isinstance(a,tuple) and isinstance(a[0],int) for a in shards]
        pairs=[pick(a) for a,m in zip(shards,self.local) if not m]
        held=[]; self.source=[]
        for a,layer in pairs:
            k=next((k for k,v in enumerate(held) if v is a),None)
            if k is None: k=len(held); held.append(a)
            self.source.append((k,layer))
        fold_=lambda s: s[:-2]+(2,2,s[-2]//4,s[-1])
        self.inputs=[a.reshape(fold_(a.shape)) for a in held]
        self.shapes=[a if m else pick(a)[0].shape[-2:] for a,m in zip(shards,self.local)]
        self.cuts=cuts
        self.units=[(w,a) for w,k in enumerate(cuts) for a in range(k)]
        self.modes=''.join(modes)
        n=len(self.units); k=3*Z+1
        self.out_shapes=[jax.ShapeDtypeStruct((Z,2)+fold_(a),BF) for a in self.shapes]
        self.out_specs=[pl.BlockSpec(memory_space=pl.ANY)]*len(shards)
        self.scratch=[pltpu.VMEM(fold_(a),BF) for a,m in zip(self.shapes,self.local) if m]+[pltpu.SemaphoreType.DMA((n,k)),pltpu.SemaphoreType.DMA((n,k)),pltpu.SemaphoreType.DMA((n,))]
        self.plan={}
        for t in range(1,Z): self.plan[lag*t]=('z',t)
        self.plan[lag*Z]=('y',0); self.plan[lag*(Z+1)]=('x',0); self.plan[lag*(Z+2)]=('end',0)
        self.last=lag*(Z+2)
        self.ahead=ahead
        self.ticks=n+self.last
    def bind(self,ins,outs,scr):
        mine=list(scr[:-3]); source=list(self.source); self.i=[]
        for m in self.local:
            if m: self.i.append(mine.pop(0))
            else:
                k,layer=source.pop(0)
                self.i.append(ins[k] if layer is None else ins[k].at[layer])
        self.o=outs; self.ss,self.rs,self.ls=scr[-3:]; self.p=Place(self.S); return self
    def cp(self,u,kind,t=0):
        p=self.p; Z=self.Z; h=self.modes[u]=='h'; w,a=self.units[u]
        wide=self.shapes[w][1]//self.cuts[w]; cs=pl.ds(a*wide,wide); o=self.o[w]; i=self.i[w]
        k={'z':t-1,'y':Z-1+t,'u':2*Z-1+t-1,'x':3*Z-2,'a':3*Z-1,'b':3*Z}[kind]
        if kind=='z':
            zo=p.zat(1-t); dev=p.next
            dst=o.at[zo,p.y,p.c,:,:,cs] if h else o.at[zo,p.y,p.c,p.x,:,cs]; src=dst
            if t==1: src=i.at[p.c,:,:,cs] if h else i.at[p.c,p.x,:,cs]
        elif kind=='y':
            dst=src=o.at[p.zat(-t),p.y,p.c,p.x,:,cs]; dev=p.over_y
            if t==0: src=i.at[p.c,p.x,:,cs]
        elif kind=='u': src=dst=o.at[p.zat(-t),p.y,p.c,p.x,:,cs]; dev=p.over_x
        elif kind=='x': src=dst=o.at[:,1-p.y,p.c,p.x,:,cs]; dev=p.over_x
        else: src=dst=o.at[:,p.y if kind=='a' else 1-p.y,p.c,:,:,cs]; dev=p.twin
        return pltpu.make_async_remote_copy(src,dst,self.ss.at[u,k],self.rs.at[u,k],device_id=dev,device_id_type=MESH)
    def own(self,u):
        p=self.p; w,a=self.units[u]; wide=self.shapes[w][1]//self.cuts[w]; cs=pl.ds(a*wide,wide)
        return pltpu.make_async_copy(self.i[w].at[p.c,:,:,cs],self.o[w].at[p.z,p.y,p.c,:,:,cs],self.ls.at[u])
    def open(self,u):
        self.cp(u,'z',1).start(); self.cp(u,'y',0).start(); self.own(u).start()
    def begin(self):
        self.p.greet()
        for u in range(min(self.ahead,len(self.units))): self.open(u)
    def stage(self,u,kind,t):
        Z=self.Z; q=self.modes[u]=='q'
        if kind=='z':
            self.cp(u,'z',t).wait_recv()
            if t+1<Z: self.cp(u,'z',t+1).start()
            self.cp(u,'y',t).start()
            if q: self.cp(u,'u',t).start()
        elif kind=='y':
            for t in range(Z): self.cp(u,'y',t).wait_recv()
            self.cp(u,'x').start()
            self.own(u).wait()
            if not q: self.cp(u,'a').start()
        elif kind=='x':
            if q:
                for t in range(1,Z): self.cp(u,'u',t).wait_recv()
                self.cp(u,'a').start()
            self.cp(u,'x').wait_recv(); self.cp(u,'b').start()
        else:
            for t in range(1,Z):
                self.cp(u,'z',t).wait_send()
                if q: self.cp(u,'u',t).wait_send()
            for t in range(Z): self.cp(u,'y',t).wait_send()
            self.cp(u,'x').wait_send(); self.cp(u,'a').wait(); self.cp(u,'b').wait()
    def run(self,lo,count):
        n=len(self.units)
        for i in range(lo,min(lo+count,self.ticks)):
            if self.ahead<=i+self.ahead<n: self.open(i+self.ahead)
            for u in range(n):
                s=self.plan.get(i-u)
                if s: self.stage(u,*s)
    def done(self,w):
        return max(u for u,(a,_) in enumerate(self.units) if a==w)+self.last+1

VM=60<<20
def call(body,name,grid,ins,in_specs,outs,out_specs,scratch,side=None,cid=None):
    any_=pl.BlockSpec(memory_space=pl.ANY)
    extra=side.inputs if side else []
    a,b,c,d,e=len(ins),len(extra),len(outs),len(side.out_shapes) if side else 0,len(scratch)
    def kernel(*refs):
        comm=None
        cut=np.cumsum([0,a,b,c,d,e]).tolist()
        part=[refs[x:y] for x,y in zip(cut,cut[1:]+[len(refs)])]
        if side:
            comm=side.bind(part[1],part[3],part[5])
        body(comm,*part[0],*part[2],*part[4])
    out=pl.pallas_call(kernel,grid=grid,out_shape=list(outs)+(side.out_shapes if side else []),in_specs=list(in_specs)+[any_]*b,
        out_specs=list(out_specs)+(side.out_specs if side else []),scratch_shapes=list(scratch)+(side.scratch if side else []),
        compiler_params=pltpu.CompilerParams(vmem_limit_bytes=VM,**(dict(collective_id=cid,has_side_effects=True) if side else {})),name=name)(*ins,*extra)
    return out[:c],out[c:]


CH=64

def aside(body):
    def run(comm,*refs):
        if comm:
            @pl.when(pl.program_id(0)==0)
            def _(): comm.begin()
        body(*refs)
        if comm: comm.spread(pl.program_id(0),pl.num_programs(0))
    return run
def whole(shape):
    return pl.BlockSpec(shape,lambda *i:(0,)*len(shape),pipeline_mode=pl.Buffered(1))
def chunks(steps,body):
    def run(i,c):
        body(pl.ds(pl.multiple_of(i*CH,CH),CH)); return c
    lax.fori_loop(0,steps//CH,run,0)
def stats(v):
    center=v-jnp.mean(v,axis=-1,keepdims=True)
    rstd=lax.rsqrt(jnp.mean(center*center,axis=-1,keepdims=True)+1e-5)
    return center*rstd,rstd
def norm_back(dy,gain,xhat,rstd):
    g=dy*gain
    return rstd*(g-jnp.mean(g,axis=-1,keepdims=True)-xhat*jnp.mean(g*xhat,axis=-1,keepdims=True))
def sigmoid(v): return 0.5*jnp.tanh(0.5*v)+0.5
def fold(v): return jnp.sum(v.reshape(v.shape[0]//8,8,v.shape[1]),axis=0)

PAD=32
RC=128
def over_columns(width,body):
    def run(i,c):
        body(pl.ds(pl.multiple_of(i*128,128),128)); return c
    lax.fori_loop(0,width//128,run,0)
def taps_of(taps,lead,residue):
    return [(a,k) for k in range(taps) for a in [lead(k)//8] if lead(k)%8==residue]
def slide(pad_ref,w_ref,lead,taps,t0,cols):
    acc=jnp.zeros((RC,128),F32)
    for b in range(8):
        use=taps_of(taps,lead,b)
        if not use: continue
        top=max(a for a,_ in use)
        slab=pad_ref[t0+b:t0+b+RC+8*top,cols]
        for a,k in use: acc=acc+w_ref[k:k+1,cols]*slab[8*a:8*a+RC]
    return acc

def points(comm,count):
    at=[-1]
    def point():
        if not comm: return
        if at[0]<0: comm.begin()
        else:
            per=-(-comm.ticks//count)
            comm.run(at[0]*per,per)
        at[0]+=1
    return point

def into_units(ref,rows):
    n,w=SUB; across=rows.shape[1]//w
    for a in range(rows.shape[0]//n):
        for b in range(across): ref[a*across+b,0]=rows[a*n:a*n+n,b*w:b*w+w]

def feed_back_kernel(norm,d_ref,x_ref,gain_ref,hid_ref,act_ref,dsl_ref,fi_ref,fo_ref,
        out_ref,dfi_ref,dfo_ref,dbin_ref,sums_ref,df_ref,acc_ref,turn_ref):
    steps=x_ref.shape[0]; j=pl.program_id(0)
    @pl.when(j==0)
    def _():
        sums_ref[...]=jnp.zeros_like(sums_ref)
        def body(r):
            df=(0.5*d_ref[r,:]).astype(BF)
            df_ref[r,:]=df
            sums_ref[2]+=fold(df.astype(F32))
        chunks(steps,body)
        turn_ref[...]=hid_ref[...].T
        acc_ref[...]=jnp.zeros_like(acc_ref)
    dpre=(nt(df_ref[...],fo_ref[...])*dsl_ref[...].astype(F32)).astype(BF)
    dbin_ref[...]=fold(dpre.astype(F32))
    acc_ref[...]+=nt(dpre,fi_ref[...])
    dfi_ref[0]=nn(turn_ref[...],dpre).astype(BF)
    into_units(dfo_ref,tn(act_ref[...],df_ref[...]).astype(BF))
    @pl.when(j==pl.num_programs(0)-1)
    def _():
        def body(r):
            xhat,rstd=stats(x_ref[r,:].astype(F32))
            dy=acc_ref[r,:]
            sums_ref[0]+=fold(dy*xhat); sums_ref[1]+=fold(dy)
            out_ref[r,:]=(d_ref[r,:]+norm_back(dy,gain_ref[norm:norm+1,:],xhat,rstd)).astype(out_ref.dtype)
        chunks(steps,body)

def feed_back(d,x,gains,hid,act,dsl,fi,fo,norm,out_type,side=None,cid=None):
    steps,width=x.shape; hidden=fi.shape[1]; tn_=SUB[1]; tiles=hidden//tn_; S=width//SUB[0]
    assert hidden//S==tn_
    units=tn_*width//(SUB[0]*SUB[1])
    ins=[d,x,gains,hid,act,dsl,fi,fo]
    return call(aside(functools.partial(feed_back_kernel,norm)),'feed_forward_back',(tiles,),ins,
        [whole(d.shape),whole(x.shape),whole(gains.shape),whole(hid.shape),pl.BlockSpec((steps,tn_),lambda j:(0,j)),pl.BlockSpec((steps,tn_),lambda j:(0,j)),pl.BlockSpec((width,tn_),lambda j:(0,j)),pl.BlockSpec((tn_,width),lambda j:(j,0))],
        [jax.ShapeDtypeStruct((steps,width),out_type),jax.ShapeDtypeStruct((tiles,width,tn_),BF),jax.ShapeDtypeStruct((units,S)+SUB,BF),jax.ShapeDtypeStruct((8,hidden),F32),jax.ShapeDtypeStruct((3,8,width),F32)],
        [whole((steps,width)),pl.BlockSpec((1,width,tn_),lambda j:(j,0,0)),pl.BlockSpec((units,1)+SUB,lambda j:(0,j,0,0)),pl.BlockSpec((8,tn_),lambda j:(0,j)),whole((3,8,width))],
        [pltpu.VMEM((steps,width),BF),pltpu.VMEM((steps,width),F32),pltpu.VMEM((width,steps),BF)],side,cid)

def in_units(ref,v):
    for j in range(ref.shape[0]): ref[j]=v[:,j*ref.shape[2]:(j+1)*ref.shape[2]]

def middle_back_kernel(taps,comm,d_ref,depth_ref,up_ref,chid_ref,cact_ref,mixed_ref,x2_ref,vec_ref,valid_ref,ao_ref,pi_ref,po_ref,
        dx2_ref,dpv_ref,dpo_ref,dpi_ref,dao_ref,ddw_ref,sums_ref,low_ref,wide_ref,pad_ref,tail_ref):
    steps,width=d_ref.shape
    gain_ref=vec_ref.at[Rows.gain:Rows.gain+8]; shift_ref=vec_ref.at[Rows.shift:Rows.shift+8]; dw_ref=vec_ref.at[Rows.taps:Rows.taps+32]
    point=points(comm,8)
    point()
    sums_ref[...]=jnp.zeros_like(sums_ref)
    def cast(r): low_ref[r,:width]=d_ref[r,:].astype(BF)
    chunks(steps,cast)
    wide_ref[:,:width]=nt(low_ref[:,:width],po_ref[...])
    point()
    in_units(dpo_ref,tn(cact_ref[...],low_ref[:,:width]).astype(BF))
    point()
    tail_ref[steps:steps+PAD,:]=jnp.zeros((PAD,width),F32)
    pad_ref[0:PAD,:]=jnp.zeros((PAD,width),F32)
    def three(i,c):
        r=pl.ds(pl.multiple_of(i*CH,CH),CH)
        xhat,rstd=stats(depth_ref[r,:])
        gain=gain_ref[3:4,:]
        z=xhat*gain+shift_ref[3:4,:]
        sg=sigmoid(z)
        dz=wide_ref[r,:width]*(sg*(1.0+z*(1.0-sg)))
        sums_ref[0]+=fold(dz*xhat); sums_ref[1]+=fold(dz)
        tail_ref[r,:]=norm_back(dz,gain,xhat,rstd)
        pad_ref[pl.ds(pl.multiple_of(i*CH+PAD,PAD),CH),:]=up_ref[r,:width].astype(F32)*sigmoid(up_ref[r,width:].astype(F32))*valid_ref[r,0:1]
        return c
    lax.fori_loop(0,steps//CH,three,0)
    point()
    def conv(cols):
        for t0 in range(0,steps,RC):
            wide_ref[t0:t0+RC,cols]=slide(tail_ref,dw_ref,lambda k:taps-1-k,taps,t0,cols)
        lead=lambda k:k+PAD-taps+1
        for b in range(8):
            use=taps_of(taps,lead,b)
            if not use: continue
            top=max(a for a,_ in use)
            parts={k:jnp.zeros((8,128),F32) for _,k in use}
            for t0 in range(0,steps,RC):
                slab=pad_ref[t0+b:t0+b+RC+8*top,cols]
                dd=tail_ref[t0:t0+RC,cols]
                for a,k in use: parts[k]=parts[k]+fold(slab[8*a:8*a+RC]*dd)
            for k,v in parts.items(): ddw_ref[k:k+1,cols]=jnp.sum(v,axis=0,keepdims=True)
    over_columns(width,conv)
    point()
    def gate(r):
        a=up_ref[r,:width].astype(F32); sg=sigmoid(up_ref[r,width:].astype(F32))
        dg=wide_ref[r,:width]*valid_ref[r,0:1]*sg
        low_ref[r,:width]=dg.astype(BF)
        low_ref[r,width:]=(dg*a*(1.0-sg)).astype(BF)
    chunks(steps,gate)
    in_units(dpi_ref,tn(chid_ref[...],low_ref[...]).astype(BF))
    point()
    wide_ref[:,:width]=nt(low_ref[...],pi_ref[...])
    point()
    def two(r):
        xhat,rstd=stats(x2_ref[r,:])
        dy=wide_ref[r,:width]
        sums_ref[2]+=fold(dy*xhat); sums_ref[3]+=fold(dy)
        dx=d_ref[r,:]+norm_back(dy,gain_ref[2:3,:],xhat,rstd)
        dx2_ref[r,:]=dx
        da=dx.astype(BF)
        low_ref[r,:width]=da
        sums_ref[4]+=fold(da.astype(F32))
    chunks(steps,two)
    point()
    dpv_ref[...]=nt(low_ref[:,:width],ao_ref[...]).astype(BF)
    in_units(dao_ref,tn(mixed_ref[...],low_ref[:,:width]).astype(BF))
    point()

def middle_back(d,depth,up,chid,cact,mixed,x2,vec,valid,ao,pi,po,taps,side=None,cid=None):
    steps,width=d.shape
    ins=[d,depth,up,chid,cact,mixed,x2,vec,valid,ao,pi,po]
    S=jax.ShapeDtypeStruct
    unit=lambda w: S((w.shape[1]//SUB[1],w.shape[0],SUB[1]),BF)
    outs=[S((steps,width),F32),S((steps,width),BF),unit(po),unit(pi),unit(ao),S((32,width),F32),S((5,8,width),F32)]
    return call(functools.partial(middle_back_kernel,taps),'convolution_module_back',(1,),ins,[whole(a.shape) for a in ins],outs,[whole(o.shape) for o in outs],
        [pltpu.VMEM((steps,2*width),BF),pltpu.VMEM((steps,width),F32),pltpu.VMEM((steps+PAD,width),F32),pltpu.VMEM((steps+PAD,width),F32)],side,cid)


def late_kernel(taps,size,vector_rows,comm,q_ref,k_ref,v_ref,p_ref,g_ref,table_ref,pick_ref,hid1_ref,ai_ref,dx2_ref,x1_ref,gain_ref,
        hid0_ref,act_ref,dsl_ref,fi_ref,fo_ref,x_ref,s5_ref,s4_ref,s23_ref,ddw_ref,dbin1_ref,out_ref,
        ds_ref,dpk_ref,dtab_ref,psum_ref,acc_ref,turn_ref,dx1_ref,df_ref,stage_ref,dbin_ref,sums_ref,vec_ref,stage_sem,left_sem):
    steps,width=x1_ref.shape; wide=SUB[1]; S=comm.S
    A=width//128; B=3*width//wide; C=act_ref.shape[1]//wide; D=C
    j=pl.program_id(0)
    made_ai,made_fi,made_small,made_fo=comm.makes
    @pl.when(j==0)
    def _():
        comm.begin()
        dtab_ref[...]=jnp.zeros_like(dtab_ref)
    def put(q,ref):
        return pltpu.make_async_copy(stage_ref.at[lax.rem(q,2)],ref,stage_sem.at[lax.rem(q,2)])
    def unit(q,value,ref):
        @pl.when(q>=2)
        def _(): put(q,ref).wait()
        stage_ref[lax.rem(q,2)]=value.reshape(stage_ref.shape[1:])
        put(q,ref).start()
    def lefts(a,slot):
        rows=act_ref.shape[1]//S
        return [pltpu.make_async_copy(act_ref.at[:,pl.ds(al(s*rows+a*SUB[0],SUB[0]),SUB[0])],dpk_ref.at[slot,:,pl.ds(s*SUB[0],SUB[0])],left_sem.at[slot,s]) for s in range(S)]
    @pl.when(j<A)
    def _():
        flip=(lax.broadcasted_iota(jnp.int32,(QB,QB),0)+lax.broadcasted_iota(jnp.int32,(QB,QB),1)==QB-1).astype(F32).astype(BF)
        here=pl.ds(al(j*128,128),128)
        parts=[]
        for hh in range(128//size):
            cols=slice(hh*size,(hh+1)*size)
            parts.append(one_head_back(q_ref,k_ref,v_ref,p_ref.at[hh],g_ref,table_ref,pick_ref,dtab_ref,ds_ref,flip,cols))
            comm.run(j*2+hh,1)
        for part in range(3):
            dpk_ref[part,:,here]=jnp.concatenate([a[part] for a in parts],axis=1)
        psum_ref[0:1,here]=jnp.sum(dpk_ref[0,:,here].astype(F32),axis=0,keepdims=True)
        psum_ref[1:2,here]=jnp.sum(dpk_ref[2,:,here].astype(F32),axis=0,keepdims=True)
    @pl.when((j>=A)&(j<A+B))
    def _():
        b=j-A; per=width//wide
        @pl.when(b==0)
        def _():
            turn_ref[...]=hid1_ref[...].T
            acc_ref[...]=jnp.zeros_like(acc_ref)
            sums_ref[...]=jnp.zeros_like(sums_ref)
        g=dpk_ref[b//per,:,pl.ds(al(lax.rem(b,per)*wide,wide),wide)]
        acc_ref[...]+=nt(g,ai_ref[...])
        unit(b,nn(turn_ref[...],g).astype(BF),made_ai.at[b])
        @pl.when(b==B-1)
        def _():
            for a in range(3):
                for cp in lefts(a,a): cp.start()
            turn_ref[...]=hid0_ref[...].T
            def body(r):
                xhat,rstd=stats(x1_ref[r,:])
                dy=acc_ref[r,:]
                sums_ref[0]+=fold(dy*xhat); sums_ref[1]+=fold(dy)
                dx=dx2_ref[r,:]+norm_back(dy,gain_ref[1:2,:],xhat,rstd)
                dx1_ref[r,:]=dx
                df=(0.5*dx).astype(BF)
                df_ref[r,:]=df
                sums_ref[4]+=fold(df.astype(F32))
            chunks(steps,body)
            acc_ref[...]=jnp.zeros_like(acc_ref)
        comm.run(2*A+b,1)
    @pl.when((j>=A+B)&(j<A+B+C))
    def _():
        c=j-A-B
        dpre=(nt(df_ref[...],fo_ref[...])*dsl_ref[...].astype(F32)).astype(BF)
        dbin_ref[:,pl.ds(al(c*wide,wide),wide)]=fold(dpre.astype(F32))
        acc_ref[...]+=nt(dpre,fi_ref[...])
        unit(B+c,nn(turn_ref[...],dpre).astype(BF),made_fi.at[c])
        @pl.when(c==C-1)
        def _():
            def body(r):
                xhat,rstd=stats(x_ref[r,:].astype(F32))
                dy=acc_ref[r,:]
                sums_ref[2]+=fold(dy*xhat); sums_ref[3]+=fold(dy)
                out_ref[r,:]=(dx1_ref[r,:]+norm_back(dy,gain_ref[0:1,:],xhat,rstd)).astype(BF)
            chunks(steps,body)
            vec_ref[...]=jnp.zeros_like(vec_ref)
            total=lambda v: jnp.sum(v,axis=0,keepdims=True)
            rows=[sums_ref[2],sums_ref[0],s23_ref[2],s23_ref[0],s4_ref[0],s5_ref[0],sums_ref[3],sums_ref[1],s23_ref[3],s23_ref[1],s4_ref[1],s5_ref[1],sums_ref[4],s4_ref[2]]
            rows=[total(v) for v in rows]+[psum_ref[0:1,:],psum_ref[1:2,:],total(s23_ref[4])]
            L=width//S
            for i,v in enumerate(rows):
                for s in range(S): vec_ref[s,i:i+1,0:L]=v[:,s*L:s*L+L]
            k=len(rows)
            for i,ref in enumerate((dbin_ref,dbin1_ref)):
                v=total(ref[...])
                for s in range(S): vec_ref[s,k+i:k+i+1,:]=v[:,s*wide:s*wide+wide]
            for s in range(S):
                vec_ref[s,32:32+taps,0:L]=ddw_ref[0:taps,s*L:s*L+L]
                n=dtab_ref.shape[0]//S
                vec_ref[s,vector_rows:vector_rows+n,0:size]=dtab_ref[s*n:s*n+n,:]
        comm.run(2*A+B+c,1)
    @pl.when((j>=A+B+C)&(j<A+B+C+D))
    def _():
        d=j-A-B-C; across=width//wide
        @pl.when(d==0)
        def _(): unit(B+C,vec_ref[...].astype(BF).reshape(S*SUB[0],wide),made_small.at[0])
        a=d//across
        for slot in range(3):
            @pl.when((lax.rem(a,3)==slot)&(lax.rem(d,across)==0))
            def _(slot=slot):
                for cp in lefts(a,slot): cp.wait()
        unit(B+C+1+d,tn(dpk_ref[lax.rem(a,3)],df_ref[:,pl.ds(al(lax.rem(d,across)*wide,wide),wide)]).astype(BF),made_fo.at[d])
        @pl.when(d==across-1)
        def _():
            for a in range(3,D//across):
                for cp in lefts(a,a-3): cp.start()
        comm.run(2*A+B+C+d,1)
    @pl.when(j==A+B+C+D)
    def _():
        for q in (0,1): put(B+C+D+1+q,made_fo.at[0]).wait()
        lo=2*A+B+C+D
        comm.run(lo,comm.ticks-lo)

def one_head_back(q_ref,k_ref,v_ref,p_ref,g_ref,table_ref,pick_ref,dtab_ref,ds_ref,flip,cols):
    steps=q_ref.shape[0]; nb=steps//QB; span=steps+QB; size=cols.stop-cols.start
    scale=1.0/math.sqrt(size)
    k=k_ref[:,cols]; v=v_ref[:,cols]; dqs=[]
    for i in range(nb):
        rows=slice(i*QB,(i+1)*QB)
        q=q_ref[rows,cols]
        p=p_ref[rows,:].astype(F32)
        t=p*nt(g_ref[rows,cols],v)
        ds=(t-p*jnp.sum(t,axis=1,keepdims=True)).astype(BF)
        ds_ref[rows,:]=ds
        wide=jnp.concatenate([nn(flip,ds),jnp.zeros((QB,span-steps),F32)],axis=1)
        back=pltpu.roll(wide,span-QB+1,1,stride=1,stride_axis=0).astype(BF)
        drel=nn(flip,(nt(back,pick_ref[i])*scale).astype(BF)).astype(BF)
        dqs.append((nn(ds,k)*scale+nn(drel,table_ref[...])).astype(BF))
        dtab_ref[...]+=tn(drel,q)
    return jnp.concatenate(dqs,axis=0),(tn(ds_ref[...],q_ref[:,cols])*scale).astype(BF),tn(p_ref[...],g_ref[:,cols]).astype(BF)

VECTOR_ROWS=64
def late(S,packed,p,grad,table,pick,heads,hid1,ai,dx2,x1,gains,hid0,act,dsl,fi,fo,tokens,s5,s4,s23,ddw,dbin1,taps,ready,places,out_shapes,cid):
    steps,width=x1.shape; size=width//heads; wide=SUB[1]
    A=width//128; B=3*width//wide; C=act.shape[1]//wide; D=C; per=128//size
    assert act.shape[1]//S==wide and width//S==SUB[0] and wide//SUB[0]<=4
    comm=Scatter(S,ready+[B,C,1,D],places,out_shapes,common=(sum(a.shape[0] for a in ready)+B+C,VECTOR_ROWS,table.shape[0]//S))
    head=lambda o:pl.BlockSpec((steps,128),lambda j:(0,o*A+jnp.minimum(j,A-1)))
    tile=lambda lo,n:(lambda j:jnp.minimum(jnp.maximum(j-lo,0),n-1))
    tb,tc=tile(A,B),tile(A+B,C)
    ins=[packed,packed,packed,p,grad,table,pick,hid1,ai,dx2,x1,gains,hid0,act,dsl,fi,fo,tokens,s5,s4,s23,ddw,dbin1]
    specs=[head(0),head(1),head(2),pl.BlockSpec((per,steps,steps),lambda j:(jnp.minimum(j,A-1),0,0)),head(0),whole(table.shape),whole(pick.shape),
        whole(hid1.shape),pl.BlockSpec((width,wide),lambda j:(0,tb(j))),whole(dx2.shape),whole(x1.shape),whole(gains.shape),whole(hid0.shape),pl.BlockSpec(memory_space=pl.ANY),
        pl.BlockSpec((steps,wide),lambda j:(0,tc(j))),pl.BlockSpec((width,wide),lambda j:(0,tc(j))),pl.BlockSpec((wide,width),lambda j:(tc(j),0)),whole(tokens.shape)]
    specs+=[whole(a.shape) for a in (s5,s4,s23,ddw,dbin1)]
    V=pltpu.VMEM; Z=S//2
    scratch=[V((steps,steps),BF),V((3,steps,width),BF),V((128,size),F32),V((8,width),F32),V((steps,width),F32),V((width,steps),BF),V((steps,width),F32),V((steps,width),BF),
        V((2,Z,2,2,SUB[0]//2,wide),BF),V((8,act.shape[1]),F32),V((5,8,width),F32),V((S,)+SUB,F32),pltpu.SemaphoreType.DMA((2,)),pltpu.SemaphoreType.DMA((3,S))]
    return call(functools.partial(late_kernel,taps,size,VECTOR_ROWS),'attend_back_and_sums',(A+B+C+D+1,),ins,specs,[jax.ShapeDtypeStruct((steps,width),BF)],[whole((steps,width))],scratch,comm,cid)

class Rows:
    gain=0; shift=8; inner=16; outer=24; packed=26; mixed=28; taps=32; count=64

def early_kernel(heads,taps,comm,gain_in,shift_in,inner_in,outer_in,packed_in,mixed_in,taps_in,tok_ref,cot_ref,valid_ref,mask_ref,table_ref,pick_ref,
        hid0_ref,act0_ref,dsl0_ref,x1_ref,hid1_ref,packed_ref,mixed_ref,p_ref,x2_ref,chid_ref,up_ref,depth_ref,cact_ref,x3_ref,hid4_ref,act1_ref,dsl1_ref,dx4_ref,res_ref,s5_ref,vec_ref,
        own_ref,land_ref,land_sem,acc_ref,wa_ref,wb_ref,sem_a,sem_b,rel_ref,qkv_ref,pad_ref,wide_ref):
    steps,width=tok_ref.shape; tile=wa_ref.shape[-1]; S=comm.S
    small,fi0,fo0,ai,ao,pi,po,fi1,fo1=comm.o
    F,B,M0,M1,M2=[w.shape[-1]//tile for w in (fi0,ai,ao,pi,po)]; A=width//128
    size=width//heads
    cut=np.cumsum([0,F,B,A,M0,M1,M2,F]).tolist()
    j=pl.program_id(0)
    L=width//S
    def row(i): return vec_ref[i:i+1,:]
    def column(w,i,slot): return pltpu.make_async_copy(w.at[:,:,:,:,:,pl.ds(al(i*tile,tile),tile)],wa_ref.at[slot],sem_a.at[slot])
    def band(w,i,slot): return pltpu.make_async_copy(w.at[i//2,lax.rem(i,2)],wb_ref.at[slot],sem_b.at[slot])
    def wa(slot): return wa_ref[slot].reshape(width,tile)
    want=[comm.done(2),comm.done(3),comm.done(4),comm.done(5),comm.done(6),comm.done(8)]
    at={}; done=want[0]
    times=[20/F]*F+[10/B]*B+[35/A]*A+[3]*M0+[2]*(M1-1)+[14]+[3]*M2
    need={cut[1]-1:want[1],cut[3]-1:want[2],cut[4]-1:want[3],cut[5]-1:want[4],cut[6]-1:comm.ticks-1}
    for st in range(cut[6]):
        target=want[0]+int((comm.ticks-1-want[0])*sum(times[:st+1])/sum(times))
        target=max(target,need.get(st,0))
        if target>done: at[st]=(done,target-done); done=target
    def ticks():
        for st,(lo,n) in at.items():
            @pl.when(j==st)
            def _(lo=lo,n=n): comm.run(lo,n)
    @pl.when(j==0)
    def _():
        own_ref[...]=jnp.zeros_like(own_ref)
        for at_,ref in ((Rows.gain,gain_in),(Rows.shift,shift_in),(Rows.outer,outer_in),(Rows.packed,packed_in),(Rows.mixed,mixed_in),(Rows.taps,taps_in)):
            own_ref[at_:at_+ref.shape[0],:]=ref[...].astype(F32)
        k=inner_in.shape[1]//L
        for l in range(2):
            for i in range(k): own_ref[Rows.inner+l*k+i:Rows.inner+l*k+i+1,:]=inner_in[l:l+1,i*L:i*L+L].astype(F32)
        comm.i[0][...]=own_ref[...].astype(BF).reshape(comm.i[0].shape)
        comm.begin()
        comm.run(0,want[0])
        cp=pltpu.make_async_copy(small,land_ref,land_sem.at[0]); cp.start()
        column(fi0,0,0).start(); band(fo0,0,0).start()
        cp.wait()
        for s in range(S): vec_ref[:,s*L:s*L+L]=land_ref[s//2,s%2].reshape(Rows.count,L).astype(F32)
        for i in range(steps//QB): rel_ref[i]=tn(table_ref[...],pick_ref[i]).astype(BF)
        def body(r):
            xhat,_r=stats(tok_ref[r,:].astype(F32))
            hid0_ref[r,:]=(xhat*row(Rows.gain)+row(Rows.shift)).astype(BF)
        chunks(steps,body)
        acc_ref[...]=jnp.zeros_like(acc_ref)
        pad_ref[0:PAD,:]=jnp.zeros((PAD,width),F32)
    def feed_tile(i,tau,l,hid_ref,act_ref,dsl_ref,fi,fo):
        slot=lax.rem(tau,2); k=tile//L
        column(fi,i,slot).wait(); band(fo,i,lax.rem(i,2)).wait()
        @pl.when(i+1<F)
        def _(): column(fi,i+1,lax.rem(tau+1,2)).start(); band(fo,i+1,lax.rem(i+1,2)).start()
        bias=jnp.concatenate([vec_ref[Rows.inner+l*k+a:Rows.inner+l*k+a+1,pl.ds(al(i*L,L),L)] for a in range(k)],axis=1)
        pre=nn(hid_ref[...],wa(slot))+bias
        sg=sigmoid(pre)
        act_ref[...]=(pre*sg).astype(BF)
        dsl_ref[...]=(sg*(1.0+pre*(1.0-sg))).astype(BF)
        acc_ref[...]+=nn(act_ref[...],wb_ref[lax.rem(i,2)].reshape(tile,width))
    @pl.when(j<cut[1])
    def _(): feed_tile(j,j,0,hid0_ref,act0_ref,dsl0_ref,fi0,fo0)
    @pl.when(j==cut[1]-1)
    def _():
        def body(r):
            x=tok_ref[r,:].astype(F32)+0.5*(acc_ref[r,:]+row(Rows.outer))
            x1_ref[r,:]=x
            xhat,_r=stats(x)
            hid1_ref[r,:]=(xhat*row(Rows.gain+1)+row(Rows.shift+1)).astype(BF)
        chunks(steps,body)
    def stream(w,lo,n,tau0,use):
        @pl.when((j>=lo)&(j<lo+n))
        def _():
            i=j-lo; slot=lax.rem(tau0+i,2)
            column(w,i,slot).wait()
            @pl.when(i+1<n)
            def _(): column(w,i+1,lax.rem(tau0+i+1,2)).start()
            use(i,slot)
    def after(step,w,tau):
        @pl.when(j==step)
        def _(): column(w,0,lax.rem(tau,2)).start()
    def here(i): return pl.ds(al(i*tile,tile),tile)
    def pack(i,slot):
        v=nn(hid1_ref[...],wa(slot))
        per=width//tile
        @pl.when(i<per)
        def _(): packed_ref[:,here(i)]=(v+vec_ref[Rows.packed:Rows.packed+1,here(lax.rem(i,per))]).astype(BF)
        @pl.when((i>=per)&(i<2*per))
        def _(): packed_ref[:,here(i)]=v.astype(BF)
        @pl.when(i>=2*per)
        def _(): packed_ref[:,here(i)]=(v+vec_ref[Rows.packed+1:Rows.packed+2,here(lax.rem(i,per))]).astype(BF)
    stream(ai,cut[1],B,F,pack)
    @pl.when((j>=cut[2])&(j<cut[3]))
    def _():
        h=j-cut[2]
        for a in range(3): qkv_ref[a]=packed_ref[:,pl.ds(al(a*width+h*128,128),128)]
        scale=1.0/math.sqrt(size)
        for i in range(steps//QB):
            rows=slice(i*QB,(i+1)*QB); outs=[]
            for hh in range(128//size):
                cols=slice(hh*size,(hh+1)*size)
                q=qkv_ref[0,rows,cols]
                rel=pltpu.roll(nn(q,rel_ref[i]),0,1,stride=1,stride_axis=0)[:,:steps]
                s=(nt(q,qkv_ref[1,:,cols])+rel)*scale+mask_ref[0:1,:]
                e=jnp.exp(s-jnp.max(s,axis=1,keepdims=True))
                p=(e*(1.0/jnp.sum(e,axis=1,keepdims=True))).astype(BF)
                p_ref[hh,rows,:]=p
                outs.append(nn(p,qkv_ref[2,:,cols]).astype(BF))
            mixed_ref[rows,pl.ds(al(h*128,128),128)]=jnp.concatenate(outs,axis=1)
    def join(i,slot):
        x2_ref[:,here(i)]=x1_ref[:,here(i)]+nn(mixed_ref[...],wa(slot))+vec_ref[Rows.mixed:Rows.mixed+1,here(i)]
        @pl.when(i==M0-1)
        def _():
            def body(r):
                xhat,_r=stats(x2_ref[r,:])
                chid_ref[r,:]=(xhat*row(Rows.gain+2)+row(Rows.shift+2)).astype(BF)
            chunks(steps,body)
    stream(ao,cut[3],M0,F+B,join)
    def raise_(i,slot):
        wide_ref[:,here(i)]=nn(chid_ref[...],wa(slot))
        @pl.when(i==M1-1)
        def _():
            def gate(k,c):
                r=pl.ds(pl.multiple_of(k*CH,CH),CH)
                a=wide_ref[r,:width]; b=wide_ref[r,width:]
                up_ref[r,:width]=a.astype(BF); up_ref[r,width:]=b.astype(BF)
                pad_ref[pl.ds(pl.multiple_of(k*CH+PAD,PAD),CH),:]=a*sigmoid(b)*valid_ref[r,0:1]
                return c
            lax.fori_loop(0,steps//CH,gate,0)
            weights=vec_ref.at[Rows.taps:Rows.taps+32]
            def conv(cols):
                for t0 in range(0,steps,RC):
                    depth_ref[t0:t0+RC,cols]=slide(pad_ref,weights,lambda k:k+PAD-taps+1,taps,t0,cols)
            over_columns(width,conv)
            def body(r):
                xhat,_r=stats(depth_ref[r,:])
                z=xhat*row(Rows.gain+3)+row(Rows.shift+3)
                cact_ref[r,:]=(z*sigmoid(z)).astype(BF)
            chunks(steps,body)
    stream(pi,cut[4],M1,F+B+M0,raise_)
    def lower(i,slot):
        x3_ref[:,here(i)]=x2_ref[:,here(i)]+nn(cact_ref[...],wa(slot))
        @pl.when(i==M2-1)
        def _():
            def body(r):
                xhat,_r=stats(x3_ref[r,:])
                hid4_ref[r,:]=(xhat*row(Rows.gain+4)+row(Rows.shift+4)).astype(BF)
            chunks(steps,body)
            acc_ref[...]=jnp.zeros_like(acc_ref)
    stream(po,cut[5],M2,F+B+M0+M1,lower)
    ticks()
    tau=F+B+M0+M1+M2
    after(cut[1]-1,ai,F); after(cut[3]-1,ao,F+B); after(cut[4]-1,pi,F+B+M0); after(cut[5]-1,po,F+B+M0+M1)
    @pl.when(j==cut[6]-1)
    def _():
        comm.run(comm.ticks-1,1)
        column(fi1,0,tau%2).start(); band(fo1,0,0).start()
    @pl.when(j>=cut[6])
    def _(): feed_tile(j-cut[6],tau+j-cut[6],1,hid4_ref,act1_ref,dsl1_ref,fi1,fo1)
    @pl.when(j==cut[7]-1)
    def _():
        s5_ref[...]=jnp.zeros_like(s5_ref)
        def body(r):
            y=x3_ref[r,:]+0.5*(acc_ref[r,:]+row(Rows.outer+1))
            xhat,rstd=stats(y)
            ok=valid_ref[r,0:1]
            gain=row(Rows.gain+5)
            res_ref[r,:]=((xhat*gain+row(Rows.shift+5))*ok).astype(BF)
            dy=cot_ref[r,:].astype(F32)*ok
            dx4_ref[r,:]=norm_back(dy,gain,xhat,rstd)
            s5_ref[0]+=fold(dy*xhat)
            s5_ref[1]+=fold(dy)
        chunks(steps,body)

LAG=2; CUTS=[1,4,4,3,1,2,1,4,4]; MODES=['h','qhhq','hhqh','hqh','h','qh','h','qhhq','hhqh']
def early(S,vectors,tokens,cot,valid,mask,table,pick,heads,weights,cid):
    steps,width=tokens.shape; tile=512; taps=vectors[-1].shape[0]; L=vectors[0].shape[1]
    comm=Gather(S,[(Rows.count,L)]+weights,cuts=CUTS,modes=MODES,lag=LAG)
    hidden=comm.shapes[1][1]; size=width//heads
    F,B,A=hidden//tile,comm.shapes[3][1]//tile,width//128
    M=[comm.shapes[i][1]//tile for i in (4,5,6)]
    assert comm.shapes[2][0]*S==hidden and tile==hidden//S
    cut=np.cumsum([0,F,B,A]+M+[F]).tolist()
    within=lambda lo,n:(lambda j:jnp.minimum(jnp.maximum(j-lo,0),n-1))
    f0,at,f1=within(0,F),within(cut[2],A),within(cut[6],F)
    ins=list(vectors)+[tokens,cot,valid,mask,table,pick]
    D=jax.ShapeDtypeStruct
    b=D((steps,width),BF); f=D((steps,width),F32); hid=D((steps,hidden),BF)
    outs=[b,hid,hid,f,b,D((steps,3*width),BF),b,D((heads,steps,steps),BF),f,b,D((steps,2*width),BF),f,b,f,b,hid,hid,f,b,D((2,8,width),F32),D((Rows.count,width),F32)]
    specs=[whole(o.shape) for o in outs]
    for i,t in ((1,f0),(2,f0),(15,f1),(16,f1)): specs[i]=pl.BlockSpec((steps,tile),lambda j,t=t:(0,t(j)))
    specs[7]=pl.BlockSpec((128//size,steps,steps),lambda j:(at(j),0,0))
    V=pltpu.VMEM; sem=lambda n: pltpu.SemaphoreType.DMA((n,))
    scratch=[V((Rows.count,L),F32),V(comm.out_shapes[0].shape,BF),sem(1),V((steps,width),F32),V((2,)+comm.out_shapes[1].shape[:-1]+(tile,),BF),V((2,)+comm.out_shapes[2].shape[2:],BF),sem(2),sem(2),
        V((steps//QB,size,steps+QB),BF),V((3,steps,128),BF),V((steps+PAD,width),F32),V((steps,2*width),F32)]
    out=call(functools.partial(early_kernel,heads,taps),'gather_and_forward',(cut[-1],),ins,[whole(a.shape) for a in ins],outs,specs,scratch,comm,cid)
    return out[0],[a.reshape(-1,a.shape[-1]) for a in out[1]]


def local(S,R,tokens,lengths,cotangent,norm_gain,norm_shift,feed_in,feed_in_bias,feed_out,feed_out_bias,attention_in,attention_in_bias,attention_out,attention_out_bias,relative_table,pointwise_in,depthwise,pointwise_out):
    steps,width=tokens.shape; taps=depthwise.shape[0]
    live=jnp.arange(steps,dtype=jnp.int32)<lengths[0]
    valid=jnp.broadcast_to(live.astype(F32)[:,None],(steps,128))
    mask=jnp.broadcast_to(jnp.where(live,0.0,-1e30).astype(F32)[None,:],(8,steps))
    rows=relative_table.shape[0]
    table=jnp.pad(relative_table,((0,128-rows),(0,0)))
    pick=jnp.asarray(picker_table(steps,QB).astype(np.float32)).astype(BF)
    vectors=[norm_gain,norm_shift,feed_in_bias,feed_out_bias,attention_in_bias,attention_out_bias.reshape(1,-1),depthwise]
    weights=[(feed_in,0),(feed_out,0),attention_in,attention_out,pointwise_in,pointwise_out,(feed_in,1),(feed_out,1)]
    outs,full=early(S,vectors,tokens,cotangent,valid,mask,table,pick,HEADS,weights,0)
    hid0,act0,dsl0,x1,hid1,packed,mixed,p,x2,chid,up,depth,cact,x3,hid4,act1,dsl1,dx4,result,s5,vec=outs
    fi0,fo0,ai,ao,pi,po,fi1,fo1=full[1:]
    flat=lambda a:a.reshape(a.shape[0],S*SUB[0],SUB[1])
    (dx3,dfi1,dfo1,dbin1,s4),_=feed_back(dx4,x3,vec,hid4,act1,dsl1,fi1,fo1,4,F32)
    (dx2,dpv,dpo,dpi,dao,ddw,s23),_=middle_back(dx3,depth,up,chid,cact,mixed,x2,vec,valid,ao,pi,po,taps)
    ready=[dfi1,flat(dfo1),dpo,dpi,dao]
    across=width//SUB[1]; k=dfi1.shape[0]
    places=[(0,1,k),(1,1,across),(5,None,across),(4,None,2*across),(3,None,across),(2,None,3*across),(0,0,k),(6,None,1),(1,0,across)]
    shapes=[feed_in.shape,feed_out.shape]+[a.shape for a in (attention_in,attention_out,pointwise_in,pointwise_out)]+[SUB]
    (dtok,),outs=late(S,packed,p,dpv,table,pick,HEADS,hid1,ai,dx2,x1,vec,hid0,act0,dsl0,fi0,fo0,tokens,s5,s4,s23,ddw,dbin1,taps,ready,places,shapes,7)
    sums=list(outs[:7])+[outs[-1]]
    if R>4:
        groups=[[g*4+i for g in range(R//4)] for i in range(4)]
        sums=[lax.psum(a,'rep',axis_index_groups=groups) for a in sums]
    gfi,gfo,gai,gao,gpi,gpo,small,common=[a.astype(F32) for a in sums]
    L=norm_gain.shape[1]
    ggain,gshift,gbout,gpbias,gmbias=[small[a:b,:L] for a,b in ((0,6),(6,12),(12,14),(14,16),(16,17))]
    gbin=small[17:19]; gdw=small[32:32+taps,:L]
    gtab=common.reshape(-1,SUB[1])[:rows,:relative_table.shape[1]]
    return (result,dtok,ggain,gshift,gfi,gbin,gfo,gbout,gai,gpbias,gao,gmbias[0],gtab,gpi,gdw,gpo)

HEADS=16

def solution(mesh):
    R,S=mesh.shape['rep'],mesh.shape['shard']
    rows=P(('rep','shard'),None)
    last,mid,first=P(None,'shard'),P(None,'shard',None),P('shard',None)
    weights=(last,last,mid,last,mid,last,first,last,first,P('shard'),P(),first,last,first)
    return jax.shard_map(functools.partial(local,S,R),mesh=mesh,in_specs=(rows,P(('rep','shard')),rows)+weights,out_specs=(rows,rows)+weights,check_vma=False)
```

```python
import functools, math
import numpy as np
import jax, jax.numpy as jnp
from jax import lax
from jax.experimental import pallas as pl
from jax.experimental.pallas import tpu as pltpu
from jax.sharding import PartitionSpec as P
LEFT=64; RIGHT=8
BF=jnp.bfloat16; F32=jnp.float32

def nn(a,b): return lax.dot_general(a,b,(((1,),(0,)),((),())),preferred_element_type=F32)
def nt(a,b): return lax.dot_general(a,b,(((1,),(1,)),((),())),preferred_element_type=F32)
def tn(a,b): return lax.dot_general(a,b,(((0,),(0,)),((),())),preferred_element_type=F32)

def picker_table(steps, block):
    span=steps+block
    n=np.arange(span)
    rows=[]
    for i in range(steps//block):
        off=np.where(n<steps, n, n-span)-block*i
        row=np.clip(off,-LEFT,RIGHT)+LEFT
        rows.append(np.arange(128)[:,None]==row[None,:])
    return np.stack(rows)

QB=128

MESH=pl.DeviceIdType.MESH
def al(v,m): return pl.multiple_of(v,m)
def during(lo,hi,body):
    def run(i,c):
        body(i); return c
    lax.fori_loop(lo,hi,run,0)

class Place:
    def __init__(self,S):
        self.S=S; self.Z=S//2
        r=lax.axis_index('rep'); s=lax.axis_index('shard')
        self.r,self.s=r,s
        self.c=lax.rem(r,2); self.x=lax.rem(r//2,2); self.y=lax.rem(s,2); self.z=s//2
        base=r-2*self.x-self.c
        self.d=1-2*self.c
        self.next=(r,2*self.zat(1)+self.y); self.prev=(r,2*self.zat(-1)+self.y)
        self.over_y=(r,2*self.z+1-self.y); self.over_x=(base+2*(1-self.x)+self.c,s); self.twin=(base+2*self.x+1-self.c,s)
    def zat(self,k): return lax.rem(self.z+self.d*k+2*self.Z,self.Z)
    def greet(self):
        bar=pltpu.get_barrier_semaphore()
        for dev in (self.next,self.prev,self.over_y,self.over_x,self.twin):
            pl.semaphore_signal(bar,inc=1,device_id=dev,device_id_type=MESH)
        pl.semaphore_wait(bar,5)

SUB=(128,512)
class Scatter:
    OWN=18; RING=6; GAP=2
    def __init__(self,S,counts,places,out_shapes,common=None,pause=None):
        self.places=places; self.counts=counts
        self.common=common
        self.S=S; Z=S//2
        n=self.n=sum(counts)
        (rows,wide)=SUB
        h,q=rows//2,rows//4
        self.h,self.q,self.Z=h,q,Z
        self.at=np.cumsum([0]+counts).tolist()
        self.inputs=[]
        self.finals=len(out_shapes)
        self.out_shapes=[jax.ShapeDtypeStruct(a,BF) for a in out_shapes]+[jax.ShapeDtypeStruct((n,Z,2,2,h,wide),BF)]
        G=self.GAP
        self.lag=[0]+[G*k for k in range(1,5+Z)]
        self.lag[4+Z]=self.lag[3+Z]+1
        self.lag.append(self.lag[4+Z]+1)
        self.gate,self.wait=pause or (n,0)
        self.ticks=n+self.wait+self.lag[-1]
        own,ring=min(n,self.OWN),min(n,self.RING)
        self.slots=own; self.ring=ring
        assert own>self.lag[-1] and n+self.wait<2*(self.gate+self.wait)
        V=lambda *d: pltpu.VMEM(d,BF)
        self.scratch=[V(n,rows,wide),V(own,Z,2,h,wide),V(ring,Z,2,h,wide),V(ring,Z,q,wide),V(ring,Z,q,wide),V(ring,Z-1,h,wide),V(ring,h,wide),
            pltpu.SemaphoreType.DMA((n,)),pltpu.SemaphoreType.DMA((n,5+Z)),pltpu.SemaphoreType.DMA((n,5+Z)),pltpu.SemaphoreType.DMA((n,2)),pltpu.SemaphoreType.REGULAR((4+Z,))]
        if common:
            self.out_shapes.append(jax.ShapeDtypeStruct((Z,2,common[2],wide),BF))
            self.scratch+=[V(Z,2,common[2],wide),pltpu.SemaphoreType.DMA((Z,)),pltpu.SemaphoreType.DMA((Z,)),pltpu.SemaphoreType.DMA((1,))]
            self.begin_common=common[0]+self.wait+self.lag[-1]+1
            self.ticks=max(self.ticks,self.begin_common+Z+1)
        self.out_specs=[pl.BlockSpec(memory_space=pl.ANY)]*len(self.out_shapes)
    def bind(self,ins,outs,scr):
        self.out=outs[:self.finals]; self.made=outs[self.finals]
        if self.common: self.all,self.cs,self.ct,self.co=scr[-4:]; self.all_out=outs[-1]; scr=scr[:-4]
        self.o,self.own,self.cr,self.xr,self.yr,self.zr,self.fr,self.os,self.ss,self.rs,self.ls,self.free=scr
        self.p=Place(self.S); return self
    def slot(self,i): return i if self.slots==self.n else lax.rem(i,self.slots)
    def land(self,i): return i if self.ring==self.n else lax.rem(i,self.ring)
    def remote(self,i,k,src,dst,dev):
        return pltpu.make_async_remote_copy(src,dst,self.ss.at[i,k],self.rs.at[i,k],device_id=dev,device_id_type=MESH)
    def column(self,yy): return 1-self.p.y if yy else self.p.y
    def first(self,i,yy):
        return self.remote(i,yy,self.made.at[i,:,self.column(yy),1-self.p.c],self.cr.at[self.land(i),:,self.column(yy)],self.p.twin)
    def load(self,i,yy):
        return pltpu.make_async_copy(self.made.at[i,:,self.column(yy),self.p.c],self.own.at[self.slot(i),:,self.column(yy)],self.ls.at[i,yy])
    def part(self,i,col,x): return self.own.at[self.slot(i),:,col,pl.ds(al(x*self.q,self.q),self.q)]
    def cross(self,i): return self.remote(i,2,self.part(i,1-self.p.y,1-self.p.x),self.xr.at[self.land(i)],self.p.over_x)
    def side(self,i): return self.remote(i,3,self.part(i,1-self.p.y,self.p.x),self.yr.at[self.land(i)],self.p.over_y)
    def hop(self,i,s): return self.remote(i,3+s,self.own.at[self.slot(i),self.p.zat(-s),self.p.y],self.zr.at[self.land(i),s-1],self.p.next)
    def swap(self,i): return self.remote(i,3+self.Z,self.own.at[self.slot(i),self.p.z,self.p.y],self.fr.at[self.land(i)],self.p.over_x)
    def half(self,i): return self.o.at[i,pl.ds(al(self.p.c*self.h,self.h),self.h)]
    def share(self,i): return self.remote(i,4+self.Z,self.half(i),self.half(i),self.p.twin)
    def save(self,i,place,unit):
        index,layer,across=place; rows,wide=SUB
        ref=self.out[index] if layer is None else self.out[index].at[layer]
        return pltpu.make_async_copy(self.o.at[i],ref.at[pl.ds(al(unit//across*rows,rows),rows),pl.ds(al(lax.rem(unit,across)*wide,wide),wide)],self.os.at[i])
    def ask(self,i,k):
        if self.ring<self.n:
            @pl.when(i>=self.ring)
            def _(): pl.semaphore_wait(self.free.at[k],1)
    def tell(self,i,k,dev):
        if self.ring<self.n:
            @pl.when(i<self.n-self.ring)
            def _(): pl.semaphore_signal(self.free.at[k],inc=1,device_id=dev,device_id_type=MESH)
    def begin(self): self.p.greet()
    def phase(self,k,i):
        p=self.p; Z=self.Z; here=self.slot(i); land=self.land(i)
        if k==0:
            self.ask(i,0)
            for yy in (1,0): self.first(i,yy).start(); self.load(i,yy).start()
        elif k==1:
            for yy in (1,0):
                col=self.column(yy)
                self.load(i,yy).wait(); self.first(i,yy).wait_recv()
                self.own[here,:,col]=self.own[here,:,col]+self.cr[land,:,col]
                if yy: self.ask(i,1); self.cross(i).start()
            self.tell(i,0,p.twin)
        elif k==2:
            self.cross(i).wait_recv()
            ref=self.part(i,1-p.y,p.x); ref[...]=ref[...]+self.xr[land]
            self.tell(i,1,p.over_x)
            self.ask(i,2); self.side(i).start()
        elif k==3:
            self.side(i).wait_recv()
            ref=self.part(i,p.y,p.x); ref[...]=ref[...]+self.yr[land]
            self.tell(i,2,p.over_y)
            self.ask(i,3); self.hop(i,1).start()
        elif k<3+Z:
            s=k-3
            self.hop(i,s).wait_recv()
            ref=self.own.at[here,p.zat(-1-s),p.y]; ref[...]=ref[...]+self.zr[land,s-1]
            self.tell(i,2+s,p.prev)
            self.ask(i,3+s)
            (self.hop(i,s+1) if s+1<Z else self.swap(i)).start()
        elif k==3+Z:
            self.swap(i).wait_recv()
            ref=self.half(i); ref[...]=self.own[here,p.z,p.y]+self.fr[land]
            self.tell(i,2+Z,p.over_x)
            self.share(i).start()
        elif k==4+Z:
            for yy in (0,1): self.first(i,yy).wait_send()
            self.cross(i).wait_send(); self.side(i).wait_send()
            for s in range(1,Z): self.hop(i,s).wait_send()
            self.swap(i).wait_send(); self.share(i).wait()
            for at,count,place in zip(self.at,self.counts,self.places):
                @pl.when((i>=at)&(i<at+count))
                def _(at=at,place=place): self.save(i,place,i-at).start()
        else: self.save(i,self.places[0],0).wait()
    def relay(self,s):
        p=self.p
        ref=self.all.at[p.z,p.y] if s==0 else self.all.at[p.zat(1-s)]
        return pltpu.make_async_remote_copy(ref,ref,self.cs.at[s],self.ct.at[s],device_id=p.over_y if s==0 else p.next,device_id_type=MESH)
    def spread_common(self,k):
        p=self.p; unit,at,count=self.common
        if k==0: self.all[p.z,p.y]=self.o[unit,at:at+count]
        else: self.relay(k-1).wait()
        if k<self.Z: self.relay(k).start()
        else:
            cp=pltpu.make_async_copy(self.all,self.all_out,self.co.at[0]); cp.start(); cp.wait()
    def run(self,lo,count):
        def tick(u):
            for k in reversed(range(len(self.lag))):
                v=u-self.lag[k]; turn=self.gate+self.wait
                @pl.when((v>=0)&(v<self.n+self.wait)&((v<self.gate)|(v>=turn)))
                def _(k=k,v=v): self.phase(k,v-self.wait*(v//turn) if self.wait else v)
            if self.common:
                for k in range(self.Z+1):
                    @pl.when(u==self.begin_common+k)
                    def _(k=k): self.spread_common(k)
        during(0,count,lambda v:tick(lo+v))
    def spread(self,step,steps):
        per=-(-self.ticks//steps)
        self.run(step*per,per)

class Gather:
    def __init__(self,S,shards,cuts,modes,lag=2,ahead=1):
        self.S=S; Z=self.Z=S//2
        pick=lambda a: a if isinstance(a,tuple) else (a,None)
        self.local=[isinstance(a,tuple) and isinstance(a[0],int) for a in shards]
        pairs=[pick(a) for a,m in zip(shards,self.local) if not m]
        held=[]; self.source=[]
        for a,layer in pairs:
            k=next((k for k,v in enumerate(held) if v is a),None)
            if k is None: k=len(held); held.append(a)
            self.source.append((k,layer))
        fold_=lambda s: s[:-2]+(2,2,s[-2]//4,s[-1])
        self.inputs=[a.reshape(fold_(a.shape)) for a in held]
        self.shapes=[a if m else pick(a)[0].shape[-2:] for a,m in zip(shards,self.local)]
        self.cuts=cuts
        self.units=[(w,a) for w,k in enumerate(cuts) for a in range(k)]
        self.modes=''.join(modes)
        n=len(self.units); k=3*Z+1
        self.out_shapes=[jax.ShapeDtypeStruct((Z,2)+fold_(a),BF) for a in self.shapes]
        self.out_specs=[pl.BlockSpec(memory_space=pl.ANY)]*len(shards)
        self.scratch=[pltpu.VMEM(fold_(a),BF) for a,m in zip(self.shapes,self.local) if m]+[pltpu.SemaphoreType.DMA((n,k)),pltpu.SemaphoreType.DMA((n,k)),pltpu.SemaphoreType.DMA((n,))]
        self.plan={}
        for t in range(1,Z): self.plan[lag*t]=('z',t)
        self.plan[lag*Z]=('y',0); self.plan[lag*(Z+1)]=('x',0); self.plan[lag*(Z+2)]=('end',0)
        self.last=lag*(Z+2)
        self.ahead=ahead
        self.ticks=n+self.last
    def bind(self,ins,outs,scr):
        mine=list(scr[:-3]); source=list(self.source); self.i=[]
        for m in self.local:
            if m: self.i.append(mine.pop(0))
            else:
                k,layer=source.pop(0)
                self.i.append(ins[k] if layer is None else ins[k].at[layer])
        self.o=outs; self.ss,self.rs,self.ls=scr[-3:]; self.p=Place(self.S); return self
    def cp(self,u,kind,t=0):
        p=self.p; Z=self.Z; h=self.modes[u]=='h'; w,a=self.units[u]
        wide=self.shapes[w][1]//self.cuts[w]; cs=pl.ds(a*wide,wide); o=self.o[w]; i=self.i[w]
        k={'z':t-1,'y':Z-1+t,'u':2*Z-1+t-1,'x':3*Z-2,'a':3*Z-1,'b':3*Z}[kind]
        if kind=='z':
            zo=p.zat(1-t); dev=p.next
            dst=o.at[zo,p.y,p.c,:,:,cs] if h else o.at[zo,p.y,p.c,p.x,:,cs]; src=dst
            if t==1: src=i.at[p.c,:,:,cs] if h else i.at[p.c,p.x,:,cs]
        elif kind=='y':
            dst=src=o.at[p.zat(-t),p.y,p.c,p.x,:,cs]; dev=p.over_y
            if t==0: src=i.at[p.c,p.x,:,cs]
        elif kind=='u': src=dst=o.at[p.zat(-t),p.y,p.c,p.x,:,cs]; dev=p.over_x
        elif kind=='x': src=dst=o.at[:,1-p.y,p.c,p.x,:,cs]; dev=p.over_x
        else: src=dst=o.at[:,p.y if kind=='a' else 1-p.y,p.c,:,:,cs]; dev=p.twin
        return pltpu.make_async_remote_copy(src,dst,self.ss.at[u,k],self.rs.at[u,k],device_id=dev,device_id_type=MESH)
    def own(self,u):
        p=self.p; w,a=self.units[u]; wide=self.shapes[w][1]//self.cuts[w]; cs=pl.ds(a*wide,wide)
        return pltpu.make_async_copy(self.i[w].at[p.c,:,:,cs],self.o[w].at[p.z,p.y,p.c,:,:,cs],self.ls.at[u])
    def open(self,u):
        self.cp(u,'z',1).start(); self.cp(u,'y',0).start(); self.own(u).start()
    def begin(self):
        self.p.greet()
        for u in range(min(self.ahead,len(self.units))): self.open(u)
    def stage(self,u,kind,t):
        Z=self.Z; q=self.modes[u]=='q'
        if kind=='z':
            self.cp(u,'z',t).wait_recv()
            if t+1<Z: self.cp(u,'z',t+1).start()
            self.cp(u,'y',t).start()
            if q: self.cp(u,'u',t).start()
        elif kind=='y':
            for t in range(Z): self.cp(u,'y',t).wait_recv()
            self.cp(u,'x').start()
            self.own(u).wait()
            if not q: self.cp(u,'a').start()
        elif kind=='x':
            if q:
                for t in range(1,Z): self.cp(u,'u',t).wait_recv()
                self.cp(u,'a').start()
            self.cp(u,'x').wait_recv(); self.cp(u,'b').start()
        else:
            for t in range(1,Z):
                self.cp(u,'z',t).wait_send()
                if q: self.cp(u,'u',t).wait_send()
            for t in range(Z): self.cp(u,'y',t).wait_send()
            self.cp(u,'x').wait_send(); self.cp(u,'a').wait(); self.cp(u,'b').wait()
    def run(self,lo,count):
        n=len(self.units)
        for i in range(lo,min(lo+count,self.ticks)):
            if self.ahead<=i+self.ahead<n: self.open(i+self.ahead)
            for u in range(n):
                s=self.plan.get(i-u)
                if s: self.stage(u,*s)
    def done(self,w):
        return max(u for u,(a,_) in enumerate(self.units) if a==w)+self.last+1

VM=60<<20
def call(body,name,grid,ins,in_specs,outs,out_specs,scratch,side=None,cid=None):
    any_=pl.BlockSpec(memory_space=pl.ANY)
    extra=side.inputs if side else []
    a,b,c,d,e=len(ins),len(extra),len(outs),len(side.out_shapes) if side else 0,len(scratch)
    def kernel(*refs):
        comm=None
        cut=np.cumsum([0,a,b,c,d,e]).tolist()
        part=[refs[x:y] for x,y in zip(cut,cut[1:]+[len(refs)])]
        if side:
            comm=side.bind(part[1],part[3],part[5])
        body(comm,*part[0],*part[2],*part[4])
    out=pl.pallas_call(kernel,grid=grid,out_shape=list(outs)+(side.out_shapes if side else []),in_specs=list(in_specs)+[any_]*b,
        out_specs=list(out_specs)+(side.out_specs if side else []),scratch_shapes=list(scratch)+(side.scratch if side else []),
        compiler_params=pltpu.CompilerParams(vmem_limit_bytes=VM,**(dict(collective_id=cid,has_side_effects=True) if side else {})),name=name)(*ins,*extra)
    return out[:c],out[c:]


CH=64

def aside(body):
    def run(comm,*refs):
        if comm:
            @pl.when(pl.program_id(0)==0)
            def _(): comm.begin()
        body(*refs)
        if comm: comm.spread(pl.program_id(0),pl.num_programs(0))
    return run
def whole(shape):
    return pl.BlockSpec(shape,lambda *i:(0,)*len(shape),pipeline_mode=pl.Buffered(1))
def chunks(steps,body):
    def run(i,c):
        body(pl.ds(pl.multiple_of(i*CH,CH),CH)); return c
    lax.fori_loop(0,steps//CH,run,0)
def stats(v):
    center=v-jnp.mean(v,axis=-1,keepdims=True)
    rstd=lax.rsqrt(jnp.mean(center*center,axis=-1,keepdims=True)+1e-5)
    return center*rstd,rstd
def norm_back(dy,gain,xhat,rstd):
    g=dy*gain
    return rstd*(g-jnp.mean(g,axis=-1,keepdims=True)-xhat*jnp.mean(g*xhat,axis=-1,keepdims=True))
def sigmoid(v): return 0.5*jnp.tanh(0.5*v)+0.5
def fold(v): return jnp.sum(v.reshape(v.shape[0]//8,8,v.shape[1]),axis=0)

PAD=32
RC=128
def over_columns(width,body):
    def run(i,c):
        body(pl.ds(pl.multiple_of(i*128,128),128)); return c
    lax.fori_loop(0,width//128,run,0)
def taps_of(taps,lead,residue):
    return [(a,k) for k in range(taps) for a in [lead(k)//8] if lead(k)%8==residue]
def slide(pad_ref,w_ref,lead,taps,t0,cols):
    acc=jnp.zeros((RC,128),F32)
    for b in range(8):
        use=taps_of(taps,lead,b)
        if not use: continue
        top=max(a for a,_ in use)
        slab=pad_ref[t0+b:t0+b+RC+8*top,cols]
        for a,k in use: acc=acc+w_ref[k:k+1,cols]*slab[8*a:8*a+RC]
    return acc

VECTOR_ROWS=64
def plan_ticks(comm,phases,pace,limit):
    at=[]; done=0; spent=0.0
    for st,t in enumerate(phases):
        spent+=t
        target=max(done,min(int(spent/pace),limit(st),comm.ticks))
        at.append((done,target-done)); done=target
    return at

def backward_kernel(taps,size,comm,q_ref,k_ref,v_ref,p_ref,table_ref,pick_ref,vec_ref,valid_ref,tok_ref,s5_ref,
        dx4,x3,x2,x1,hid4,hid1,hid0,chid,cact,mixed,up,depth,act1,act0,dsl1,dsl0,fi1,fo1,ai,ao,pi,po,fi0,fo0,out_ref,
        d_ref,x_ref,acc_ref,low_ref,turn_ref,hid_ref,big_ref,stage_ref,ds_ref,grad_ref,wa_ref,wb_ref,wd_ref,pad_ref,tail_ref,rows_ref,sums_ref,ddw_ref,dbin_ref,psum_ref,dtab_ref,
        sem_d,sem_x,sem_hid,sem_big,sem_a,sem_b,sem_c,stage_sem):
    steps,width=d_ref.shape; wide=SUB[1]; S=comm.S; across=width//wide; CUT=act1.shape[1]//S
    F=act1.shape[1]//wide; A=width//128; B=ai.shape[1]//wide; M0,M1,M2=po.shape[1]//wide,pi.shape[1]//wide,ao.shape[1]//wide
    cut=np.cumsum([0,F,F,M0,1,M1,M2,A,B,F,F,1]).tolist()
    FB,FD,MP,MC,MI,MO,AT,PB,CB,CD,EN=cut[:11]
    units=np.cumsum([0,F,F,M0,M1,M2,B,F,1,F]).tolist()
    j=pl.program_id(0)
    made=[]; n=0
    for st in range(cut[-1]):
        n+=0 if MC<=st<MI or AT<=st<PB or st==EN else 1
        if st==CD: n+=1
        made.append(n)
    def limit(st):
        if AT<=st<PB: return comm.gate+comm.wait
        return made[st]-2+(comm.wait if st>=PB else 0)
    times=[2.9]*F+[1.0]*F+[3]*M0+[15]+[2.5]*(M1-1)+[5]+[3]*M2+[4.7]*A+[2.8]*B+[3.8]*F+[1.0]*F+[0]
    at=plan_ticks(comm,times,PACE,limit)
    def ticks(step,share=(0,1)):
        lo,n=at[step]; a,b=n*share[0]//share[1],n*(share[0]+1)//share[1]
        if b>a: comm.run(lo+a,b-a)
    def ticks_of(lo,hi):
        for st in range(lo,hi):
            if at[st][1]:
                @pl.when(j==st)
                def _(st=st): ticks(st)
    def phase(lo,hi):
        return pl.when((j>=lo)&(j<hi))
    def last(step): return pl.when(j==step)
    def fill(src,dst,sem): return pltpu.make_async_copy(src,dst,sem)
    def row(i): return vec_ref[i:i+1,:]
    def here(i): return pl.ds(al(i*wide,wide),wide)
    def column(w,i,slot): return fill(w.at[:,here(i)],wa_ref.at[slot],sem_a.at[slot])
    def band(w,i): return fill(w.at[here(i)],wb_ref.at[lax.rem(i,2)],sem_b.at[lax.rem(i,2)])
    def slope(w,i): return fill(w.at[:,here(i)],wd_ref.at[lax.rem(i,2)],sem_c.at[lax.rem(i,2)])
    def load(ref,dst,sem): return fill(ref,dst,sem.at[0])
    def lefts(act,a,slot):
        return [fill(act.at[:,pl.ds(al(s*CUT+a*SUB[0],SUB[0]),SUB[0])],big_ref.at[slot,:,pl.ds(s*SUB[0],SUB[0])],sem_big.at[slot,s]) for s in range(S)]
    def whole_big(src,slot): return fill(src,big_ref.at[slot],sem_big.at[slot,0])
    def put(q): return fill(stage_ref.at[lax.rem(q,2)],comm.made.at[q],stage_sem.at[lax.rem(q,2)])
    first_late=units[5]
    def unit(q,value):
        @pl.when((q>=2)&((q<first_late)|(q>=first_late+2)))
        def _(): put(q-2).wait()
        stage_ref[lax.rem(q,2)]=value.reshape(stage_ref.shape[1:])
        put(q).start()
    def stream(w,lo,n,tau0,use):
        @phase(lo,lo+n)
        def _():
            i=j-lo; slot=lax.rem(tau0+i,2)
            column(w,i,slot).wait()
            @pl.when(i+1<n)
            def _(): column(w,i+1,lax.rem(tau0+i+1,2)).start()
            use(i,wa_ref.at[slot])
    def ahead(w,tau): column(w,0,tau%2).start()
    tau=np.cumsum([0,F,M0,M1,M2,B]).tolist()

    def feed_step(i,w_out,slopes,q,side,fi):
        band(w_out,i).wait(); slope(slopes,i).wait()
        @pl.when(i+1<F)
        def _(): band(w_out,i+1).start(); slope(slopes,i+1).start()
        s=lax.rem(i,2)
        dpre=(nt(low_ref[:,:width],wb_ref[s])*wd_ref[s].astype(F32)).astype(BF)
        dbin_ref[side,:,here(i)]=fold(dpre.astype(F32))
        acc_ref[...]+=nt(dpre,fi[...])
        unit(q+i,nn(turn_ref[...],dpre).astype(BF))
    def norm_step(source,i,at_,after):
        def body(r):
            xhat,rstd=stats(source[r,:].astype(F32))
            dy=acc_ref[r,:]
            sums_ref[at_]+=fold(dy*xhat); sums_ref[at_+1]+=fold(dy)
            after(r,d_ref[r,:]+norm_back(dy,row(Rows.gain+i),xhat,rstd))
        chunks(steps,body)
    def out_units(act,lo,q):
        @phase(lo,lo+F)
        def _():
            d=j-lo; a=d//across
            for slot in range(3):
                @pl.when((lax.rem(a,3)==slot)&(lax.rem(d,across)==0))
                def _(slot=slot):
                    for cp in lefts(act,a,slot): cp.wait()
            unit(q+d,tn(big_ref[lax.rem(a,3)],low_ref[:,here(lax.rem(d,across))]).astype(BF))
            @pl.when(d==across-1)
            def _():
                for a in range(3,F//across):
                    for cp in lefts(act,a,a-3): cp.start()
    def start_feed(act,fo,slopes):
        for a in range(3):
            for cp in lefts(act,a,a): cp.start()
        band(fo,0).start(); slope(slopes,0).start()

    @last(0)
    def _():
        comm.begin()
        load(dx4,d_ref,sem_d).start(); load(hid4,hid_ref,sem_hid).start(); load(x3,x_ref,sem_x).start()
        ahead(fi1,0); start_feed(act1,fo1,dsl1)
        sums_ref[...]=jnp.zeros_like(sums_ref)
        dtab_ref[...]=jnp.zeros_like(dtab_ref)
        acc_ref[...]=jnp.zeros_like(acc_ref)
        tail_ref[steps:steps+PAD,:]=jnp.zeros((PAD,width),F32)
        pad_ref[0:PAD,:]=jnp.zeros((PAD,width),F32)
        load(dx4,d_ref,sem_d).wait()
        def body(r):
            df=(0.5*d_ref[r,:]).astype(BF)
            low_ref[r,:width]=df
            sums_ref[12]+=fold(df.astype(F32))
        chunks(steps,body)
        load(hid4,hid_ref,sem_hid).wait()
        turn_ref[...]=hid_ref[...].T
        load(chid,hid_ref,sem_hid).start()
    stream(fi1,FB,F,tau[0],lambda i,w: feed_step(i,fo1,dsl1,units[0],0,w))
    @last(FD-1)
    def _():
        load(x3,x_ref,sem_x).wait()
        def after(r,v): d_ref[r,:]=v
        norm_step(x_ref,4,8,after)
        load(depth,x_ref,sem_x).start()
        ahead(po,tau[1])
    out_units(act1,FD,units[1])
    @last(MP-1)
    def _():
        whole_big(up.at[:,:width],0).start(); whole_big(up.at[:,width:],1).start(); whole_big(cact,2).start()
        def body(r): low_ref[r,:width]=d_ref[r,:].astype(BF)
        chunks(steps,body)
        acc_ref[...]=jnp.zeros_like(acc_ref)
    def lower(i,w):
        @pl.when(i==0)
        def _(): whole_big(cact,2).wait()
        acc_ref[...]+=nt(low_ref[:,here(i)],w[...])
        unit(units[2]+i,tn(big_ref[2],low_ref[:,here(i)]).astype(BF))
        @pl.when(i==M0-1)
        def _(): ahead(pi,tau[2])
    stream(po,MP,M0,tau[1],lower)
    @last(MC)
    def _():
        weights=vec_ref.at[Rows.taps:Rows.taps+32]
        load(depth,x_ref,sem_x).wait(); whole_big(cact,0).wait(); whole_big(cact,1).wait()
        def three(i,c):
            r=pl.ds(pl.multiple_of(i*CH,CH),CH)
            xhat,rstd=stats(x_ref[r,:])
            gain=row(Rows.gain+3)
            z=xhat*gain+row(Rows.shift+3)
            sg=sigmoid(z)
            dz=acc_ref[r,:]*(sg*(1.0+z*(1.0-sg)))
            sums_ref[6]+=fold(dz*xhat); sums_ref[7]+=fold(dz)
            tail_ref[r,:]=norm_back(dz,gain,xhat,rstd)
            pad_ref[pl.ds(pl.multiple_of(i*CH+PAD,PAD),CH),:]=big_ref[0,r,:].astype(F32)*sigmoid(big_ref[1,r,:].astype(F32))*valid_ref[r,0:1]
            return c
        lax.fori_loop(0,steps//CH,three,0)
        load(x2,x_ref,sem_x).start()
        ticks(MC,(0,3))
        def conv(cols):
            for t0 in range(0,steps,RC):
                acc_ref[t0:t0+RC,cols]=slide(tail_ref,weights,lambda k:taps-1-k,taps,t0,cols)
        over_columns(width,conv)
        ticks(MC,(1,3))
        def gate(r):
            a=big_ref[0,r,:].astype(F32); sg=sigmoid(big_ref[1,r,:].astype(F32))
            dg=acc_ref[r,:]*valid_ref[r,0:1]*sg
            low_ref[r,:width]=dg.astype(BF)
            low_ref[r,width:]=(dg*a*(1.0-sg)).astype(BF)
        chunks(steps,gate)
        acc_ref[...]=jnp.zeros_like(acc_ref)
        ticks(MC,(2,3))
    def raised(i,w):
        @pl.when(i==0)
        def _(): load(chid,hid_ref,sem_hid).wait()
        acc_ref[...]+=nt(low_ref[:,here(i)],w[...])
        unit(units[3]+i,tn(hid_ref[...],low_ref[:,here(i)]).astype(BF))
        @pl.when(i==M1-1)
        def _():
            load(mixed,hid_ref,sem_hid).start()
            ahead(ao,tau[3])
            load(x2,x_ref,sem_x).wait()
            def after(r,v):
                d_ref[r,:]=v
                da=v.astype(BF)
                low_ref[r,:width]=da
                sums_ref[13]+=fold(da.astype(F32))
            norm_step(x_ref,2,4,after)
            load(x1,x_ref,sem_x).start()
            acc_ref[...]=jnp.zeros_like(acc_ref)
    stream(pi,MI,M1,tau[2],raised)
    def joined(i,w):
        @pl.when(i==0)
        def _(): load(mixed,hid_ref,sem_hid).wait()
        acc_ref[...]+=nt(low_ref[:,here(i)],w[...])
        unit(units[4]+i,tn(hid_ref[...],low_ref[:,here(i)]).astype(BF))
        @pl.when(i==M2-1)
        def _():
            load(hid1,hid_ref,sem_hid).start()
            ahead(ai,tau[4])
            low_ref[:,width:]=acc_ref[...].astype(BF)
            acc_ref[...]=jnp.zeros_like(acc_ref)
    stream(ao,MO,M2,tau[3],joined)
    ticks_of(FB,MC); ticks_of(MI,AT)
    @last(AT)
    def _():
        for q in (first_late-2,first_late-1): put(q).wait()
    lo_at=at[AT][0]
    @phase(AT,PB)
    def _():
        h=j-AT
        mine=pl.ds(al(h*128,128),128)
        grad_ref[...]=low_ref[:,pl.ds(al(width+h*128,128),128)]
        parts=heads_back(q_ref,k_ref,v_ref,p_ref,grad_ref,table_ref,pick_ref,dtab_ref,ds_ref,size)
        for part in range(3): big_ref[part,:,mine]=parts[part]
        psum_ref[0:1,mine]=jnp.sum(big_ref[0,:,mine].astype(F32),axis=0,keepdims=True)
        psum_ref[1:2,mine]=jnp.sum(big_ref[2,:,mine].astype(F32),axis=0,keepdims=True)
        comm.run(lo_at+h*ATICKS,ATICKS)
    start=lo_at+ATICKS*A
    assert start<=comm.gate+comm.wait
    late=plan_ticks(comm,times[PB:],PACE2,lambda st: limit(PB+st)-start)
    for st in range(PB,EN): at[st]=(start+late[st-PB][0],late[st-PB][1])
    def packed_back(b,w):
        @pl.when(b==0)
        def _():
            load(hid1,hid_ref,sem_hid).wait()
            turn_ref[...]=hid_ref[...].T
            load(hid0,hid_ref,sem_hid).start()
        g=big_ref[b//across,:,here(lax.rem(b,across))]
        acc_ref[...]+=nt(g,w[...])
        unit(units[5]+b,nn(turn_ref[...],g).astype(BF))
        @pl.when(b==B-1)
        def _():
            ahead(fi0,tau[5]); start_feed(act0,fo0,dsl0)
            load(x1,x_ref,sem_x).wait(); load(hid0,hid_ref,sem_hid).wait()
            turn_ref[...]=hid_ref[...].T
            def after(r,v):
                d_ref[r,:]=v
                df=(0.5*v).astype(BF)
                low_ref[r,:width]=df
                sums_ref[11]+=fold(df.astype(F32))
            norm_step(x_ref,1,2,after)
            acc_ref[...]=jnp.zeros_like(acc_ref)
    stream(ai,PB,B,tau[4],packed_back)
    stream(fi0,CB,F,tau[5],lambda i,w: feed_step(i,fo0,dsl0,units[6],1,w))
    @phase(CB,CD)
    def _():
        def conv_weights(cols):
            lead=lambda k:k+PAD-taps+1
            for b in range(8):
                use=taps_of(taps,lead,b)
                if not use: continue
                top=max(a for a,_ in use)
                parts={k:jnp.zeros((8,128),F32) for _,k in use}
                for t0 in range(0,steps,RC):
                    slab=pad_ref[t0+b:t0+b+RC+8*top,cols]
                    dd=tail_ref[t0:t0+RC,cols]
                    for a,k in use: parts[k]=parts[k]+fold(slab[8*a:8*a+RC]*dd)
                for k,v in parts.items(): ddw_ref[k:k+1,cols]=jnp.sum(v,axis=0,keepdims=True)
        for a in range(A//F): conv_weights(pl.ds(al((j-CB)*(A//F)*128+a*128,128),128))
    @last(CD-1)
    def _():
        def after(r,v): out_ref[r,:]=v.astype(BF)
        norm_step(tok_ref,0,0,after)
        rows_ref[...]=jnp.zeros_like(rows_ref)
        total=lambda v: jnp.sum(v,axis=0,keepdims=True)
        rows=[sums_ref[0],sums_ref[2],sums_ref[4],sums_ref[6],sums_ref[8],s5_ref[0],sums_ref[1],sums_ref[3],sums_ref[5],sums_ref[7],sums_ref[9],s5_ref[1],sums_ref[11],sums_ref[12]]
        rows=[total(v) for v in rows]+[psum_ref[0:1,:],psum_ref[1:2,:],total(sums_ref[13])]
        L=width//S
        for i,v in enumerate(rows):
            for s in range(S): rows_ref[s,i:i+1,0:L]=v[:,s*L:s*L+L]
        k=len(rows)
        for i in range(2):
            v=total(dbin_ref[1-i])
            for s in range(S): rows_ref[s,k+i:k+i+1,:]=v[:,s*wide:s*wide+wide]
        n=dtab_ref.shape[0]//S
        for s in range(S):
            rows_ref[s,32:32+taps,0:L]=ddw_ref[0:taps,s*L:s*L+L]
            rows_ref[s,VECTOR_ROWS:VECTOR_ROWS+n,0:size]=dtab_ref[s*n:s*n+n,:]
    @last(CD)
    def _(): unit(units[7],rows_ref[...].astype(BF).reshape(S*SUB[0],wide))
    out_units(act0,CD,units[8])
    ticks_of(PB,EN)
    @last(EN)
    def _():
        for q in (units[9]-2,units[9]-1): put(q).wait()
        lo=sum(at[EN-1])
        comm.run(lo,comm.ticks-lo)

def heads_back(q_ref,k_ref,v_ref,p_ref,g_ref,table_ref,pick_ref,dtab_ref,ds_ref,size):
    steps=q_ref.shape[0]; nb=steps//QB; span=steps+QB
    scale=1.0/math.sqrt(size)
    flip=(lax.broadcasted_iota(jnp.int32,(QB,QB),0)+lax.broadcasted_iota(jnp.int32,(QB,QB),1)==QB-1).astype(F32).astype(BF)
    sl=[slice(i*QB,(i+1)*QB) for i in range(nb)]
    out=[]
    for hh in range(q_ref.shape[1]//size):
        cols=slice(hh*size,(hh+1)*size)
        dss=[]
        for r in sl:
            p=p_ref[hh,r,:].astype(F32)
            t=p*nt(g_ref[r,cols],v_ref[:,cols])
            dss.append((t-p*jnp.sum(t,axis=1,keepdims=True)).astype(BF))
        for r,ds in zip(sl,dss): ds_ref[r,:]=ds
        xs=[nn(flip,ds) for ds in dss]
        xs=[pltpu.roll(jnp.concatenate([x,jnp.zeros((QB,QB),F32)],axis=1),span-QB+1,1,stride=1,stride_axis=0).astype(BF) for x in xs]
        xs=[(nt(x,pick_ref[i])*scale).astype(BF) for i,x in enumerate(xs)]
        drel=jnp.concatenate([nn(flip,x).astype(BF) for x in xs],axis=0)
        dq=(nn(ds_ref[...],k_ref[:,cols])*scale+nn(drel,table_ref[...])).astype(BF)
        dtab_ref[...]+=tn(drel,q_ref[:,cols])
        out.append((dq,(tn(ds_ref[...],q_ref[:,cols])*scale).astype(BF),tn(p_ref[hh],g_ref[:,cols]).astype(BF)))
    return [jnp.concatenate([a[part] for a in out],axis=1) for part in range(3)]

PACE=4.3; PAUSE=1; PACE2=2.0; ATICKS=1
def backward(S,packed,p,table,pick,heads,vec,valid,tokens,s5,rest,taps,out_shapes,cid):
    steps,width=tokens.shape; size=width//heads; wide=SUB[1]; across=width//wide
    act1,ai,ao,pi,po=rest[12],rest[18],rest[19],rest[20],rest[21]
    hidden=act1.shape[1]; F=hidden//wide; A=width//128; B=ai.shape[1]//wide; M0,M1,M2=[a.shape[1]//wide for a in (po,pi,ao)]
    assert hidden//S==wide and width//S==SUB[0] and wide//SUB[0]<=4 and A%F==0
    counts=[F,F,M0,M1,M2,B,F,1,F]
    places=[(0,1,F),(1,1,across),(5,None,across),(4,None,2*across),(3,None,across),(2,None,3*across),(0,0,F),(6,None,1),(1,0,across)]
    comm=Scatter(S,counts,places,out_shapes,common=(sum(counts[:7]),VECTOR_ROWS,table.shape[0]//S),pause=(sum(counts[:5]),PAUSE))
    start=2*F+M0+1+M1+M2
    head=lambda o:pl.BlockSpec((steps,128),lambda j:(0,o*A+jnp.minimum(jnp.maximum(j-start,0),A-1)))
    ins=[packed,packed,packed,p,table,pick,vec,valid,tokens,s5]
    specs=[head(0),head(1),head(2),pl.BlockSpec((128//size,steps,steps),lambda j:(jnp.minimum(jnp.maximum(j-start,0),A-1),0,0))]+[whole(a.shape) for a in ins[4:]]
    specs+=[pl.BlockSpec(memory_space=pl.ANY)]*len(rest)
    V=pltpu.VMEM; Z=S//2; sem=lambda *n: pltpu.SemaphoreType.DMA(n)
    sq=lambda t: V((steps,width),t)
    scratch=[sq(F32),sq(F32),sq(F32),V((steps,2*width),BF),V((width,steps),BF),sq(BF),V((3,steps,width),BF),V((2,Z,2,2,SUB[0]//2,wide),BF),V((steps,steps),BF),V((steps,128),BF),
        V((2,width,wide),BF),V((2,wide,width),BF),V((2,steps,wide),BF),V((steps+PAD,width),F32),V((steps+PAD,width),F32),V((S,)+SUB,F32),V((14,8,width),F32),V((32,width),F32),V((2,8,hidden),F32),V((8,width),F32),V((128,size),F32),
        sem(1),sem(1),sem(1),sem(3,S),sem(2),sem(2),sem(2),sem(2)]
    return call(functools.partial(backward_kernel,taps,size),'backward_and_sums',(start+A+B+2*F+1,),ins+list(rest),specs,[jax.ShapeDtypeStruct((steps,width),BF)],[whole((steps,width))],scratch,comm,cid)

class Rows:
    gain=0; shift=8; inner=16; outer=24; packed=26; mixed=28; taps=32; count=64

def early_kernel(heads,taps,comm,gain_in,shift_in,inner_in,outer_in,packed_in,mixed_in,taps_in,tok_ref,cot_ref,valid_ref,mask_ref,table_ref,pick_ref,
        hid0_ref,act0_ref,dsl0_ref,x1_ref,hid1_ref,packed_ref,mixed_ref,p_ref,x2_ref,chid_ref,up_ref,depth_ref,cact_ref,x3_ref,hid4_ref,act1_ref,dsl1_ref,dx4_ref,res_ref,s5_ref,vec_ref,
        own_ref,land_ref,land_sem,acc_ref,wa_ref,wb_ref,sem_a,sem_b,rel_ref,qkv_ref,pad_ref,wide_ref):
    steps,width=tok_ref.shape; tile=wa_ref.shape[-1]; S=comm.S
    small,fi0,fo0,ai,ao,pi,po,fi1,fo1=comm.o
    F,B,M0,M1,M2=[w.shape[-1]//tile for w in (fi0,ai,ao,pi,po)]; A=width//128
    size=width//heads
    cut=np.cumsum([0,F,B,A,M0,M1,M2,F]).tolist()
    j=pl.program_id(0)
    L=width//S
    def row(i): return vec_ref[i:i+1,:]
    def column(w,i,slot): return pltpu.make_async_copy(w.at[:,:,:,:,:,pl.ds(al(i*tile,tile),tile)],wa_ref.at[slot],sem_a.at[slot])
    def band(w,i,slot): return pltpu.make_async_copy(w.at[i//2,lax.rem(i,2)],wb_ref.at[slot],sem_b.at[slot])
    def wa(slot): return wa_ref[slot].reshape(width,tile)
    want=[comm.done(2),comm.done(3),comm.done(4),comm.done(5),comm.done(6),comm.done(8)]
    at={}; done=want[0]
    times=[20/F]*F+[10/B]*B+[26/A]*A+[3]*M0+[2]*(M1-1)+[14]+[3]*M2
    need={cut[1]-1:want[1],cut[3]-1:want[2],cut[4]-1:want[3],cut[5]-1:want[4],cut[6]-1:comm.ticks-1}
    for st in range(cut[6]):
        target=want[0]+int((comm.ticks-1-want[0])*sum(times[:st+1])/sum(times))
        target=max(target,need.get(st,0))
        if target>done: at[st]=(done,target-done); done=target
    def ticks():
        for st,(lo,n) in at.items():
            @pl.when(j==st)
            def _(lo=lo,n=n): comm.run(lo,n)
    @pl.when(j==0)
    def _():
        own_ref[...]=jnp.zeros_like(own_ref)
        for at_,ref in ((Rows.gain,gain_in),(Rows.shift,shift_in),(Rows.outer,outer_in),(Rows.packed,packed_in),(Rows.mixed,mixed_in),(Rows.taps,taps_in)):
            own_ref[at_:at_+ref.shape[0],:]=ref[...].astype(F32)
        k=inner_in.shape[1]//L
        for l in range(2):
            for i in range(k): own_ref[Rows.inner+l*k+i:Rows.inner+l*k+i+1,:]=inner_in[l:l+1,i*L:i*L+L].astype(F32)
        comm.i[0][...]=own_ref[...].astype(BF).reshape(comm.i[0].shape)
        comm.begin()
        comm.run(0,want[0])
        cp=pltpu.make_async_copy(small,land_ref,land_sem.at[0]); cp.start()
        column(fi0,0,0).start(); band(fo0,0,0).start()
        cp.wait()
        for s in range(S): vec_ref[:,s*L:s*L+L]=land_ref[s//2,s%2].reshape(Rows.count,L).astype(F32)
        for i in range(steps//QB): rel_ref[i]=tn(table_ref[...],pick_ref[i]).astype(BF)
        def body(r):
            xhat,_r=stats(tok_ref[r,:].astype(F32))
            hid0_ref[r,:]=(xhat*row(Rows.gain)+row(Rows.shift)).astype(BF)
        chunks(steps,body)
        acc_ref[...]=jnp.zeros_like(acc_ref)
        pad_ref[0:PAD,:]=jnp.zeros((PAD,width),F32)
    def feed_tile(i,tau,l,hid_ref,act_ref,dsl_ref,fi,fo):
        slot=lax.rem(tau,2); k=tile//L
        column(fi,i,slot).wait(); band(fo,i,lax.rem(i,2)).wait()
        @pl.when(i+1<F)
        def _(): column(fi,i+1,lax.rem(tau+1,2)).start(); band(fo,i+1,lax.rem(i+1,2)).start()
        bias=jnp.concatenate([vec_ref[Rows.inner+l*k+a:Rows.inner+l*k+a+1,pl.ds(al(i*L,L),L)] for a in range(k)],axis=1)
        pre=nn(hid_ref[...],wa(slot))+bias
        sg=sigmoid(pre)
        act_ref[...]=(pre*sg).astype(BF)
        dsl_ref[...]=(sg*(1.0+pre*(1.0-sg))).astype(BF)
        acc_ref[...]+=nn(act_ref[...],wb_ref[lax.rem(i,2)].reshape(tile,width))
    @pl.when(j<cut[1])
    def _(): feed_tile(j,j,0,hid0_ref,act0_ref,dsl0_ref,fi0,fo0)
    @pl.when(j==cut[1]-1)
    def _():
        def body(r):
            x=tok_ref[r,:].astype(F32)+0.5*(acc_ref[r,:]+row(Rows.outer))
            x1_ref[r,:]=x
            xhat,_r=stats(x)
            hid1_ref[r,:]=(xhat*row(Rows.gain+1)+row(Rows.shift+1)).astype(BF)
        chunks(steps,body)
    def stream(w,lo,n,tau0,use):
        @pl.when((j>=lo)&(j<lo+n))
        def _():
            i=j-lo; slot=lax.rem(tau0+i,2)
            column(w,i,slot).wait()
            @pl.when(i+1<n)
            def _(): column(w,i+1,lax.rem(tau0+i+1,2)).start()
            use(i,slot)
    def after(step,w,tau):
        @pl.when(j==step)
        def _(): column(w,0,lax.rem(tau,2)).start()
    def here(i): return pl.ds(al(i*tile,tile),tile)
    def pack(i,slot):
        v=nn(hid1_ref[...],wa(slot))
        per=width//tile
        @pl.when(i<per)
        def _(): packed_ref[:,here(i)]=(v+vec_ref[Rows.packed:Rows.packed+1,here(lax.rem(i,per))]).astype(BF)
        @pl.when((i>=per)&(i<2*per))
        def _(): packed_ref[:,here(i)]=v.astype(BF)
        @pl.when(i>=2*per)
        def _(): packed_ref[:,here(i)]=(v+vec_ref[Rows.packed+1:Rows.packed+2,here(lax.rem(i,per))]).astype(BF)
    stream(ai,cut[1],B,F,pack)
    @pl.when((j>=cut[2])&(j<cut[3]))
    def _():
        h=j-cut[2]
        for a in range(3): qkv_ref[a]=packed_ref[:,pl.ds(al(a*width+h*128,128),128)]
        scale=1.0/math.sqrt(size)
        sl=[slice(i*QB,(i+1)*QB) for i in range(steps//QB)]; outs=[]
        for hh in range(128//size):
            cols=slice(hh*size,(hh+1)*size)
            rels=[nn(qkv_ref[0,r,cols],rel_ref[i]) for i,r in enumerate(sl)]
            rels=[pltpu.roll(x,0,1,stride=1,stride_axis=0)[:,:steps] for x in rels]
            ss=[(nt(qkv_ref[0,r,cols],qkv_ref[1,:,cols])+x)*scale+mask_ref[0:1,:] for r,x in zip(sl,rels)]
            es=[jnp.exp(s-jnp.max(s,axis=1,keepdims=True)) for s in ss]
            ps=[(e*(1.0/jnp.sum(e,axis=1,keepdims=True))).astype(BF) for e in es]
            for r,p in zip(sl,ps): p_ref[hh,r,:]=p
            outs.append(jnp.concatenate([nn(p,qkv_ref[2,:,cols]).astype(BF) for p in ps],axis=0))
        mixed_ref[:,pl.ds(al(h*128,128),128)]=jnp.concatenate(outs,axis=1)
    def join(i,slot):
        x2_ref[:,here(i)]=x1_ref[:,here(i)]+nn(mixed_ref[...],wa(slot))+vec_ref[Rows.mixed:Rows.mixed+1,here(i)]
        @pl.when(i==M0-1)
        def _():
            def body(r):
                xhat,_r=stats(x2_ref[r,:])
                chid_ref[r,:]=(xhat*row(Rows.gain+2)+row(Rows.shift+2)).astype(BF)
            chunks(steps,body)
    stream(ao,cut[3],M0,F+B,join)
    def raise_(i,slot):
        wide_ref[:,here(i)]=nn(chid_ref[...],wa(slot))
        @pl.when(i==M1-1)
        def _():
            def gate(k,c):
                r=pl.ds(pl.multiple_of(k*CH,CH),CH)
                a=wide_ref[r,:width]; b=wide_ref[r,width:]
                up_ref[r,:width]=a.astype(BF); up_ref[r,width:]=b.astype(BF)
                pad_ref[pl.ds(pl.multiple_of(k*CH+PAD,PAD),CH),:]=a*sigmoid(b)*valid_ref[r,0:1]
                return c
            lax.fori_loop(0,steps//CH,gate,0)
            weights=vec_ref.at[Rows.taps:Rows.taps+32]
            def conv(cols):
                for t0 in range(0,steps,RC):
                    depth_ref[t0:t0+RC,cols]=slide(pad_ref,weights,lambda k:k+PAD-taps+1,taps,t0,cols)
            over_columns(width,conv)
            def body(r):
                xhat,_r=stats(depth_ref[r,:])
                z=xhat*row(Rows.gain+3)+row(Rows.shift+3)
                cact_ref[r,:]=(z*sigmoid(z)).astype(BF)
            chunks(steps,body)
    stream(pi,cut[4],M1,F+B+M0,raise_)
    def lower(i,slot):
        x3_ref[:,here(i)]=x2_ref[:,here(i)]+nn(cact_ref[...],wa(slot))
        @pl.when(i==M2-1)
        def _():
            def body(r):
                xhat,_r=stats(x3_ref[r,:])
                hid4_ref[r,:]=(xhat*row(Rows.gain+4)+row(Rows.shift+4)).astype(BF)
            chunks(steps,body)
            acc_ref[...]=jnp.zeros_like(acc_ref)
    stream(po,cut[5],M2,F+B+M0+M1,lower)
    ticks()
    tau=F+B+M0+M1+M2
    after(cut[1]-1,ai,F); after(cut[3]-1,ao,F+B); after(cut[4]-1,pi,F+B+M0); after(cut[5]-1,po,F+B+M0+M1)
    @pl.when(j==cut[6]-1)
    def _():
        comm.run(comm.ticks-1,1)
        column(fi1,0,tau%2).start(); band(fo1,0,0).start()
    @pl.when(j>=cut[6])
    def _(): feed_tile(j-cut[6],tau+j-cut[6],1,hid4_ref,act1_ref,dsl1_ref,fi1,fo1)
    @pl.when(j==cut[7]-1)
    def _():
        s5_ref[...]=jnp.zeros_like(s5_ref)
        def body(r):
            y=x3_ref[r,:]+0.5*(acc_ref[r,:]+row(Rows.outer+1))
            xhat,rstd=stats(y)
            ok=valid_ref[r,0:1]
            gain=row(Rows.gain+5)
            res_ref[r,:]=((xhat*gain+row(Rows.shift+5))*ok).astype(BF)
            dy=cot_ref[r,:].astype(F32)*ok
            dx4_ref[r,:]=norm_back(dy,gain,xhat,rstd)
            s5_ref[0]+=fold(dy*xhat)
            s5_ref[1]+=fold(dy)
        chunks(steps,body)

LAG=2; CUTS=[1,4,4,3,1,2,1,4,4]; MODES=['h','qhhq','hhqh','hqh','h','qh','h','qhhq','hhqh']
def early(S,vectors,tokens,cot,valid,mask,table,pick,heads,weights,cid):
    steps,width=tokens.shape; tile=512; taps=vectors[-1].shape[0]; L=vectors[0].shape[1]
    comm=Gather(S,[(Rows.count,L)]+weights,cuts=CUTS,modes=MODES,lag=LAG)
    hidden=comm.shapes[1][1]; size=width//heads
    F,B,A=hidden//tile,comm.shapes[3][1]//tile,width//128
    M=[comm.shapes[i][1]//tile for i in (4,5,6)]
    assert comm.shapes[2][0]*S==hidden and tile==hidden//S
    cut=np.cumsum([0,F,B,A]+M+[F]).tolist()
    within=lambda lo,n:(lambda j:jnp.minimum(jnp.maximum(j-lo,0),n-1))
    f0,at,f1=within(0,F),within(cut[2],A),within(cut[6],F)
    ins=list(vectors)+[tokens,cot,valid,mask,table,pick]
    D=jax.ShapeDtypeStruct
    b=D((steps,width),BF); f=D((steps,width),F32); hid=D((steps,hidden),BF)
    outs=[b,hid,hid,f,b,D((steps,3*width),BF),b,D((heads,steps,steps),BF),f,b,D((steps,2*width),BF),f,b,f,b,hid,hid,f,b,D((2,8,width),F32),D((Rows.count,width),F32)]
    specs=[whole(o.shape) for o in outs]
    for i,t in ((1,f0),(2,f0),(15,f1),(16,f1)): specs[i]=pl.BlockSpec((steps,tile),lambda j,t=t:(0,t(j)))
    specs[7]=pl.BlockSpec((128//size,steps,steps),lambda j:(at(j),0,0))
    V=pltpu.VMEM; sem=lambda n: pltpu.SemaphoreType.DMA((n,))
    scratch=[V((Rows.count,L),F32),V(comm.out_shapes[0].shape,BF),sem(1),V((steps,width),F32),V((2,)+comm.out_shapes[1].shape[:-1]+(tile,),BF),V((2,)+comm.out_shapes[2].shape[2:],BF),sem(2),sem(2),
        V((steps//QB,size,steps+QB),BF),V((3,steps,128),BF),V((steps+PAD,width),F32),V((steps,2*width),F32)]
    out=call(functools.partial(early_kernel,heads,taps),'gather_and_forward',(cut[-1],),ins,[whole(a.shape) for a in ins],outs,specs,scratch,comm,cid)
    return out[0],[a.reshape(-1,a.shape[-1]) for a in out[1]]


def local(S,R,tokens,lengths,cotangent,norm_gain,norm_shift,feed_in,feed_in_bias,feed_out,feed_out_bias,attention_in,attention_in_bias,attention_out,attention_out_bias,relative_table,pointwise_in,depthwise,pointwise_out):
    steps,width=tokens.shape; taps=depthwise.shape[0]
    live=jnp.arange(steps,dtype=jnp.int32)<lengths[0]
    valid=jnp.broadcast_to(live.astype(F32)[:,None],(steps,128))
    mask=jnp.broadcast_to(jnp.where(live,0.0,-1e30).astype(F32)[None,:],(8,steps))
    rows=relative_table.shape[0]
    table=jnp.pad(relative_table,((0,128-rows),(0,0)))
    pick=jnp.asarray(picker_table(steps,QB).astype(np.float32)).astype(BF)
    vectors=[norm_gain,norm_shift,feed_in_bias,feed_out_bias,attention_in_bias,attention_out_bias.reshape(1,-1),depthwise]
    weights=[(feed_in,0),(feed_out,0),attention_in,attention_out,pointwise_in,pointwise_out,(feed_in,1),(feed_out,1)]
    outs,full=early(S,vectors,tokens,cotangent,valid,mask,table,pick,HEADS,weights,0)
    hid0,act0,dsl0,x1,hid1,packed,mixed,p,x2,chid,up,depth,cact,x3,hid4,act1,dsl1,dx4,result,s5,vec=outs
    fi0,fo0,ai,ao,pi,po,fi1,fo1=full[1:]
    shapes=[feed_in.shape,feed_out.shape]+[a.shape for a in (attention_in,attention_out,pointwise_in,pointwise_out)]+[SUB]
    rest=[dx4,x3,x2,x1,hid4,hid1,hid0,chid,cact,mixed,up,depth,act1,act0,dsl1,dsl0,fi1,fo1,ai,ao,pi,po,fi0,fo0]
    (dtok,),outs=backward(S,packed,p,table,pick,HEADS,vec,valid,tokens,s5,rest,taps,shapes,1)
    sums=list(outs[:7])+[outs[-1]]
    if R>4:
        groups=[[g*4+i for g in range(R//4)] for i in range(4)]
        sums=[lax.psum(a,'rep',axis_index_groups=groups) for a in sums]
    gfi,gfo,gai,gao,gpi,gpo,small,common=[a.astype(F32) for a in sums]
    L=norm_gain.shape[1]
    ggain,gshift,gbout,gpbias,gmbias=[small[a:b,:L] for a,b in ((0,6),(6,12),(12,14),(14,16),(16,17))]
    gbin=small[17:19]; gdw=small[32:32+taps,:L]
    gtab=common.reshape(-1,SUB[1])[:rows,:relative_table.shape[1]]
    return (result,dtok,ggain,gshift,gfi,gbin,gfo,gbout,gai,gpbias,gao,gmbias[0],gtab,gpi,gdw,gpo)

HEADS=16

def solution(mesh):
    R,S=mesh.shape['rep'],mesh.shape['shard']
    rows=P(('rep','shard'),None)
    last,mid,first=P(None,'shard'),P(None,'shard',None),P('shard',None)
    weights=(last,last,mid,last,mid,last,first,last,first,P('shard'),P(),first,last,first)
    return jax.shard_map(functools.partial(local,S,R),mesh=mesh,in_specs=(rows,P(('rep','shard')),rows)+weights,out_specs=(rows,rows)+weights,check_vma=False)
```

```python
import functools, math
import numpy as np
import jax, jax.numpy as jnp
from jax import lax
from jax.experimental import pallas as pl
from jax.experimental.pallas import tpu as pltpu
from jax.sharding import PartitionSpec as P
LEFT=64; RIGHT=8
BF=jnp.bfloat16; F32=jnp.float32

def nn(a,b): return lax.dot_general(a,b,(((1,),(0,)),((),())),preferred_element_type=F32)
def nt(a,b): return lax.dot_general(a,b,(((1,),(1,)),((),())),preferred_element_type=F32)
def tn(a,b): return lax.dot_general(a,b,(((0,),(0,)),((),())),preferred_element_type=F32)

def picker_table(steps, block):
    span=steps+block
    n=np.arange(span)
    rows=[]
    for i in range(steps//block):
        off=np.where(n<steps, n, n-span)-block*i
        row=np.clip(off,-LEFT,RIGHT)+LEFT
        rows.append(np.arange(128)[:,None]==row[None,:])
    return np.stack(rows)

QB=128

MESH=pl.DeviceIdType.MESH
def al(v,m): return pl.multiple_of(v,m)
def during(lo,hi,body):
    def run(i,c):
        body(i); return c
    lax.fori_loop(lo,hi,run,0)

class Place:
    def __init__(self,S):
        self.S=S; self.Z=S//2
        r=lax.axis_index('rep'); s=lax.axis_index('shard')
        self.r,self.s=r,s
        self.c=lax.rem(r,2); self.x=lax.rem(r//2,2); self.y=lax.rem(s,2); self.z=s//2
        base=r-2*self.x-self.c
        self.d=1-2*self.c
        self.next=(r,2*self.zat(1)+self.y); self.prev=(r,2*self.zat(-1)+self.y)
        self.over_y=(r,2*self.z+1-self.y); self.over_x=(base+2*(1-self.x)+self.c,s); self.twin=(base+2*self.x+1-self.c,s)
    def zat(self,k): return lax.rem(self.z+self.d*k+2*self.Z,self.Z)
    def greet(self):
        bar=pltpu.get_barrier_semaphore()
        for dev in (self.next,self.prev,self.over_y,self.over_x,self.twin):
            pl.semaphore_signal(bar,inc=1,device_id=dev,device_id_type=MESH)
        pl.semaphore_wait(bar,5)

SUB=(128,512)
class Scatter:
    OWN=16; RING=8; GAP=2
    def __init__(self,S,counts,places,out_shapes,common=None,pause=None):
        self.places=places; self.counts=counts
        self.common=common
        self.S=S; Z=S//2
        n=self.n=sum(counts)
        (rows,wide)=SUB
        h,q=rows//2,rows//4
        self.h,self.q,self.Z=h,q,Z
        self.at=np.cumsum([0]+counts).tolist()
        self.inputs=[]
        self.finals=len(out_shapes)
        self.out_shapes=[jax.ShapeDtypeStruct(a,BF) for a in out_shapes]+[jax.ShapeDtypeStruct((n,Z,2,2,h,wide),BF)]
        G=self.GAP
        self.lag=[0]+[G*k for k in range(1,5+Z)]
        self.lag[4+Z]=self.lag[3+Z]+1
        self.lag.append(self.lag[4+Z]+1)
        self.gate,self.wait=pause or (n,0)
        self.ticks=n+self.wait+self.lag[-1]
        own,ring=min(n,self.OWN),min(n,self.RING)
        self.slots=own; self.ring=ring
        assert own>=self.lag[-1] and (self.wait==0 or n+self.wait<2*(self.gate+self.wait))
        V=lambda *d: pltpu.VMEM(d,BF)
        self.scratch=[V(n,rows,wide),V(own,Z,2,h,wide),V(ring,Z,2,h,wide),V(ring,Z,q,wide),V(ring,Z,q,wide),V(ring,Z-1,h,wide),V(ring,h,wide),
            pltpu.SemaphoreType.DMA((n,)),pltpu.SemaphoreType.DMA((n,5+Z)),pltpu.SemaphoreType.DMA((n,5+Z)),pltpu.SemaphoreType.DMA((n,2)),pltpu.SemaphoreType.REGULAR((4+Z,))]
        if common:
            self.out_shapes.append(jax.ShapeDtypeStruct((Z,2,common[2],wide),BF))
            self.scratch+=[V(Z,2,common[2],wide),pltpu.SemaphoreType.DMA((Z,)),pltpu.SemaphoreType.DMA((Z,)),pltpu.SemaphoreType.DMA((1,))]
            self.begin_common=common[0]+self.wait+self.lag[-1]+1
            self.ticks=max(self.ticks,self.begin_common+Z+1)
        self.out_specs=[pl.BlockSpec(memory_space=pl.ANY)]*len(self.out_shapes)
    def bind(self,ins,outs,scr):
        self.out=outs[:self.finals]; self.made=outs[self.finals]
        if self.common: self.all,self.cs,self.ct,self.co=scr[-4:]; self.all_out=outs[-1]; scr=scr[:-4]
        self.o,self.own,self.cr,self.xr,self.yr,self.zr,self.fr,self.os,self.ss,self.rs,self.ls,self.free=scr
        self.p=Place(self.S); return self
    def slot(self,i): return i if self.slots==self.n else lax.rem(i,self.slots)
    def land(self,i): return i if self.ring==self.n else lax.rem(i,self.ring)
    def remote(self,i,k,src,dst,dev):
        return pltpu.make_async_remote_copy(src,dst,self.ss.at[i,k],self.rs.at[i,k],device_id=dev,device_id_type=MESH)
    def first(self,i):
        return self.remote(i,0,self.made.at[i,:,:,1-self.p.c],self.cr.at[self.land(i)],self.p.twin)
    def load(self,i):
        return pltpu.make_async_copy(self.made.at[i,:,:,self.p.c],self.own.at[self.slot(i)],self.ls.at[i,0])
    def part(self,i,col,x): return self.own.at[self.slot(i),:,col,pl.ds(al(x*self.q,self.q),self.q)]
    def cross(self,i): return self.remote(i,2,self.part(i,1-self.p.y,1-self.p.x),self.xr.at[self.land(i)],self.p.over_x)
    def side(self,i): return self.remote(i,3,self.part(i,1-self.p.y,self.p.x),self.yr.at[self.land(i)],self.p.over_y)
    def hop(self,i,s): return self.remote(i,3+s,self.own.at[self.slot(i),self.p.zat(-s),self.p.y],self.zr.at[self.land(i),s-1],self.p.next)
    def swap(self,i): return self.remote(i,3+self.Z,self.own.at[self.slot(i),self.p.z,self.p.y],self.fr.at[self.land(i)],self.p.over_x)
    def half(self,i): return self.o.at[i,pl.ds(al(self.p.c*self.h,self.h),self.h)]
    def share(self,i): return self.remote(i,4+self.Z,self.half(i),self.half(i),self.p.twin)
    def save(self,i,place,unit):
        index,layer,across=place; rows,wide=SUB
        ref=self.out[index] if layer is None else self.out[index].at[layer]
        return pltpu.make_async_copy(self.o.at[i],ref.at[pl.ds(al(unit//across*rows,rows),rows),pl.ds(al(lax.rem(unit,across)*wide,wide),wide)],self.os.at[i])
    def ask(self,i,k):
        if self.ring<self.n:
            @pl.when(i>=self.ring)
            def _(): pl.semaphore_wait(self.free.at[k],1)
    def tell(self,i,k,dev):
        if self.ring<self.n:
            @pl.when(i<self.n-self.ring)
            def _(): pl.semaphore_signal(self.free.at[k],inc=1,device_id=dev,device_id_type=MESH)
    def begin(self): self.p.greet()
    def phase(self,k,i):
        p=self.p; Z=self.Z; here=self.slot(i); land=self.land(i)
        if k==0:
            self.first(i).start(); self.load(i).start()
        elif k==1:
            self.load(i).wait(); self.first(i).wait_recv()
            for col in (1-p.y,p.y):
                self.own[here,:,col]=self.own[here,:,col]+self.cr[land,:,col]
                if col is not p.y: self.cross(i).start()
        elif k==2:
            self.cross(i).wait_recv()
            ref=self.part(i,1-p.y,p.x); ref[...]=ref[...]+self.xr[land]
            self.side(i).start()
        elif k==3:
            self.side(i).wait_recv()
            ref=self.part(i,p.y,p.x); ref[...]=ref[...]+self.yr[land]
            self.ask(i,3); self.hop(i,1).start()
        elif k<3+Z:
            s=k-3
            self.hop(i,s).wait_recv()
            ref=self.own.at[here,p.zat(-1-s),p.y]; ref[...]=ref[...]+self.zr[land,s-1]
            self.tell(i,2+s,p.prev)
            if s+1<Z: self.ask(i,3+s); self.hop(i,s+1).start()
            else: self.swap(i).start()
        elif k==3+Z:
            self.swap(i).wait_recv()
            ref=self.half(i); ref[...]=self.own[here,p.z,p.y]+self.fr[land]
            self.share(i).start()
        elif k==4+Z:
            self.first(i).wait_send()
            self.cross(i).wait_send(); self.side(i).wait_send()
            for s in range(1,Z): self.hop(i,s).wait_send()
            self.swap(i).wait_send(); self.share(i).wait()
            for at,count,place in zip(self.at,self.counts,self.places):
                @pl.when((i>=at)&(i<at+count))
                def _(at=at,place=place): self.save(i,place,i-at).start()
        else: self.save(i,self.places[0],0).wait()
    def relay(self,s):
        p=self.p
        ref=self.all.at[p.z,p.y] if s==0 else self.all.at[p.zat(1-s)]
        return pltpu.make_async_remote_copy(ref,ref,self.cs.at[s],self.ct.at[s],device_id=p.over_y if s==0 else p.next,device_id_type=MESH)
    def spread_common(self,k):
        p=self.p; unit,at,count=self.common
        if k==0: self.all[p.z,p.y]=self.o[unit,at:at+count]
        else: self.relay(k-1).wait()
        if k<self.Z: self.relay(k).start()
        else:
            cp=pltpu.make_async_copy(self.all,self.all_out,self.co.at[0]); cp.start(); cp.wait()
    def run(self,lo,count):
        def tick(u):
            for k in reversed(range(len(self.lag))):
                v=u-self.lag[k]; turn=self.gate+self.wait
                inside=(v>=0)&(v<self.n+self.wait)
                @pl.when(inside&((v<self.gate)|(v>=turn)) if self.wait else inside)
                def _(k=k,v=v): self.phase(k,v-self.wait*(v//turn) if self.wait else v)
            if self.common:
                for k in range(self.Z+1):
                    @pl.when(u==self.begin_common+k)
                    def _(k=k): self.spread_common(k)
        during(0,count,lambda v:tick(lo+v))
    def spread(self,step,steps):
        per=-(-self.ticks//steps)
        self.run(step*per,per)

class Gather:
    def __init__(self,S,shards,cuts,modes,lag=2,ahead=1):
        self.S=S; Z=self.Z=S//2
        pick=lambda a: a if isinstance(a,tuple) else (a,None)
        self.local=[isinstance(a,tuple) and isinstance(a[0],int) for a in shards]
        pairs=[pick(a) for a,m in zip(shards,self.local) if not m]
        held=[]; self.source=[]
        for a,layer in pairs:
            k=next((k for k,v in enumerate(held) if v is a),None)
            if k is None: k=len(held); held.append(a)
            self.source.append((k,layer))
        fold_=lambda s: s[:-2]+(2,2,s[-2]//4,s[-1])
        self.inputs=[a.reshape(fold_(a.shape)) for a in held]
        self.shapes=[a if m else pick(a)[0].shape[-2:] for a,m in zip(shards,self.local)]
        self.cuts=cuts
        self.units=[(w,a) for w,k in enumerate(cuts) for a in range(k)]
        self.modes=''.join(modes)
        n=len(self.units); k=3*Z+1
        self.out_shapes=[jax.ShapeDtypeStruct((Z,2)+fold_(a),BF) for a in self.shapes]
        self.out_specs=[pl.BlockSpec(memory_space=pl.ANY)]*len(shards)
        self.scratch=[pltpu.VMEM(fold_(a),BF) for a,m in zip(self.shapes,self.local) if m]+[pltpu.SemaphoreType.DMA((n,k)),pltpu.SemaphoreType.DMA((n,k)),pltpu.SemaphoreType.DMA((n,))]
        self.plan={}
        for t in range(1,Z): self.plan[lag*t]=('z',t)
        self.plan[lag*Z]=('y',0); self.plan[lag*(Z+1)]=('x',0); self.plan[lag*(Z+2)]=('end',0)
        self.last=lag*(Z+2)
        self.ahead=ahead
        self.ticks=n+self.last
    def bind(self,ins,outs,scr):
        mine=list(scr[:-3]); source=list(self.source); self.i=[]
        for m in self.local:
            if m: self.i.append(mine.pop(0))
            else:
                k,layer=source.pop(0)
                self.i.append(ins[k] if layer is None else ins[k].at[layer])
        self.o=outs; self.ss,self.rs,self.ls=scr[-3:]; self.p=Place(self.S); return self
    def cp(self,u,kind,t=0):
        p=self.p; Z=self.Z; h=self.modes[u]=='h'; w,a=self.units[u]
        wide=self.shapes[w][1]//self.cuts[w]; cs=pl.ds(a*wide,wide); o=self.o[w]; i=self.i[w]
        k={'z':t-1,'y':Z-1+t,'u':2*Z-1+t-1,'x':3*Z-2,'a':3*Z-1,'b':3*Z}[kind]
        if kind=='z':
            zo=p.zat(1-t); dev=p.next
            dst=o.at[zo,p.y,p.c,:,:,cs] if h else o.at[zo,p.y,p.c,p.x,:,cs]; src=dst
            if t==1: src=i.at[p.c,:,:,cs] if h else i.at[p.c,p.x,:,cs]
        elif kind=='y':
            dst=src=o.at[p.zat(-t),p.y,p.c,p.x,:,cs]; dev=p.over_y
            if t==0: src=i.at[p.c,p.x,:,cs]
        elif kind=='u': src=dst=o.at[p.zat(-t),p.y,p.c,p.x,:,cs]; dev=p.over_x
        elif kind=='x': src=dst=o.at[:,1-p.y,p.c,p.x,:,cs]; dev=p.over_x
        else: src=dst=o.at[:,p.y if kind=='a' else 1-p.y,p.c,:,:,cs]; dev=p.twin
        return pltpu.make_async_remote_copy(src,dst,self.ss.at[u,k],self.rs.at[u,k],device_id=dev,device_id_type=MESH)
    def own(self,u):
        p=self.p; w,a=self.units[u]; wide=self.shapes[w][1]//self.cuts[w]; cs=pl.ds(a*wide,wide)
        return pltpu.make_async_copy(self.i[w].at[p.c,:,:,cs],self.o[w].at[p.z,p.y,p.c,:,:,cs],self.ls.at[u])
    def open(self,u):
        self.cp(u,'z',1).start(); self.cp(u,'y',0).start(); self.own(u).start()
    def begin(self):
        self.p.greet()
        for u in range(min(self.ahead,len(self.units))): self.open(u)
    def stage(self,u,kind,t):
        Z=self.Z; q=self.modes[u]=='q'
        if kind=='z':
            self.cp(u,'z',t).wait_recv()
            if t+1<Z: self.cp(u,'z',t+1).start()
            self.cp(u,'y',t).start()
            if q: self.cp(u,'u',t).start()
        elif kind=='y':
            for t in range(Z): self.cp(u,'y',t).wait_recv()
            self.cp(u,'x').start()
            self.own(u).wait()
            if not q: self.cp(u,'a').start()
        elif kind=='x':
            if q:
                for t in range(1,Z): self.cp(u,'u',t).wait_recv()
                self.cp(u,'a').start()
            self.cp(u,'x').wait_recv(); self.cp(u,'b').start()
        else:
            for t in range(1,Z):
                self.cp(u,'z',t).wait_send()
                if q: self.cp(u,'u',t).wait_send()
            for t in range(Z): self.cp(u,'y',t).wait_send()
            self.cp(u,'x').wait_send(); self.cp(u,'a').wait(); self.cp(u,'b').wait()
    def run(self,lo,count):
        n=len(self.units)
        for i in range(lo,min(lo+count,self.ticks)):
            if self.ahead<=i+self.ahead<n: self.open(i+self.ahead)
            for u in range(n):
                s=self.plan.get(i-u)
                if s: self.stage(u,*s)
    def done(self,w):
        return max(u for u,(a,_) in enumerate(self.units) if a==w)+self.last+1

VM=60<<20
def call(body,name,grid,ins,in_specs,outs,out_specs,scratch,side=None,cid=None):
    any_=pl.BlockSpec(memory_space=pl.ANY)
    extra=side.inputs if side else []
    a,b,c,d,e=len(ins),len(extra),len(outs),len(side.out_shapes) if side else 0,len(scratch)
    def kernel(*refs):
        comm=None
        cut=np.cumsum([0,a,b,c,d,e]).tolist()
        part=[refs[x:y] for x,y in zip(cut,cut[1:]+[len(refs)])]
        if side:
            comm=side.bind(part[1],part[3],part[5])
        body(comm,*part[0],*part[2],*part[4])
    out=pl.pallas_call(kernel,grid=grid,out_shape=list(outs)+(side.out_shapes if side else []),in_specs=list(in_specs)+[any_]*b,
        out_specs=list(out_specs)+(side.out_specs if side else []),scratch_shapes=list(scratch)+(side.scratch if side else []),
        compiler_params=pltpu.CompilerParams(vmem_limit_bytes=VM,**(dict(collective_id=cid,has_side_effects=True) if side else {})),name=name)(*ins,*extra)
    return out[:c],out[c:]


CH=64

def aside(body):
    def run(comm,*refs):
        if comm:
            @pl.when(pl.program_id(0)==0)
            def _(): comm.begin()
        body(*refs)
        if comm: comm.spread(pl.program_id(0),pl.num_programs(0))
    return run
def whole(shape):
    return pl.BlockSpec(shape,lambda *i:(0,)*len(shape),pipeline_mode=pl.Buffered(1))
def chunks(steps,body):
    def run(i,c):
        body(pl.ds(pl.multiple_of(i*CH,CH),CH)); return c
    lax.fori_loop(0,steps//CH,run,0)
def stats(v):
    center=v-jnp.mean(v,axis=-1,keepdims=True)
    rstd=lax.rsqrt(jnp.mean(center*center,axis=-1,keepdims=True)+1e-5)
    return center*rstd,rstd
def norm_back(dy,gain,xhat,rstd):
    g=dy*gain
    return rstd*(g-jnp.mean(g,axis=-1,keepdims=True)-xhat*jnp.mean(g*xhat,axis=-1,keepdims=True))
def sigmoid(v): return 0.5*jnp.tanh(0.5*v)+0.5
def fold(v): return jnp.sum(v.reshape(v.shape[0]//8,8,v.shape[1]),axis=0)

PAD=32
RC=128
def over_columns(width,body):
    def run(i,c):
        body(pl.ds(pl.multiple_of(i*128,128),128)); return c
    lax.fori_loop(0,width//128,run,0)
def taps_of(taps,lead,residue):
    return [(a,k) for k in range(taps) for a in [lead(k)//8] if lead(k)%8==residue]
def slide(pad_ref,w_ref,lead,taps,t0,cols):
    acc=jnp.zeros((RC,128),F32)
    for b in range(8):
        use=taps_of(taps,lead,b)
        if not use: continue
        top=max(a for a,_ in use)
        slab=pad_ref[t0+b:t0+b+RC+8*top,cols]
        for a,k in use: acc=acc+w_ref[k:k+1,cols]*slab[8*a:8*a+RC]
    return acc

VECTOR_ROWS=64
def plan_ticks(comm,phases,pace,limit):
    at=[]; done=0; spent=0.0
    for st,t in enumerate(phases):
        spent+=t
        target=max(done,min(int(spent/pace),limit(st),comm.ticks))
        at.append((done,target-done)); done=target
    return at

def backward_kernel(taps,size,comm,q_ref,k_ref,v_ref,p_ref,table_ref,pick_ref,vec_ref,valid_ref,tok_ref,s5_ref,
        dx4,x3,x2,x1,hid4,hid1,hid0,chid,cact,mixed,up,depth,act1,act0,dsl1,dsl0,fi1,fo1,ai,ao,pi,po,fi0,fo0,out_ref,
        d_ref,x_ref,acc_ref,low_ref,turn_ref,hid_ref,big_ref,stage_ref,ds_ref,grad_ref,wa_ref,wb_ref,wd_ref,pad_ref,tail_ref,rows_ref,sums_ref,ddw_ref,dbin_ref,psum_ref,dtab_ref,
        sem_d,sem_x,sem_hid,sem_big,sem_a,sem_b,sem_c,stage_sem):
    steps,width=d_ref.shape; wide=SUB[1]; S=comm.S; across=width//wide; CUT=act1.shape[1]//S
    F=act1.shape[1]//wide; A=width//128; B=ai.shape[1]//wide; M0,M1,M2=po.shape[1]//wide,pi.shape[1]//wide,ao.shape[1]//wide
    cut=np.cumsum([0,F,F,M0,1,M1,M2,A,B,F,F,1]).tolist()
    FB,FD,MP,MC,MI,MO,AT,PB,CB,CD,EN=cut[:11]
    units=np.cumsum([0,F,F,M0,M1,M2,B,F,1,F]).tolist()
    j=pl.program_id(0)
    made=[]; n=0
    for st in range(cut[-1]):
        n+=0 if MC<=st<MI or AT<=st<PB or st==EN else 1
        if st==CD: n+=1
        made.append(n)
    def limit(st):
        if AT<=st<PB: return comm.gate+comm.wait
        return made[st]-2+(comm.wait if st>=PB else 0)
    times=[2.9]*F+[1.0]*F+[3]*M0+[15]+[2.5]*(M1-1)+[5]+[3]*M2+[4.7]*A+[2.8]*B+[3.8]*F+[1.0]*F+[0]
    at=plan_ticks(comm,times,PACE,limit)
    def ticks(step,share=(0,1)):
        lo,n=at[step]; a,b=n*share[0]//share[1],n*(share[0]+1)//share[1]
        if b>a: comm.run(lo+a,b-a)
    def ticks_of(lo,hi):
        for st in range(lo,hi):
            if at[st][1]:
                @pl.when(j==st)
                def _(st=st): ticks(st)
    def phase(lo,hi):
        return pl.when((j>=lo)&(j<hi))
    def last(step): return pl.when(j==step)
    def fill(src,dst,sem): return pltpu.make_async_copy(src,dst,sem)
    def row(i): return vec_ref[i:i+1,:]
    def here(i): return pl.ds(al(i*wide,wide),wide)
    def column(w,i,slot): return fill(w.at[:,here(i)],wa_ref.at[slot],sem_a.at[slot])
    def band(w,i): return fill(w.at[here(i)],wb_ref.at[lax.rem(i,2)],sem_b.at[lax.rem(i,2)])
    def slope(w,i): return fill(w.at[:,here(i)],wd_ref.at[lax.rem(i,2)],sem_c.at[lax.rem(i,2)])
    def load(ref,dst,sem): return fill(ref,dst,sem.at[0])
    def lefts(act,a,slot):
        return [fill(act.at[:,pl.ds(al(s*CUT+a*SUB[0],SUB[0]),SUB[0])],big_ref.at[slot,:,pl.ds(s*SUB[0],SUB[0])],sem_big.at[slot,s]) for s in range(S)]
    def whole_big(src,slot): return fill(src,big_ref.at[slot],sem_big.at[slot,0])
    def put(q): return fill(stage_ref.at[lax.rem(q,2)],comm.made.at[q],stage_sem.at[lax.rem(q,2)])
    first_late=units[5]
    def unit(q,value):
        @pl.when((q>=2)&((q<first_late)|(q>=first_late+2)))
        def _(): put(q-2).wait()
        stage_ref[lax.rem(q,2)]=value.reshape(stage_ref.shape[1:])
        put(q).start()
    def stream(w,lo,n,tau0,use):
        @phase(lo,lo+n)
        def _():
            i=j-lo; slot=lax.rem(tau0+i,2)
            column(w,i,slot).wait()
            @pl.when(i+1<n)
            def _(): column(w,i+1,lax.rem(tau0+i+1,2)).start()
            use(i,wa_ref.at[slot])
    def ahead(w,tau): column(w,0,tau%2).start()
    tau=np.cumsum([0,F,M0,M1,M2,B]).tolist()

    def feed_step(i,w_out,slopes,q,side,fi):
        band(w_out,i).wait(); slope(slopes,i).wait()
        @pl.when(i+1<F)
        def _(): band(w_out,i+1).start(); slope(slopes,i+1).start()
        s=lax.rem(i,2)
        dpre=(nt(low_ref[:,:width],wb_ref[s])*wd_ref[s].astype(F32)).astype(BF)
        dbin_ref[side,:,here(i)]=fold(dpre.astype(F32))
        acc_ref[...]+=nt(dpre,fi[...])
        unit(q+i,nn(turn_ref[...],dpre).astype(BF))
    def norm_step(source,i,at_,after):
        def body(r):
            xhat,rstd=stats(source[r,:].astype(F32))
            dy=acc_ref[r,:]
            sums_ref[at_]+=fold(dy*xhat); sums_ref[at_+1]+=fold(dy)
            after(r,d_ref[r,:]+norm_back(dy,row(Rows.gain+i),xhat,rstd))
        chunks(steps,body)
    def out_units(act,lo,q):
        @phase(lo,lo+F)
        def _():
            d=j-lo; a=d//across
            for slot in range(3):
                @pl.when((lax.rem(a,3)==slot)&(lax.rem(d,across)==0))
                def _(slot=slot):
                    for cp in lefts(act,a,slot): cp.wait()
            unit(q+d,tn(big_ref[lax.rem(a,3)],low_ref[:,here(lax.rem(d,across))]).astype(BF))
            @pl.when(d==across-1)
            def _():
                for a in range(3,F//across):
                    for cp in lefts(act,a,a-3): cp.start()
    def start_feed(act,fo,slopes):
        for a in range(3):
            for cp in lefts(act,a,a): cp.start()
        band(fo,0).start(); slope(slopes,0).start()

    @last(0)
    def _():
        comm.begin()
        load(dx4,d_ref,sem_d).start(); load(hid4,hid_ref,sem_hid).start(); load(x3,x_ref,sem_x).start()
        ahead(fi1,0); start_feed(act1,fo1,dsl1)
        sums_ref[...]=jnp.zeros_like(sums_ref)
        dtab_ref[...]=jnp.zeros_like(dtab_ref)
        acc_ref[...]=jnp.zeros_like(acc_ref)
        tail_ref[steps:steps+PAD,:]=jnp.zeros((PAD,width),F32)
        pad_ref[0:PAD,:]=jnp.zeros((PAD,width),F32)
        load(dx4,d_ref,sem_d).wait()
        def body(r):
            df=(0.5*d_ref[r,:]).astype(BF)
            low_ref[r,:width]=df
            sums_ref[12]+=fold(df.astype(F32))
        chunks(steps,body)
        load(hid4,hid_ref,sem_hid).wait()
        turn_ref[...]=hid_ref[...].T
        load(chid,hid_ref,sem_hid).start()
    stream(fi1,FB,F,tau[0],lambda i,w: feed_step(i,fo1,dsl1,units[0],0,w))
    @last(FD-1)
    def _():
        load(x3,x_ref,sem_x).wait()
        def after(r,v): d_ref[r,:]=v
        norm_step(x_ref,4,8,after)
        load(depth,x_ref,sem_x).start()
        ahead(po,tau[1])
    out_units(act1,FD,units[1])
    @last(MP-1)
    def _():
        whole_big(up.at[:,:width],0).start(); whole_big(up.at[:,width:],1).start(); whole_big(cact,2).start()
        def body(r): low_ref[r,:width]=d_ref[r,:].astype(BF)
        chunks(steps,body)
        acc_ref[...]=jnp.zeros_like(acc_ref)
    def lower(i,w):
        @pl.when(i==0)
        def _(): whole_big(cact,2).wait()
        acc_ref[...]+=nt(low_ref[:,here(i)],w[...])
        unit(units[2]+i,tn(big_ref[2],low_ref[:,here(i)]).astype(BF))
        @pl.when(i==M0-1)
        def _(): ahead(pi,tau[2])
    stream(po,MP,M0,tau[1],lower)
    @last(MC)
    def _():
        weights=vec_ref.at[Rows.taps:Rows.taps+32]
        load(depth,x_ref,sem_x).wait(); whole_big(cact,0).wait(); whole_big(cact,1).wait()
        def three(i,c):
            r=pl.ds(pl.multiple_of(i*CH,CH),CH)
            xhat,rstd=stats(x_ref[r,:])
            gain=row(Rows.gain+3)
            z=xhat*gain+row(Rows.shift+3)
            sg=sigmoid(z)
            dz=acc_ref[r,:]*(sg*(1.0+z*(1.0-sg)))
            sums_ref[6]+=fold(dz*xhat); sums_ref[7]+=fold(dz)
            tail_ref[r,:]=norm_back(dz,gain,xhat,rstd)
            pad_ref[pl.ds(pl.multiple_of(i*CH+PAD,PAD),CH),:]=big_ref[0,r,:].astype(F32)*sigmoid(big_ref[1,r,:].astype(F32))*valid_ref[r,0:1]
            return c
        lax.fori_loop(0,steps//CH,three,0)
        load(x2,x_ref,sem_x).start()
        ticks(MC,(0,3))
        def conv(cols):
            for t0 in range(0,steps,RC):
                acc_ref[t0:t0+RC,cols]=slide(tail_ref,weights,lambda k:taps-1-k,taps,t0,cols)
        over_columns(width,conv)
        ticks(MC,(1,3))
        def gate(r):
            a=big_ref[0,r,:].astype(F32); sg=sigmoid(big_ref[1,r,:].astype(F32))
            dg=acc_ref[r,:]*valid_ref[r,0:1]*sg
            low_ref[r,:width]=dg.astype(BF)
            low_ref[r,width:]=(dg*a*(1.0-sg)).astype(BF)
        chunks(steps,gate)
        acc_ref[...]=jnp.zeros_like(acc_ref)
        ticks(MC,(2,3))
    def raised(i,w):
        @pl.when(i==0)
        def _(): load(chid,hid_ref,sem_hid).wait()
        acc_ref[...]+=nt(low_ref[:,here(i)],w[...])
        unit(units[3]+i,tn(hid_ref[...],low_ref[:,here(i)]).astype(BF))
        @pl.when(i==M1-1)
        def _():
            load(mixed,hid_ref,sem_hid).start()
            ahead(ao,tau[3])
            load(x2,x_ref,sem_x).wait()
            def after(r,v):
                d_ref[r,:]=v
                da=v.astype(BF)
                low_ref[r,:width]=da
                sums_ref[13]+=fold(da.astype(F32))
            norm_step(x_ref,2,4,after)
            load(x1,x_ref,sem_x).start()
            acc_ref[...]=jnp.zeros_like(acc_ref)
    stream(pi,MI,M1,tau[2],raised)
    def joined(i,w):
        @pl.when(i==0)
        def _(): load(mixed,hid_ref,sem_hid).wait()
        acc_ref[...]+=nt(low_ref[:,here(i)],w[...])
        unit(units[4]+i,tn(hid_ref[...],low_ref[:,here(i)]).astype(BF))
        @pl.when(i==M2-1)
        def _():
            load(hid1,hid_ref,sem_hid).start()
            ahead(ai,tau[4])
            low_ref[:,width:]=acc_ref[...].astype(BF)
            acc_ref[...]=jnp.zeros_like(acc_ref)
    stream(ao,MO,M2,tau[3],joined)
    ticks_of(FB,MC); ticks_of(MI,AT)
    @last(AT)
    def _():
        for q in (first_late-2,first_late-1): put(q).wait()
    lo_at=at[AT][0]
    @phase(AT,PB)
    def _():
        h=j-AT
        mine=pl.ds(al(h*128,128),128)
        grad_ref[...]=low_ref[:,pl.ds(al(width+h*128,128),128)]
        parts=heads_back(q_ref,k_ref,v_ref,p_ref,grad_ref,table_ref,pick_ref,dtab_ref,ds_ref,size)
        for part in range(3): big_ref[part,:,mine]=parts[part]
        psum_ref[0:1,mine]=jnp.sum(big_ref[0,:,mine].astype(F32),axis=0,keepdims=True)
        psum_ref[1:2,mine]=jnp.sum(big_ref[2,:,mine].astype(F32),axis=0,keepdims=True)
        comm.run(lo_at+h*ATICKS,ATICKS)
    start=lo_at+ATICKS*A
    assert start<=comm.gate+comm.wait
    late=plan_ticks(comm,times[PB:],PACE2,lambda st: limit(PB+st)-start)
    for st in range(PB,EN): at[st]=(start+late[st-PB][0],late[st-PB][1])
    def packed_back(b,w):
        @pl.when(b==0)
        def _():
            load(hid1,hid_ref,sem_hid).wait()
            turn_ref[...]=hid_ref[...].T
            load(hid0,hid_ref,sem_hid).start()
        g=big_ref[b//across,:,here(lax.rem(b,across))]
        acc_ref[...]+=nt(g,w[...])
        unit(units[5]+b,nn(turn_ref[...],g).astype(BF))
        @pl.when(b==B-1)
        def _():
            ahead(fi0,tau[5]); start_feed(act0,fo0,dsl0)
            load(x1,x_ref,sem_x).wait(); load(hid0,hid_ref,sem_hid).wait()
            turn_ref[...]=hid_ref[...].T
            def after(r,v):
                d_ref[r,:]=v
                df=(0.5*v).astype(BF)
                low_ref[r,:width]=df
                sums_ref[11]+=fold(df.astype(F32))
            norm_step(x_ref,1,2,after)
            acc_ref[...]=jnp.zeros_like(acc_ref)
    stream(ai,PB,B,tau[4],packed_back)
    stream(fi0,CB,F,tau[5],lambda i,w: feed_step(i,fo0,dsl0,units[6],1,w))
    @phase(CB,CD)
    def _():
        def conv_weights(cols):
            lead=lambda k:k+PAD-taps+1
            for b in range(8):
                use=taps_of(taps,lead,b)
                if not use: continue
                top=max(a for a,_ in use)
                parts={k:jnp.zeros((8,128),F32) for _,k in use}
                for t0 in range(0,steps,RC):
                    slab=pad_ref[t0+b:t0+b+RC+8*top,cols]
                    dd=tail_ref[t0:t0+RC,cols]
                    for a,k in use: parts[k]=parts[k]+fold(slab[8*a:8*a+RC]*dd)
                for k,v in parts.items(): ddw_ref[k:k+1,cols]=jnp.sum(v,axis=0,keepdims=True)
        for a in range(A//F): conv_weights(pl.ds(al((j-CB)*(A//F)*128+a*128,128),128))
    @last(CD-1)
    def _():
        def after(r,v): out_ref[r,:]=v.astype(BF)
        norm_step(tok_ref,0,0,after)
        rows_ref[...]=jnp.zeros_like(rows_ref)
        total=lambda v: jnp.sum(v,axis=0,keepdims=True)
        rows=[sums_ref[0],sums_ref[2],sums_ref[4],sums_ref[6],sums_ref[8],s5_ref[0],sums_ref[1],sums_ref[3],sums_ref[5],sums_ref[7],sums_ref[9],s5_ref[1],sums_ref[11],sums_ref[12]]
        rows=[total(v) for v in rows]+[psum_ref[0:1,:],psum_ref[1:2,:],total(sums_ref[13])]
        L=width//S
        for i,v in enumerate(rows):
            for s in range(S): rows_ref[s,i:i+1,0:L]=v[:,s*L:s*L+L]
        k=len(rows)
        for i in range(2):
            v=total(dbin_ref[1-i])
            for s in range(S): rows_ref[s,k+i:k+i+1,:]=v[:,s*wide:s*wide+wide]
        n=dtab_ref.shape[0]//S
        for s in range(S):
            rows_ref[s,32:32+taps,0:L]=ddw_ref[0:taps,s*L:s*L+L]
            rows_ref[s,VECTOR_ROWS:VECTOR_ROWS+n,0:size]=dtab_ref[s*n:s*n+n,:]
    @last(CD)
    def _(): unit(units[7],rows_ref[...].astype(BF).reshape(S*SUB[0],wide))
    out_units(act0,CD,units[8])
    ticks_of(PB,EN)
    @last(EN)
    def _():
        for q in (units[9]-2,units[9]-1): put(q).wait()
        lo=sum(at[EN-1])
        comm.run(lo,comm.ticks-lo)

def heads_back(q_ref,k_ref,v_ref,p_ref,g_ref,table_ref,pick_ref,dtab_ref,ds_ref,size):
    steps=q_ref.shape[0]; nb=steps//QB; span=steps+QB
    scale=1.0/math.sqrt(size)
    flip=(lax.broadcasted_iota(jnp.int32,(QB,QB),0)+lax.broadcasted_iota(jnp.int32,(QB,QB),1)==QB-1).astype(F32).astype(BF)
    sl=[slice(i*QB,(i+1)*QB) for i in range(nb)]
    out=[]
    for hh in range(q_ref.shape[1]//size):
        cols=slice(hh*size,(hh+1)*size)
        dss=[]
        for r in sl:
            p=p_ref[hh,r,:].astype(F32)
            t=p*nt(g_ref[r,cols],v_ref[:,cols])
            dss.append((t-p*jnp.sum(t,axis=1,keepdims=True)).astype(BF))
        for r,ds in zip(sl,dss): ds_ref[r,:]=ds
        xs=[nn(flip,ds) for ds in dss]
        xs=[pltpu.roll(jnp.concatenate([x,jnp.zeros((QB,QB),F32)],axis=1),span-QB+1,1,stride=1,stride_axis=0).astype(BF) for x in xs]
        xs=[(nt(x,pick_ref[i])*scale).astype(BF) for i,x in enumerate(xs)]
        drel=jnp.concatenate([nn(flip,x).astype(BF) for x in xs],axis=0)
        dq=(nn(ds_ref[...],k_ref[:,cols])*scale+nn(drel,table_ref[...])).astype(BF)
        dtab_ref[...]+=tn(drel,q_ref[:,cols])
        out.append((dq,(tn(ds_ref[...],q_ref[:,cols])*scale).astype(BF),tn(p_ref[hh],g_ref[:,cols]).astype(BF)))
    return [jnp.concatenate([a[part] for a in out],axis=1) for part in range(3)]

PACE=4.5; PAUSE=0; PACE2=2.0; ATICKS=1
def backward(S,packed,p,table,pick,heads,vec,valid,tokens,s5,rest,taps,out_shapes,cid):
    steps,width=tokens.shape; size=width//heads; wide=SUB[1]; across=width//wide
    act1,ai,ao,pi,po=rest[12],rest[18],rest[19],rest[20],rest[21]
    hidden=act1.shape[1]; F=hidden//wide; A=width//128; B=ai.shape[1]//wide; M0,M1,M2=[a.shape[1]//wide for a in (po,pi,ao)]
    assert hidden//S==wide and width//S==SUB[0] and wide//SUB[0]<=4 and A%F==0
    counts=[F,F,M0,M1,M2,B,F,1,F]
    places=[(0,1,F),(1,1,across),(5,None,across),(4,None,2*across),(3,None,across),(2,None,3*across),(0,0,F),(6,None,1),(1,0,across)]
    comm=Scatter(S,counts,places,out_shapes,common=(sum(counts[:7]),VECTOR_ROWS,table.shape[0]//S),pause=(sum(counts[:5]),PAUSE))
    start=2*F+M0+1+M1+M2
    head=lambda o:pl.BlockSpec((steps,128),lambda j:(0,o*A+jnp.minimum(jnp.maximum(j-start,0),A-1)))
    ins=[packed,packed,packed,p,table,pick,vec,valid,tokens,s5]
    specs=[head(0),head(1),head(2),pl.BlockSpec((128//size,steps,steps),lambda j:(jnp.minimum(jnp.maximum(j-start,0),A-1),0,0))]+[whole(a.shape) for a in ins[4:]]
    specs+=[pl.BlockSpec(memory_space=pl.ANY)]*len(rest)
    V=pltpu.VMEM; Z=S//2; sem=lambda *n: pltpu.SemaphoreType.DMA(n)
    sq=lambda t: V((steps,width),t)
    scratch=[sq(F32),sq(F32),sq(F32),V((steps,2*width),BF),V((width,steps),BF),sq(BF),V((3,steps,width),BF),V((2,Z,2,2,SUB[0]//2,wide),BF),V((steps,steps),BF),V((steps,128),BF),
        V((2,width,wide),BF),V((2,wide,width),BF),V((2,steps,wide),BF),V((steps+PAD,width),F32),V((steps+PAD,width),F32),V((S,)+SUB,F32),V((14,8,width),F32),V((32,width),F32),V((2,8,hidden),F32),V((8,width),F32),V((128,size),F32),
        sem(1),sem(1),sem(1),sem(3,S),sem(2),sem(2),sem(2),sem(2)]
    return call(functools.partial(backward_kernel,taps,size),'backward_and_sums',(start+A+B+2*F+1,),ins+list(rest),specs,[jax.ShapeDtypeStruct((steps,width),BF)],[whole((steps,width))],scratch,comm,cid)

class Rows:
    gain=0; shift=8; inner=16; outer=24; packed=26; mixed=28; taps=32; count=64

def early_kernel(heads,taps,comm,gain_in,shift_in,inner_in,outer_in,packed_in,mixed_in,taps_in,tok_ref,cot_ref,valid_ref,mask_ref,table_ref,pick_ref,
        hid0_ref,act0_ref,dsl0_ref,x1_ref,hid1_ref,packed_ref,mixed_ref,p_ref,x2_ref,chid_ref,up_ref,depth_ref,cact_ref,x3_ref,hid4_ref,act1_ref,dsl1_ref,dx4_ref,res_ref,s5_ref,vec_ref,
        own_ref,land_ref,land_sem,acc_ref,wa_ref,wb_ref,sem_a,sem_b,rel_ref,qkv_ref,pad_ref,wide_ref):
    steps,width=tok_ref.shape; tile=wa_ref.shape[-1]; S=comm.S
    small,fi0,fo0,ai,ao,pi,po,fi1,fo1=comm.o
    F,B,M0,M1,M2=[w.shape[-1]//tile for w in (fi0,ai,ao,pi,po)]; A=width//128
    size=width//heads
    cut=np.cumsum([0,F,B,A,M0,M1,M2,F]).tolist()
    j=pl.program_id(0)
    L=width//S
    def row(i): return vec_ref[i:i+1,:]
    def column(w,i,slot): return pltpu.make_async_copy(w.at[:,:,:,:,:,pl.ds(al(i*tile,tile),tile)],wa_ref.at[slot],sem_a.at[slot])
    def band(w,i,slot): return pltpu.make_async_copy(w.at[i//2,lax.rem(i,2)],wb_ref.at[slot],sem_b.at[slot])
    def wa(slot): return wa_ref[slot].reshape(width,tile)
    want=[comm.done(2),comm.done(3),comm.done(4),comm.done(5),comm.done(6),comm.done(8)]
    at={}; done=want[0]
    times=[20/F]*F+[10/B]*B+[26/A]*A+[3]*M0+[2]*(M1-1)+[14]+[3]*M2
    need={cut[1]-1:want[1],cut[3]-1:want[2],cut[4]-1:want[3],cut[5]-1:want[4],cut[6]-1:comm.ticks-1}
    for st in range(cut[6]):
        target=want[0]+int((comm.ticks-1-want[0])*sum(times[:st+1])/sum(times))
        target=max(target,need.get(st,0))
        if target>done: at[st]=(done,target-done); done=target
    def ticks():
        for st,(lo,n) in at.items():
            @pl.when(j==st)
            def _(lo=lo,n=n): comm.run(lo,n)
    @pl.when(j==0)
    def _():
        own_ref[...]=jnp.zeros_like(own_ref)
        for at_,ref in ((Rows.gain,gain_in),(Rows.shift,shift_in),(Rows.outer,outer_in),(Rows.packed,packed_in),(Rows.mixed,mixed_in),(Rows.taps,taps_in)):
            own_ref[at_:at_+ref.shape[0],:]=ref[...].astype(F32)
        k=inner_in.shape[1]//L
        for l in range(2):
            for i in range(k): own_ref[Rows.inner+l*k+i:Rows.inner+l*k+i+1,:]=inner_in[l:l+1,i*L:i*L+L].astype(F32)
        comm.i[0][...]=own_ref[...].astype(BF).reshape(comm.i[0].shape)
        comm.begin()
        comm.run(0,want[0])
        cp=pltpu.make_async_copy(small,land_ref,land_sem.at[0]); cp.start()
        column(fi0,0,0).start(); band(fo0,0,0).start()
        cp.wait()
        for s in range(S): vec_ref[:,s*L:s*L+L]=land_ref[s//2,s%2].reshape(Rows.count,L).astype(F32)
        for i in range(steps//QB): rel_ref[i]=tn(table_ref[...],pick_ref[i]).astype(BF)
        def body(r):
            xhat,_r=stats(tok_ref[r,:].astype(F32))
            hid0_ref[r,:]=(xhat*row(Rows.gain)+row(Rows.shift)).astype(BF)
        chunks(steps,body)
        acc_ref[...]=jnp.zeros_like(acc_ref)
        pad_ref[0:PAD,:]=jnp.zeros((PAD,width),F32)
    def feed_tile(i,tau,l,hid_ref,act_ref,dsl_ref,fi,fo):
        slot=lax.rem(tau,2); k=tile//L
        column(fi,i,slot).wait(); band(fo,i,lax.rem(i,2)).wait()
        @pl.when(i+1<F)
        def _(): column(fi,i+1,lax.rem(tau+1,2)).start(); band(fo,i+1,lax.rem(i+1,2)).start()
        bias=jnp.concatenate([vec_ref[Rows.inner+l*k+a:Rows.inner+l*k+a+1,pl.ds(al(i*L,L),L)] for a in range(k)],axis=1)
        pre=nn(hid_ref[...],wa(slot))+bias
        sg=sigmoid(pre)
        act_ref[...]=(pre*sg).astype(BF)
        dsl_ref[...]=(sg*(1.0+pre*(1.0-sg))).astype(BF)
        acc_ref[...]+=nn(act_ref[...],wb_ref[lax.rem(i,2)].reshape(tile,width))
    @pl.when(j<cut[1])
    def _(): feed_tile(j,j,0,hid0_ref,act0_ref,dsl0_ref,fi0,fo0)
    @pl.when(j==cut[1]-1)
    def _():
        def body(r):
            x=tok_ref[r,:].astype(F32)+0.5*(acc_ref[r,:]+row(Rows.outer))
            x1_ref[r,:]=x
            xhat,_r=stats(x)
            hid1_ref[r,:]=(xhat*row(Rows.gain+1)+row(Rows.shift+1)).astype(BF)
        chunks(steps,body)
    def stream(w,lo,n,tau0,use):
        @pl.when((j>=lo)&(j<lo+n))
        def _():
            i=j-lo; slot=lax.rem(tau0+i,2)
            column(w,i,slot).wait()
            @pl.when(i+1<n)
            def _(): column(w,i+1,lax.rem(tau0+i+1,2)).start()
            use(i,slot)
    def after(step,w,tau):
        @pl.when(j==step)
        def _(): column(w,0,lax.rem(tau,2)).start()
    def here(i): return pl.ds(al(i*tile,tile),tile)
    def pack(i,slot):
        v=nn(hid1_ref[...],wa(slot))
        per=width//tile
        @pl.when(i<per)
        def _(): packed_ref[:,here(i)]=(v+vec_ref[Rows.packed:Rows.packed+1,here(lax.rem(i,per))]).astype(BF)
        @pl.when((i>=per)&(i<2*per))
        def _(): packed_ref[:,here(i)]=v.astype(BF)
        @pl.when(i>=2*per)
        def _(): packed_ref[:,here(i)]=(v+vec_ref[Rows.packed+1:Rows.packed+2,here(lax.rem(i,per))]).astype(BF)
    stream(ai,cut[1],B,F,pack)
    @pl.when((j>=cut[2])&(j<cut[3]))
    def _():
        h=j-cut[2]
        for a in range(3): qkv_ref[a]=packed_ref[:,pl.ds(al(a*width+h*128,128),128)]
        scale=1.0/math.sqrt(size)
        sl=[slice(i*QB,(i+1)*QB) for i in range(steps//QB)]; outs=[]
        for hh in range(128//size):
            cols=slice(hh*size,(hh+1)*size)
            rels=[nn(qkv_ref[0,r,cols],rel_ref[i]) for i,r in enumerate(sl)]
            rels=[pltpu.roll(x,0,1,stride=1,stride_axis=0)[:,:steps] for x in rels]
            ss=[(nt(qkv_ref[0,r,cols],qkv_ref[1,:,cols])+x)*scale+mask_ref[0:1,:] for r,x in zip(sl,rels)]
            es=[jnp.exp(s-jnp.max(s,axis=1,keepdims=True)) for s in ss]
            ps=[(e*(1.0/jnp.sum(e,axis=1,keepdims=True))).astype(BF) for e in es]
            for r,p in zip(sl,ps): p_ref[hh,r,:]=p
            outs.append(jnp.concatenate([nn(p,qkv_ref[2,:,cols]).astype(BF) for p in ps],axis=0))
        mixed_ref[:,pl.ds(al(h*128,128),128)]=jnp.concatenate(outs,axis=1)
    def join(i,slot):
        x2_ref[:,here(i)]=x1_ref[:,here(i)]+nn(mixed_ref[...],wa(slot))+vec_ref[Rows.mixed:Rows.mixed+1,here(i)]
        @pl.when(i==M0-1)
        def _():
            def body(r):
                xhat,_r=stats(x2_ref[r,:])
                chid_ref[r,:]=(xhat*row(Rows.gain+2)+row(Rows.shift+2)).astype(BF)
            chunks(steps,body)
    stream(ao,cut[3],M0,F+B,join)
    def raise_(i,slot):
        wide_ref[:,here(i)]=nn(chid_ref[...],wa(slot))
        @pl.when(i==M1-1)
        def _():
            def gate(k,c):
                r=pl.ds(pl.multiple_of(k*CH,CH),CH)
                a=wide_ref[r,:width]; b=wide_ref[r,width:]
                up_ref[r,:width]=a.astype(BF); up_ref[r,width:]=b.astype(BF)
                pad_ref[pl.ds(pl.multiple_of(k*CH+PAD,PAD),CH),:]=a*sigmoid(b)*valid_ref[r,0:1]
                return c
            lax.fori_loop(0,steps//CH,gate,0)
            weights=vec_ref.at[Rows.taps:Rows.taps+32]
            def conv(cols):
                for t0 in range(0,steps,RC):
                    depth_ref[t0:t0+RC,cols]=slide(pad_ref,weights,lambda k:k+PAD-taps+1,taps,t0,cols)
            over_columns(width,conv)
            def body(r):
                xhat,_r=stats(depth_ref[r,:])
                z=xhat*row(Rows.gain+3)+row(Rows.shift+3)
                cact_ref[r,:]=(z*sigmoid(z)).astype(BF)
            chunks(steps,body)
    stream(pi,cut[4],M1,F+B+M0,raise_)
    def lower(i,slot):
        x3_ref[:,here(i)]=x2_ref[:,here(i)]+nn(cact_ref[...],wa(slot))
        @pl.when(i==M2-1)
        def _():
            def body(r):
                xhat,_r=stats(x3_ref[r,:])
                hid4_ref[r,:]=(xhat*row(Rows.gain+4)+row(Rows.shift+4)).astype(BF)
            chunks(steps,body)
            acc_ref[...]=jnp.zeros_like(acc_ref)
    stream(po,cut[5],M2,F+B+M0+M1,lower)
    ticks()
    tau=F+B+M0+M1+M2
    after(cut[1]-1,ai,F); after(cut[3]-1,ao,F+B); after(cut[4]-1,pi,F+B+M0); after(cut[5]-1,po,F+B+M0+M1)
    @pl.when(j==cut[6]-1)
    def _():
        comm.run(comm.ticks-1,1)
        column(fi1,0,tau%2).start(); band(fo1,0,0).start()
    @pl.when(j>=cut[6])
    def _(): feed_tile(j-cut[6],tau+j-cut[6],1,hid4_ref,act1_ref,dsl1_ref,fi1,fo1)
    @pl.when(j==cut[7]-1)
    def _():
        s5_ref[...]=jnp.zeros_like(s5_ref)
        def body(r):
            y=x3_ref[r,:]+0.5*(acc_ref[r,:]+row(Rows.outer+1))
            xhat,rstd=stats(y)
            ok=valid_ref[r,0:1]
            gain=row(Rows.gain+5)
            res_ref[r,:]=((xhat*gain+row(Rows.shift+5))*ok).astype(BF)
            dy=cot_ref[r,:].astype(F32)*ok
            dx4_ref[r,:]=norm_back(dy,gain,xhat,rstd)
            s5_ref[0]+=fold(dy*xhat)
            s5_ref[1]+=fold(dy)
        chunks(steps,body)

LAG=2; CUTS=[1,8,8,6,2,4,2,8,8]; MODES=['h','qhhqhhqh','hqhhqhhq','hhqhhq','hh','qhhq','hh','qhhqhhqh','hqhhqhhq']
def early(S,vectors,tokens,cot,valid,mask,table,pick,heads,weights,cid):
    steps,width=tokens.shape; tile=512; taps=vectors[-1].shape[0]; L=vectors[0].shape[1]
    comm=Gather(S,[(Rows.count,L)]+weights,cuts=CUTS,modes=MODES,lag=LAG)
    hidden=comm.shapes[1][1]; size=width//heads
    F,B,A=hidden//tile,comm.shapes[3][1]//tile,width//128
    M=[comm.shapes[i][1]//tile for i in (4,5,6)]
    assert comm.shapes[2][0]*S==hidden and tile==hidden//S
    cut=np.cumsum([0,F,B,A]+M+[F]).tolist()
    within=lambda lo,n:(lambda j:jnp.minimum(jnp.maximum(j-lo,0),n-1))
    f0,at,f1=within(0,F),within(cut[2],A),within(cut[6],F)
    ins=list(vectors)+[tokens,cot,valid,mask,table,pick]
    D=jax.ShapeDtypeStruct
    b=D((steps,width),BF); f=D((steps,width),F32); hid=D((steps,hidden),BF)
    outs=[b,hid,hid,f,b,D((steps,3*width),BF),b,D((heads,steps,steps),BF),f,b,D((steps,2*width),BF),f,b,f,b,hid,hid,f,b,D((2,8,width),F32),D((Rows.count,width),F32)]
    specs=[whole(o.shape) for o in outs]
    for i,t in ((1,f0),(2,f0),(15,f1),(16,f1)): specs[i]=pl.BlockSpec((steps,tile),lambda j,t=t:(0,t(j)))
    specs[7]=pl.BlockSpec((128//size,steps,steps),lambda j:(at(j),0,0))
    V=pltpu.VMEM; sem=lambda n: pltpu.SemaphoreType.DMA((n,))
    scratch=[V((Rows.count,L),F32),V(comm.out_shapes[0].shape,BF),sem(1),V((steps,width),F32),V((2,)+comm.out_shapes[1].shape[:-1]+(tile,),BF),V((2,)+comm.out_shapes[2].shape[2:],BF),sem(2),sem(2),
        V((steps//QB,size,steps+QB),BF),V((3,steps,128),BF),V((steps+PAD,width),F32),V((steps,2*width),F32)]
    out=call(functools.partial(early_kernel,heads,taps),'gather_and_forward',(cut[-1],),ins,[whole(a.shape) for a in ins],outs,specs,scratch,comm,cid)
    return out[0],[a.reshape(-1,a.shape[-1]) for a in out[1]]


def local(S,R,tokens,lengths,cotangent,norm_gain,norm_shift,feed_in,feed_in_bias,feed_out,feed_out_bias,attention_in,attention_in_bias,attention_out,attention_out_bias,relative_table,pointwise_in,depthwise,pointwise_out):
    steps,width=tokens.shape; taps=depthwise.shape[0]
    live=jnp.arange(steps,dtype=jnp.int32)<lengths[0]
    valid=jnp.broadcast_to(live.astype(F32)[:,None],(steps,128))
    mask=jnp.broadcast_to(jnp.where(live,0.0,-1e30).astype(F32)[None,:],(8,steps))
    rows=relative_table.shape[0]
    table=jnp.pad(relative_table,((0,128-rows),(0,0)))
    pick=jnp.asarray(picker_table(steps,QB).astype(np.float32)).astype(BF)
    vectors=[norm_gain,norm_shift,feed_in_bias,feed_out_bias,attention_in_bias,attention_out_bias.reshape(1,-1),depthwise]
    weights=[(feed_in,0),(feed_out,0),attention_in,attention_out,pointwise_in,pointwise_out,(feed_in,1),(feed_out,1)]
    outs,full=early(S,vectors,tokens,cotangent,valid,mask,table,pick,HEADS,weights,0)
    hid0,act0,dsl0,x1,hid1,packed,mixed,p,x2,chid,up,depth,cact,x3,hid4,act1,dsl1,dx4,result,s5,vec=outs
    fi0,fo0,ai,ao,pi,po,fi1,fo1=full[1:]
    shapes=[feed_in.shape,feed_out.shape]+[a.shape for a in (attention_in,attention_out,pointwise_in,pointwise_out)]+[SUB]
    rest=[dx4,x3,x2,x1,hid4,hid1,hid0,chid,cact,mixed,up,depth,act1,act0,dsl1,dsl0,fi1,fo1,ai,ao,pi,po,fi0,fo0]
    (dtok,),outs=backward(S,packed,p,table,pick,HEADS,vec,valid,tokens,s5,rest,taps,shapes,1)
    sums=list(outs[:7])+[outs[-1]]
    if R>4:
        groups=[[g*4+i for g in range(R//4)] for i in range(4)]
        sums=[lax.psum(a,'rep',axis_index_groups=groups) for a in sums]
    gfi,gfo,gai,gao,gpi,gpo,small,common=[a.astype(F32) for a in sums]
    L=norm_gain.shape[1]
    ggain,gshift,gbout,gpbias,gmbias=[small[a:b,:L] for a,b in ((0,6),(6,12),(12,14),(14,16),(16,17))]
    gbin=small[17:19]; gdw=small[32:32+taps,:L]
    gtab=common.reshape(-1,SUB[1])[:rows,:relative_table.shape[1]]
    return (result,dtok,ggain,gshift,gfi,gbin,gfo,gbout,gai,gpbias,gao,gmbias[0],gtab,gpi,gdw,gpo)

HEADS=16

def solution(mesh):
    R,S=mesh.shape['rep'],mesh.shape['shard']
    rows=P(('rep','shard'),None)
    last,mid,first=P(None,'shard'),P(None,'shard',None),P('shard',None)
    weights=(last,last,mid,last,mid,last,first,last,first,P('shard'),P(),first,last,first)
    return jax.shard_map(functools.partial(local,S,R),mesh=mesh,in_specs=(rows,P(('rep','shard')),rows)+weights,out_specs=(rows,rows)+weights,check_vma=False)
```

```python
import functools, math
import numpy as np
import jax, jax.numpy as jnp
from jax import lax
from jax.experimental import pallas as pl
from jax.experimental.pallas import tpu as pltpu
from jax.sharding import PartitionSpec as P
LEFT=64; RIGHT=8
BF=jnp.bfloat16; F32=jnp.float32

def nn(a,b): return lax.dot_general(a,b,(((1,),(0,)),((),())),preferred_element_type=F32)
def nt(a,b): return lax.dot_general(a,b,(((1,),(1,)),((),())),preferred_element_type=F32)
def tn(a,b): return lax.dot_general(a,b,(((0,),(0,)),((),())),preferred_element_type=F32)

def picker_table(steps, block):
    span=steps+block
    n=np.arange(span)
    rows=[]
    for i in range(steps//block):
        off=np.where(n<steps, n, n-span)-block*i
        row=np.clip(off,-LEFT,RIGHT)+LEFT
        rows.append(np.arange(128)[:,None]==row[None,:])
    return np.stack(rows)

QB=128

MESH=pl.DeviceIdType.MESH
def al(v,m): return pl.multiple_of(v,m)
def during(lo,hi,body):
    def run(i,c):
        body(i); return c
    lax.fori_loop(lo,hi,run,0)

class Place:
    def __init__(self,S):
        self.S=S; self.Z=S//2
        r=lax.axis_index('rep'); s=lax.axis_index('shard')
        self.r,self.s=r,s
        self.c=lax.rem(r,2); self.x=lax.rem(r//2,2); self.y=lax.rem(s,2); self.z=s//2
        base=r-2*self.x-self.c
        self.d=1-2*self.c
        self.next=(r,2*self.zat(1)+self.y); self.prev=(r,2*self.zat(-1)+self.y)
        self.over_y=(r,2*self.z+1-self.y); self.over_x=(base+2*(1-self.x)+self.c,s); self.twin=(base+2*self.x+1-self.c,s)
    def zat(self,k): return lax.rem(self.z+self.d*k+2*self.Z,self.Z)
    def greet(self):
        bar=pltpu.get_barrier_semaphore()
        for dev in (self.next,self.prev,self.over_y,self.over_x,self.twin):
            pl.semaphore_signal(bar,inc=1,device_id=dev,device_id_type=MESH)
        pl.semaphore_wait(bar,5)

SUB=(128,512)
class Scatter:
    OWN=16; RING=8; GAP=2
    def __init__(self,S,counts,places,out_shapes,common=None,pause=None):
        self.places=places; self.counts=counts
        self.common=common
        self.S=S; Z=S//2
        n=self.n=sum(counts)
        (rows,wide)=SUB
        h,q=rows//2,rows//4
        self.h,self.q,self.Z=h,q,Z
        self.at=np.cumsum([0]+counts).tolist()
        self.inputs=[]
        self.finals=len(out_shapes)
        self.out_shapes=[jax.ShapeDtypeStruct(a,BF) for a in out_shapes]+[jax.ShapeDtypeStruct((n,Z,2,2,h,wide),BF)]
        G=self.GAP
        self.lag=[0]+[G*k for k in range(1,5+Z)]
        self.lag[4+Z]=self.lag[3+Z]+1
        self.lag.append(self.lag[4+Z]+1)
        self.gate,self.wait=pause or (n,0)
        self.ticks=n+self.wait+self.lag[-1]
        own,ring=min(n,self.OWN),min(n,self.RING)
        self.slots=own; self.ring=ring
        assert own>=self.lag[-1] and (self.wait==0 or n+self.wait<2*(self.gate+self.wait))
        V=lambda *d: pltpu.VMEM(d,BF)
        self.scratch=[V(n,rows,wide),V(own,Z,2,h,wide),V(ring,Z,2,h,wide),V(ring,Z,q,wide),V(ring,Z,q,wide),V(ring,Z-1,h,wide),V(ring,h,wide),
            pltpu.SemaphoreType.DMA((n,)),pltpu.SemaphoreType.DMA((n,5+Z)),pltpu.SemaphoreType.DMA((n,5+Z)),pltpu.SemaphoreType.DMA((n,2)),pltpu.SemaphoreType.REGULAR((4+Z,))]
        if common:
            self.out_shapes.append(jax.ShapeDtypeStruct((Z,2,common[2],wide),BF))
            self.scratch+=[V(Z,2,common[2],wide),pltpu.SemaphoreType.DMA((Z,)),pltpu.SemaphoreType.DMA((Z,)),pltpu.SemaphoreType.DMA((1,))]
            self.begin_common=common[0]+self.wait+self.lag[-1]+1
            self.ticks=max(self.ticks,self.begin_common+Z+1)
        self.out_specs=[pl.BlockSpec(memory_space=pl.ANY)]*len(self.out_shapes)
    def bind(self,ins,outs,scr):
        self.out=outs[:self.finals]; self.made=outs[self.finals]
        if self.common: self.all,self.cs,self.ct,self.co=scr[-4:]; self.all_out=outs[-1]; scr=scr[:-4]
        self.o,self.own,self.cr,self.xr,self.yr,self.zr,self.fr,self.os,self.ss,self.rs,self.ls,self.free=scr
        self.p=Place(self.S); return self
    def slot(self,i): return i if self.slots==self.n else lax.rem(i,self.slots)
    def land(self,i): return i if self.ring==self.n else lax.rem(i,self.ring)
    def remote(self,i,k,src,dst,dev):
        return pltpu.make_async_remote_copy(src,dst,self.ss.at[i,k],self.rs.at[i,k],device_id=dev,device_id_type=MESH)
    def first(self,i):
        return self.remote(i,0,self.made.at[i,:,:,1-self.p.c],self.cr.at[self.land(i)],self.p.twin)
    def load(self,i):
        return pltpu.make_async_copy(self.made.at[i,:,:,self.p.c],self.own.at[self.slot(i)],self.ls.at[i,0])
    def part(self,i,col,x): return self.own.at[self.slot(i),:,col,pl.ds(al(x*self.q,self.q),self.q)]
    def cross(self,i): return self.remote(i,2,self.part(i,1-self.p.y,1-self.p.x),self.xr.at[self.land(i)],self.p.over_x)
    def side(self,i): return self.remote(i,3,self.part(i,1-self.p.y,self.p.x),self.yr.at[self.land(i)],self.p.over_y)
    def hop(self,i,s): return self.remote(i,3+s,self.own.at[self.slot(i),self.p.zat(-s),self.p.y],self.zr.at[self.land(i),s-1],self.p.next)
    def swap(self,i): return self.remote(i,3+self.Z,self.own.at[self.slot(i),self.p.z,self.p.y],self.fr.at[self.land(i)],self.p.over_x)
    def half(self,i): return self.o.at[i,pl.ds(al(self.p.c*self.h,self.h),self.h)]
    def share(self,i): return self.remote(i,4+self.Z,self.half(i),self.half(i),self.p.twin)
    def save(self,i,place,unit):
        index,layer,across=place; rows,wide=SUB
        ref=self.out[index] if layer is None else self.out[index].at[layer]
        return pltpu.make_async_copy(self.o.at[i],ref.at[pl.ds(al(unit//across*rows,rows),rows),pl.ds(al(lax.rem(unit,across)*wide,wide),wide)],self.os.at[i])
    def ask(self,i,k):
        if self.ring<self.n:
            @pl.when(i>=self.ring)
            def _(): pl.semaphore_wait(self.free.at[k],1)
    def tell(self,i,k,dev):
        if self.ring<self.n:
            @pl.when(i<self.n-self.ring)
            def _(): pl.semaphore_signal(self.free.at[k],inc=1,device_id=dev,device_id_type=MESH)
    def begin(self): self.p.greet()
    def phase(self,k,i):
        p=self.p; Z=self.Z; here=self.slot(i); land=self.land(i)
        if k==0:
            self.first(i).start(); self.load(i).start()
        elif k==1:
            self.load(i).wait(); self.first(i).wait_recv()
            for col in (1-p.y,p.y):
                self.own[here,:,col]=self.own[here,:,col]+self.cr[land,:,col]
                if col is not p.y: self.cross(i).start()
        elif k==2:
            self.cross(i).wait_recv()
            ref=self.part(i,1-p.y,p.x); ref[...]=ref[...]+self.xr[land]
            self.side(i).start()
        elif k==3:
            self.side(i).wait_recv()
            ref=self.part(i,p.y,p.x); ref[...]=ref[...]+self.yr[land]
            self.ask(i,3); self.hop(i,1).start()
        elif k<3+Z:
            s=k-3
            self.hop(i,s).wait_recv()
            ref=self.own.at[here,p.zat(-1-s),p.y]; ref[...]=ref[...]+self.zr[land,s-1]
            self.tell(i,2+s,p.prev)
            if s+1<Z: self.ask(i,3+s); self.hop(i,s+1).start()
            else: self.swap(i).start()
        elif k==3+Z:
            self.swap(i).wait_recv()
            ref=self.half(i); ref[...]=self.own[here,p.z,p.y]+self.fr[land]
            self.share(i).start()
        elif k==4+Z:
            self.first(i).wait_send()
            self.cross(i).wait_send(); self.side(i).wait_send()
            for s in range(1,Z): self.hop(i,s).wait_send()
            self.swap(i).wait_send(); self.share(i).wait()
            for at,count,place in zip(self.at,self.counts,self.places):
                @pl.when((i>=at)&(i<at+count))
                def _(at=at,place=place): self.save(i,place,i-at).start()
        else: self.save(i,self.places[0],0).wait()
    def relay(self,s):
        p=self.p
        ref=self.all.at[p.z,p.y] if s==0 else self.all.at[p.zat(1-s)]
        return pltpu.make_async_remote_copy(ref,ref,self.cs.at[s],self.ct.at[s],device_id=p.over_y if s==0 else p.next,device_id_type=MESH)
    def spread_common(self,k):
        p=self.p; unit,at,count=self.common
        if k==0: self.all[p.z,p.y]=self.o[unit,at:at+count]
        else: self.relay(k-1).wait()
        if k<self.Z: self.relay(k).start()
        else:
            cp=pltpu.make_async_copy(self.all,self.all_out,self.co.at[0]); cp.start(); cp.wait()
    def run(self,lo,count):
        def tick(u):
            for k in reversed(range(len(self.lag))):
                v=u-self.lag[k]; turn=self.gate+self.wait
                inside=(v>=0)&(v<self.n+self.wait)
                @pl.when(inside&((v<self.gate)|(v>=turn)) if self.wait else inside)
                def _(k=k,v=v): self.phase(k,v-self.wait*(v//turn) if self.wait else v)
            if self.common:
                for k in range(self.Z+1):
                    @pl.when(u==self.begin_common+k)
                    def _(k=k): self.spread_common(k)
        during(0,count,lambda v:tick(lo+v))
    def spread(self,step,steps):
        per=-(-self.ticks//steps)
        self.run(step*per,per)

class Gather:
    def __init__(self,S,shards,cuts,modes,lag=2,ahead=1):
        self.S=S; Z=self.Z=S//2
        pick=lambda a: a if isinstance(a,tuple) else (a,None)
        self.local=[isinstance(a,tuple) and isinstance(a[0],int) for a in shards]
        pairs=[pick(a) for a,m in zip(shards,self.local) if not m]
        held=[]; self.source=[]
        for a,layer in pairs:
            k=next((k for k,v in enumerate(held) if v is a),None)
            if k is None: k=len(held); held.append(a)
            self.source.append((k,layer))
        fold_=lambda s: s[:-2]+(2,2,s[-2]//4,s[-1])
        self.inputs=[a.reshape(fold_(a.shape)) for a in held]
        self.shapes=[a if m else pick(a)[0].shape[-2:] for a,m in zip(shards,self.local)]
        self.cuts=cuts
        self.units=[(w,a) for w,k in enumerate(cuts) for a in range(k)]
        self.modes=''.join(modes)
        n=len(self.units); k=3*Z+1
        self.out_shapes=[jax.ShapeDtypeStruct((Z,2)+fold_(a),BF) for a in self.shapes]
        self.out_specs=[pl.BlockSpec(memory_space=pl.ANY)]*len(shards)
        self.scratch=[pltpu.VMEM(fold_(a),BF) for a,m in zip(self.shapes,self.local) if m]+[pltpu.SemaphoreType.DMA((n,k)),pltpu.SemaphoreType.DMA((n,k)),pltpu.SemaphoreType.DMA((n,))]
        self.plan={}
        for t in range(1,Z): self.plan[lag*t]=('z',t)
        self.plan[lag*Z]=('y',0); self.plan[lag*(Z+1)]=('x',0); self.plan[lag*(Z+2)]=('end',0)
        self.last=lag*(Z+2)
        self.ahead=ahead
        self.ticks=n+self.last
    def bind(self,ins,outs,scr):
        mine=list(scr[:-3]); source=list(self.source); self.i=[]
        for m in self.local:
            if m: self.i.append(mine.pop(0))
            else:
                k,layer=source.pop(0)
                self.i.append(ins[k] if layer is None else ins[k].at[layer])
        self.o=outs; self.ss,self.rs,self.ls=scr[-3:]; self.p=Place(self.S); return self
    def cp(self,u,kind,t=0):
        p=self.p; Z=self.Z; h=self.modes[u]=='h'; w,a=self.units[u]
        wide=self.shapes[w][1]//self.cuts[w]; cs=pl.ds(a*wide,wide); o=self.o[w]; i=self.i[w]
        k={'z':t-1,'y':Z-1+t,'u':2*Z-1+t-1,'x':3*Z-2,'a':3*Z-1,'b':3*Z}[kind]
        if kind=='z':
            zo=p.zat(1-t); dev=p.next
            dst=o.at[zo,p.y,p.c,:,:,cs] if h else o.at[zo,p.y,p.c,p.x,:,cs]; src=dst
            if t==1: src=i.at[p.c,:,:,cs] if h else i.at[p.c,p.x,:,cs]
        elif kind=='y':
            dst=src=o.at[p.zat(-t),p.y,p.c,p.x,:,cs]; dev=p.over_y
            if t==0: src=i.at[p.c,p.x,:,cs]
        elif kind=='u': src=dst=o.at[p.zat(-t),p.y,p.c,p.x,:,cs]; dev=p.over_x
        elif kind=='x': src=dst=o.at[:,1-p.y,p.c,p.x,:,cs]; dev=p.over_x
        else: src=dst=o.at[:,p.y if kind=='a' else 1-p.y,p.c,:,:,cs]; dev=p.twin
        return pltpu.make_async_remote_copy(src,dst,self.ss.at[u,k],self.rs.at[u,k],device_id=dev,device_id_type=MESH)
    def own(self,u):
        p=self.p; w,a=self.units[u]; wide=self.shapes[w][1]//self.cuts[w]; cs=pl.ds(a*wide,wide)
        return pltpu.make_async_copy(self.i[w].at[p.c,:,:,cs],self.o[w].at[p.z,p.y,p.c,:,:,cs],self.ls.at[u])
    def open(self,u):
        self.cp(u,'z',1).start(); self.cp(u,'y',0).start(); self.own(u).start()
    def begin(self):
        self.p.greet()
        for u in range(min(self.ahead,len(self.units))): self.open(u)
    def stage(self,u,kind,t):
        Z=self.Z; q=self.modes[u]=='q'
        if kind=='z':
            self.cp(u,'z',t).wait_recv()
            if t+1<Z: self.cp(u,'z',t+1).start()
            self.cp(u,'y',t).start()
            if q: self.cp(u,'u',t).start()
        elif kind=='y':
            for t in range(Z): self.cp(u,'y',t).wait_recv()
            self.cp(u,'x').start()
            self.own(u).wait()
            if not q: self.cp(u,'a').start()
        elif kind=='x':
            if q:
                for t in range(1,Z): self.cp(u,'u',t).wait_recv()
                self.cp(u,'a').start()
            self.cp(u,'x').wait_recv(); self.cp(u,'b').start()
        else:
            for t in range(1,Z):
                self.cp(u,'z',t).wait_send()
                if q: self.cp(u,'u',t).wait_send()
            for t in range(Z): self.cp(u,'y',t).wait_send()
            self.cp(u,'x').wait_send(); self.cp(u,'a').wait(); self.cp(u,'b').wait()
    def run(self,lo,count):
        n=len(self.units)
        for i in range(lo,min(lo+count,self.ticks)):
            if self.ahead<=i+self.ahead<n: self.open(i+self.ahead)
            for u in range(n):
                s=self.plan.get(i-u)
                if s: self.stage(u,*s)
    def done(self,w):
        return max(u for u,(a,_) in enumerate(self.units) if a==w)+self.last+1

VM=60<<20
def call(body,name,grid,ins,in_specs,outs,out_specs,scratch,side=None,cid=None):
    any_=pl.BlockSpec(memory_space=pl.ANY)
    extra=side.inputs if side else []
    a,b,c,d,e=len(ins),len(extra),len(outs),len(side.out_shapes) if side else 0,len(scratch)
    def kernel(*refs):
        comm=None
        cut=np.cumsum([0,a,b,c,d,e]).tolist()
        part=[refs[x:y] for x,y in zip(cut,cut[1:]+[len(refs)])]
        if side:
            comm=side.bind(part[1],part[3],part[5])
        body(comm,*part[0],*part[2],*part[4])
    out=pl.pallas_call(kernel,grid=grid,out_shape=list(outs)+(side.out_shapes if side else []),in_specs=list(in_specs)+[any_]*b,
        out_specs=list(out_specs)+(side.out_specs if side else []),scratch_shapes=list(scratch)+(side.scratch if side else []),
        compiler_params=pltpu.CompilerParams(vmem_limit_bytes=VM,**(dict(collective_id=cid,has_side_effects=True) if side else {})),name=name)(*ins,*extra)
    return out[:c],out[c:]


CH=64

def aside(body):
    def run(comm,*refs):
        if comm:
            @pl.when(pl.program_id(0)==0)
            def _(): comm.begin()
        body(*refs)
        if comm: comm.spread(pl.program_id(0),pl.num_programs(0))
    return run
def whole(shape):
    return pl.BlockSpec(shape,lambda *i:(0,)*len(shape),pipeline_mode=pl.Buffered(1))
def chunks(steps,body):
    def run(i,c):
        body(pl.ds(pl.multiple_of(i*CH,CH),CH)); return c
    lax.fori_loop(0,steps//CH,run,0)
def stats(v):
    center=v-jnp.mean(v,axis=-1,keepdims=True)
    rstd=lax.rsqrt(jnp.mean(center*center,axis=-1,keepdims=True)+1e-5)
    return center*rstd,rstd
def norm_back(dy,gain,xhat,rstd):
    g=dy*gain
    return rstd*(g-jnp.mean(g,axis=-1,keepdims=True)-xhat*jnp.mean(g*xhat,axis=-1,keepdims=True))
def sigmoid(v): return 0.5*jnp.tanh(0.5*v)+0.5
def fold(v): return jnp.sum(v.reshape(v.shape[0]//8,8,v.shape[1]),axis=0)

PAD=32
RC=128
def over_columns(width,body):
    def run(i,c):
        body(pl.ds(pl.multiple_of(i*128,128),128)); return c
    lax.fori_loop(0,width//128,run,0)
def taps_of(taps,lead,residue):
    return [(a,k) for k in range(taps) for a in [lead(k)//8] if lead(k)%8==residue]
def slide(pad_ref,w_ref,lead,taps,t0,cols):
    acc=jnp.zeros((RC,128),F32)
    for b in range(8):
        use=taps_of(taps,lead,b)
        if not use: continue
        top=max(a for a,_ in use)
        slab=pad_ref[t0+b:t0+b+RC+8*top,cols]
        for a,k in use: acc=acc+w_ref[k:k+1,cols]*slab[8*a:8*a+RC]
    return acc

VECTOR_ROWS=64
def plan_ticks(comm,phases,pace,limit):
    at=[]; done=0; spent=0.0
    for st,t in enumerate(phases):
        spent+=t
        target=max(done,min(int(spent/pace),limit(st),comm.ticks))
        at.append((done,target-done)); done=target
    return at

def backward_kernel(taps,size,comm,q_ref,k_ref,v_ref,p_ref,table_ref,pick_ref,vec_ref,valid_ref,tok_ref,s5_ref,
        dx4,x3,x2,x1,hid4,hid1,hid0,chid,cact,mixed,up,depth,act1,act0,dsl1,dsl0,fi1,fo1,ai,ao,pi,po,fi0,fo0,out_ref,
        d_ref,x_ref,acc_ref,low_ref,turn_ref,hid_ref,big_ref,stage_ref,ds_ref,grad_ref,wa_ref,wb_ref,wd_ref,pad_ref,tail_ref,rows_ref,sums_ref,ddw_ref,dbin_ref,psum_ref,dtab_ref,
        sem_d,sem_x,sem_hid,sem_big,sem_a,sem_b,sem_c,stage_sem):
    steps,width=d_ref.shape; wide=SUB[1]; S=comm.S; across=width//wide; CUT=act1.shape[1]//S
    F=act1.shape[1]//wide; A=width//128; B=ai.shape[1]//wide; M0,M1,M2=po.shape[1]//wide,pi.shape[1]//wide,ao.shape[1]//wide
    cut=np.cumsum([0,F,F,M0,1,M1,M2,A,B,F,F,1]).tolist()
    FB,FD,MP,MC,MI,MO,AT,PB,CB,CD,EN=cut[:11]
    units=np.cumsum([0,F,F,M0,M1,M2,B,F,1,F]).tolist()
    j=pl.program_id(0)
    made=[]; n=0
    for st in range(cut[-1]):
        n+=0 if MC<=st<MI or AT<=st<PB or st==EN else 1
        if st==CD: n+=1
        made.append(n)
    def limit(st):
        if AT<=st<PB: return comm.gate+comm.wait
        return made[st]-2+(comm.wait if st>=PB else 0)
    times=[2.9]*F+[1.0]*F+[3]*M0+[15]+[2.5]*(M1-1)+[5]+[3]*M2+[4.7]*A+[2.8]*B+[3.8]*F+[1.0]*F+[0]
    at=plan_ticks(comm,times,PACE,limit)
    def ticks(step,share=(0,1)):
        lo,n=at[step]; a,b=n*share[0]//share[1],n*(share[0]+1)//share[1]
        if b>a: comm.run(lo+a,b-a)
    def ticks_of(lo,hi):
        for st in range(lo,hi):
            if at[st][1]:
                @pl.when(j==st)
                def _(st=st): ticks(st)
    def phase(lo,hi):
        return pl.when((j>=lo)&(j<hi))
    def last(step): return pl.when(j==step)
    def fill(src,dst,sem): return pltpu.make_async_copy(src,dst,sem)
    def row(i): return vec_ref[i:i+1,:]
    def here(i): return pl.ds(al(i*wide,wide),wide)
    def column(w,i,slot): return fill(w.at[:,here(i)],wa_ref.at[slot],sem_a.at[slot])
    def band(w,i): return fill(w.at[here(i)],wb_ref.at[lax.rem(i,2)],sem_b.at[lax.rem(i,2)])
    def slope(w,i): return fill(w.at[:,here(i)],wd_ref.at[lax.rem(i,2)],sem_c.at[lax.rem(i,2)])
    def load(ref,dst,sem): return fill(ref,dst,sem.at[0])
    def lefts(act,a,slot):
        return [fill(act.at[:,pl.ds(al(s*CUT+a*SUB[0],SUB[0]),SUB[0])],big_ref.at[slot,:,pl.ds(s*SUB[0],SUB[0])],sem_big.at[slot,s]) for s in range(S)]
    def whole_big(src,slot): return fill(src,big_ref.at[slot],sem_big.at[slot,0])
    def put(q): return fill(stage_ref.at[lax.rem(q,2)],comm.made.at[q],stage_sem.at[lax.rem(q,2)])
    first_late=units[5]
    def unit(q,value):
        @pl.when((q>=2)&((q<first_late)|(q>=first_late+2)))
        def _(): put(q-2).wait()
        stage_ref[lax.rem(q,2)]=value.reshape(stage_ref.shape[1:])
        put(q).start()
    def stream(w,lo,n,tau0,use):
        @phase(lo,lo+n)
        def _():
            i=j-lo; slot=lax.rem(tau0+i,2)
            column(w,i,slot).wait()
            @pl.when(i+1<n)
            def _(): column(w,i+1,lax.rem(tau0+i+1,2)).start()
            use(i,wa_ref.at[slot])
    def ahead(w,tau): column(w,0,tau%2).start()
    tau=np.cumsum([0,F,M0,M1,M2,B]).tolist()

    def feed_step(i,w_out,slopes,q,side,fi):
        band(w_out,i).wait(); slope(slopes,i).wait()
        @pl.when(i+1<F)
        def _(): band(w_out,i+1).start(); slope(slopes,i+1).start()
        s=lax.rem(i,2)
        dpre=(nt(low_ref[:,:width],wb_ref[s])*wd_ref[s].astype(F32)).astype(BF)
        dbin_ref[side,:,here(i)]=fold(dpre.astype(F32))
        acc_ref[...]+=nt(dpre,fi[...])
        unit(q+i,nn(turn_ref[...],dpre).astype(BF))
    def norm_step(source,i,at_,after):
        def body(r):
            xhat,rstd=stats(source[r,:].astype(F32))
            dy=acc_ref[r,:]
            sums_ref[at_]+=fold(dy*xhat); sums_ref[at_+1]+=fold(dy)
            after(r,d_ref[r,:]+norm_back(dy,row(Rows.gain+i),xhat,rstd))
        chunks(steps,body)
    def out_units(act,lo,q):
        @phase(lo,lo+F)
        def _():
            d=j-lo; a=d//across
            for slot in range(3):
                @pl.when((lax.rem(a,3)==slot)&(lax.rem(d,across)==0))
                def _(slot=slot):
                    for cp in lefts(act,a,slot): cp.wait()
            unit(q+d,tn(big_ref[lax.rem(a,3)],low_ref[:,here(lax.rem(d,across))]).astype(BF))
            @pl.when(d==across-1)
            def _():
                for a in range(3,F//across):
                    for cp in lefts(act,a,a-3): cp.start()
    def start_feed(act,fo,slopes):
        for a in range(3):
            for cp in lefts(act,a,a): cp.start()
        band(fo,0).start(); slope(slopes,0).start()

    @last(0)
    def _():
        comm.begin()
        load(dx4,d_ref,sem_d).start(); load(hid4,hid_ref,sem_hid).start(); load(x3,x_ref,sem_x).start()
        ahead(fi1,0); start_feed(act1,fo1,dsl1)
        sums_ref[...]=jnp.zeros_like(sums_ref)
        dtab_ref[...]=jnp.zeros_like(dtab_ref)
        acc_ref[...]=jnp.zeros_like(acc_ref)
        tail_ref[steps:steps+PAD,:]=jnp.zeros((PAD,width),F32)
        pad_ref[0:PAD,:]=jnp.zeros((PAD,width),F32)
        load(dx4,d_ref,sem_d).wait()
        def body(r):
            df=(0.5*d_ref[r,:]).astype(BF)
            low_ref[r,:width]=df
            sums_ref[12]+=fold(df.astype(F32))
        chunks(steps,body)
        load(hid4,hid_ref,sem_hid).wait()
        turn_ref[...]=hid_ref[...].T
        load(chid,hid_ref,sem_hid).start()
    stream(fi1,FB,F,tau[0],lambda i,w: feed_step(i,fo1,dsl1,units[0],0,w))
    @last(FD-1)
    def _():
        load(x3,x_ref,sem_x).wait()
        def after(r,v): d_ref[r,:]=v
        norm_step(x_ref,4,8,after)
        load(depth,x_ref,sem_x).start()
        ahead(po,tau[1])
    out_units(act1,FD,units[1])
    @last(MP-1)
    def _():
        whole_big(up.at[:,:width],0).start(); whole_big(up.at[:,width:],1).start(); whole_big(cact,2).start()
        def body(r): low_ref[r,:width]=d_ref[r,:].astype(BF)
        chunks(steps,body)
        acc_ref[...]=jnp.zeros_like(acc_ref)
    def lower(i,w):
        @pl.when(i==0)
        def _(): whole_big(cact,2).wait()
        acc_ref[...]+=nt(low_ref[:,here(i)],w[...])
        unit(units[2]+i,tn(big_ref[2],low_ref[:,here(i)]).astype(BF))
        @pl.when(i==M0-1)
        def _(): ahead(pi,tau[2])
    stream(po,MP,M0,tau[1],lower)
    @last(MC)
    def _():
        weights=vec_ref.at[Rows.taps:Rows.taps+32]
        load(depth,x_ref,sem_x).wait(); whole_big(cact,0).wait(); whole_big(cact,1).wait()
        def three(i,c):
            r=pl.ds(pl.multiple_of(i*CH,CH),CH)
            xhat,rstd=stats(x_ref[r,:])
            gain=row(Rows.gain+3)
            z=xhat*gain+row(Rows.shift+3)
            sg=sigmoid(z)
            dz=acc_ref[r,:]*(sg*(1.0+z*(1.0-sg)))
            sums_ref[6]+=fold(dz*xhat); sums_ref[7]+=fold(dz)
            tail_ref[r,:]=norm_back(dz,gain,xhat,rstd)
            pad_ref[pl.ds(pl.multiple_of(i*CH+PAD,PAD),CH),:]=big_ref[0,r,:].astype(F32)*sigmoid(big_ref[1,r,:].astype(F32))*valid_ref[r,0:1]
            return c
        lax.fori_loop(0,steps//CH,three,0)
        load(x2,x_ref,sem_x).start()
        ticks(MC,(0,3))
        def conv(cols):
            for t0 in range(0,steps,RC):
                acc_ref[t0:t0+RC,cols]=slide(tail_ref,weights,lambda k:taps-1-k,taps,t0,cols)
        over_columns(width,conv)
        ticks(MC,(1,3))
        def gate(r):
            a=big_ref[0,r,:].astype(F32); sg=sigmoid(big_ref[1,r,:].astype(F32))
            dg=acc_ref[r,:]*valid_ref[r,0:1]*sg
            low_ref[r,:width]=dg.astype(BF)
            low_ref[r,width:]=(dg*a*(1.0-sg)).astype(BF)
        chunks(steps,gate)
        acc_ref[...]=jnp.zeros_like(acc_ref)
        ticks(MC,(2,3))
    def raised(i,w):
        @pl.when(i==0)
        def _(): load(chid,hid_ref,sem_hid).wait()
        acc_ref[...]+=nt(low_ref[:,here(i)],w[...])
        unit(units[3]+i,tn(hid_ref[...],low_ref[:,here(i)]).astype(BF))
        @pl.when(i==M1-1)
        def _():
            load(mixed,hid_ref,sem_hid).start()
            ahead(ao,tau[3])
            load(x2,x_ref,sem_x).wait()
            def after(r,v):
                d_ref[r,:]=v
                da=v.astype(BF)
                low_ref[r,:width]=da
                sums_ref[13]+=fold(da.astype(F32))
            norm_step(x_ref,2,4,after)
            load(x1,x_ref,sem_x).start()
            acc_ref[...]=jnp.zeros_like(acc_ref)
    stream(pi,MI,M1,tau[2],raised)
    def joined(i,w):
        @pl.when(i==0)
        def _(): load(mixed,hid_ref,sem_hid).wait()
        acc_ref[...]+=nt(low_ref[:,here(i)],w[...])
        unit(units[4]+i,tn(hid_ref[...],low_ref[:,here(i)]).astype(BF))
        @pl.when(i==M2-1)
        def _():
            load(hid1,hid_ref,sem_hid).start()
            ahead(ai,tau[4])
            low_ref[:,width:]=acc_ref[...].astype(BF)
            acc_ref[...]=jnp.zeros_like(acc_ref)
    stream(ao,MO,M2,tau[3],joined)
    ticks_of(FB,MC); ticks_of(MI,AT)
    @last(AT)
    def _():
        for q in (first_late-2,first_late-1): put(q).wait()
    lo_at=at[AT][0]
    @phase(AT,PB)
    def _():
        h=j-AT
        mine=pl.ds(al(h*128,128),128)
        grad_ref[...]=low_ref[:,pl.ds(al(width+h*128,128),128)]
        parts=heads_back(q_ref,k_ref,v_ref,p_ref,grad_ref,table_ref,pick_ref,dtab_ref,ds_ref,size)
        for part in range(3): big_ref[part,:,mine]=parts[part]
        psum_ref[0:1,mine]=jnp.sum(big_ref[0,:,mine].astype(F32),axis=0,keepdims=True)
        psum_ref[1:2,mine]=jnp.sum(big_ref[2,:,mine].astype(F32),axis=0,keepdims=True)
        comm.run(lo_at+h*ATICKS,ATICKS)
    start=lo_at+ATICKS*A
    assert start<=comm.gate+comm.wait
    late=plan_ticks(comm,times[PB:],PACE2,lambda st: limit(PB+st)-start)
    for st in range(PB,EN): at[st]=(start+late[st-PB][0],late[st-PB][1])
    def packed_back(b,w):
        @pl.when(b==0)
        def _():
            load(hid1,hid_ref,sem_hid).wait()
            turn_ref[...]=hid_ref[...].T
            load(hid0,hid_ref,sem_hid).start()
        g=big_ref[b//across,:,here(lax.rem(b,across))]
        acc_ref[...]+=nt(g,w[...])
        unit(units[5]+b,nn(turn_ref[...],g).astype(BF))
        @pl.when(b==B-1)
        def _():
            ahead(fi0,tau[5]); start_feed(act0,fo0,dsl0)
            load(x1,x_ref,sem_x).wait(); load(hid0,hid_ref,sem_hid).wait()
            turn_ref[...]=hid_ref[...].T
            def after(r,v):
                d_ref[r,:]=v
                df=(0.5*v).astype(BF)
                low_ref[r,:width]=df
                sums_ref[11]+=fold(df.astype(F32))
            norm_step(x_ref,1,2,after)
            acc_ref[...]=jnp.zeros_like(acc_ref)
    stream(ai,PB,B,tau[4],packed_back)
    stream(fi0,CB,F,tau[5],lambda i,w: feed_step(i,fo0,dsl0,units[6],1,w))
    @phase(CB,CD)
    def _():
        def conv_weights(cols):
            lead=lambda k:k+PAD-taps+1
            for b in range(8):
                use=taps_of(taps,lead,b)
                if not use: continue
                top=max(a for a,_ in use)
                parts={k:jnp.zeros((8,128),F32) for _,k in use}
                for t0 in range(0,steps,RC):
                    slab=pad_ref[t0+b:t0+b+RC+8*top,cols]
                    dd=tail_ref[t0:t0+RC,cols]
                    for a,k in use: parts[k]=parts[k]+fold(slab[8*a:8*a+RC]*dd)
                for k,v in parts.items(): ddw_ref[k:k+1,cols]=jnp.sum(v,axis=0,keepdims=True)
        for a in range(A//F): conv_weights(pl.ds(al((j-CB)*(A//F)*128+a*128,128),128))
    @last(CD-1)
    def _():
        def after(r,v): out_ref[r,:]=v.astype(BF)
        norm_step(tok_ref,0,0,after)
        rows_ref[...]=jnp.zeros_like(rows_ref)
        total=lambda v: jnp.sum(v,axis=0,keepdims=True)
        rows=[sums_ref[0],sums_ref[2],sums_ref[4],sums_ref[6],sums_ref[8],s5_ref[0],sums_ref[1],sums_ref[3],sums_ref[5],sums_ref[7],sums_ref[9],s5_ref[1],sums_ref[11],sums_ref[12]]
        rows=[total(v) for v in rows]+[psum_ref[0:1,:],psum_ref[1:2,:],total(sums_ref[13])]
        L=width//S
        for i,v in enumerate(rows):
            for s in range(S): rows_ref[s,i:i+1,0:L]=v[:,s*L:s*L+L]
        k=len(rows)
        for i in range(2):
            v=total(dbin_ref[1-i])
            for s in range(S): rows_ref[s,k+i:k+i+1,:]=v[:,s*wide:s*wide+wide]
        n=dtab_ref.shape[0]//S
        for s in range(S):
            rows_ref[s,32:32+taps,0:L]=ddw_ref[0:taps,s*L:s*L+L]
            rows_ref[s,VECTOR_ROWS:VECTOR_ROWS+n,0:size]=dtab_ref[s*n:s*n+n,:]
    @last(CD)
    def _(): unit(units[7],rows_ref[...].astype(BF).reshape(S*SUB[0],wide))
    out_units(act0,CD,units[8])
    ticks_of(PB,EN)
    @last(EN)
    def _():
        for q in (units[9]-2,units[9]-1): put(q).wait()
        lo=sum(at[EN-1])
        comm.run(lo,comm.ticks-lo)

def heads_back(q_ref,k_ref,v_ref,p_ref,g_ref,table_ref,pick_ref,dtab_ref,ds_ref,size):
    steps=q_ref.shape[0]; nb=steps//QB; span=steps+QB
    scale=1.0/math.sqrt(size)
    flip=(lax.broadcasted_iota(jnp.int32,(QB,QB),0)+lax.broadcasted_iota(jnp.int32,(QB,QB),1)==QB-1).astype(F32).astype(BF)
    sl=[slice(i*QB,(i+1)*QB) for i in range(nb)]
    out=[]
    for hh in range(q_ref.shape[1]//size):
        cols=slice(hh*size,(hh+1)*size)
        dss=[]
        for r in sl:
            p=p_ref[hh,r,:].astype(F32)
            t=p*nt(g_ref[r,cols],v_ref[:,cols])
            dss.append((t-p*jnp.sum(t,axis=1,keepdims=True)).astype(BF))
        for r,ds in zip(sl,dss): ds_ref[r,:]=ds
        xs=[nn(flip,ds) for ds in dss]
        xs=[pltpu.roll(jnp.concatenate([x,jnp.zeros((QB,QB),F32)],axis=1),span-QB+1,1,stride=1,stride_axis=0).astype(BF) for x in xs]
        xs=[(nt(x,pick_ref[i])*scale).astype(BF) for i,x in enumerate(xs)]
        drel=jnp.concatenate([nn(flip,x).astype(BF) for x in xs],axis=0)
        dq=(nn(ds_ref[...],k_ref[:,cols])*scale+nn(drel,table_ref[...])).astype(BF)
        dtab_ref[...]+=tn(drel,q_ref[:,cols])
        out.append((dq,(tn(ds_ref[...],q_ref[:,cols])*scale).astype(BF),tn(p_ref[hh],g_ref[:,cols]).astype(BF)))
    return [jnp.concatenate([a[part] for a in out],axis=1) for part in range(3)]

PACE=4.5; PAUSE=0; PACE2=3.3; ATICKS=1
def backward(S,packed,p,table,pick,heads,vec,valid,tokens,s5,rest,taps,out_shapes,cid):
    steps,width=tokens.shape; size=width//heads; wide=SUB[1]; across=width//wide
    act1,ai,ao,pi,po=rest[12],rest[18],rest[19],rest[20],rest[21]
    hidden=act1.shape[1]; F=hidden//wide; A=width//128; B=ai.shape[1]//wide; M0,M1,M2=[a.shape[1]//wide for a in (po,pi,ao)]
    assert hidden//S==wide and width//S==SUB[0] and wide//SUB[0]<=4 and A%F==0
    counts=[F,F,M0,M1,M2,B,F,1,F]
    places=[(0,1,F),(1,1,across),(5,None,across),(4,None,2*across),(3,None,across),(2,None,3*across),(0,0,F),(6,None,1),(1,0,across)]
    comm=Scatter(S,counts,places,out_shapes,common=(sum(counts[:7]),VECTOR_ROWS,table.shape[0]//S),pause=(sum(counts[:5]),PAUSE))
    start=2*F+M0+1+M1+M2
    head=lambda o:pl.BlockSpec((steps,128),lambda j:(0,o*A+jnp.minimum(jnp.maximum(j-start,0),A-1)))
    ins=[packed,packed,packed,p,table,pick,vec,valid,tokens,s5]
    specs=[head(0),head(1),head(2),pl.BlockSpec((128//size,steps,steps),lambda j:(jnp.minimum(jnp.maximum(j-start,0),A-1),0,0))]+[whole(a.shape) for a in ins[4:]]
    specs+=[pl.BlockSpec(memory_space=pl.ANY)]*len(rest)
    V=pltpu.VMEM; Z=S//2; sem=lambda *n: pltpu.SemaphoreType.DMA(n)
    sq=lambda t: V((steps,width),t)
    scratch=[sq(F32),sq(F32),sq(F32),V((steps,2*width),BF),V((width,steps),BF),sq(BF),V((3,steps,width),BF),V((2,Z,2,2,SUB[0]//2,wide),BF),V((steps,steps),BF),V((steps,128),BF),
        V((2,width,wide),BF),V((2,wide,width),BF),V((2,steps,wide),BF),V((steps+PAD,width),F32),V((steps+PAD,width),F32),V((S,)+SUB,F32),V((14,8,width),F32),V((32,width),F32),V((2,8,hidden),F32),V((8,width),F32),V((128,size),F32),
        sem(1),sem(1),sem(1),sem(3,S),sem(2),sem(2),sem(2),sem(2)]
    return call(functools.partial(backward_kernel,taps,size),'backward_and_sums',(start+A+B+2*F+1,),ins+list(rest),specs,[jax.ShapeDtypeStruct((steps,width),BF)],[whole((steps,width))],scratch,comm,cid)

class Rows:
    gain=0; shift=8; inner=16; outer=24; packed=26; mixed=28; taps=32; count=64

def early_kernel(heads,taps,comm,gain_in,shift_in,inner_in,outer_in,packed_in,mixed_in,taps_in,tok_ref,cot_ref,valid_ref,mask_ref,table_ref,pick_ref,
        hid0_ref,act0_ref,dsl0_ref,x1_ref,hid1_ref,packed_ref,mixed_ref,p_ref,x2_ref,chid_ref,up_ref,depth_ref,cact_ref,x3_ref,hid4_ref,act1_ref,dsl1_ref,dx4_ref,res_ref,s5_ref,vec_ref,
        own_ref,land_ref,land_sem,acc_ref,wa_ref,wb_ref,sem_a,sem_b,rel_ref,qkv_ref,pad_ref,wide_ref):
    steps,width=tok_ref.shape; tile=wa_ref.shape[-1]; S=comm.S
    small,fi0,fo0,ai,ao,pi,po,fi1,fo1=comm.o
    F,B,M0,M1,M2=[w.shape[-1]//tile for w in (fi0,ai,ao,pi,po)]; A=width//128
    size=width//heads
    cut=np.cumsum([0,F,B,A,M0,M1,M2,F]).tolist()
    j=pl.program_id(0)
    L=width//S
    def row(i): return vec_ref[i:i+1,:]
    def column(w,i,slot): return pltpu.make_async_copy(w.at[:,:,:,:,:,pl.ds(al(i*tile,tile),tile)],wa_ref.at[slot],sem_a.at[slot])
    def band(w,i,slot): return pltpu.make_async_copy(w.at[i//2,lax.rem(i,2)],wb_ref.at[slot],sem_b.at[slot])
    def wa(slot): return wa_ref[slot].reshape(width,tile)
    want=[comm.done(2),comm.done(3),comm.done(4),comm.done(5),comm.done(6),comm.done(8)]
    at={}; done=want[0]
    times=[20/F]*F+[10/B]*B+[26/A]*A+[3]*M0+[2]*(M1-1)+[14]+[3]*M2
    need={cut[1]-1:want[1],cut[3]-1:want[2],cut[4]-1:want[3],cut[5]-1:want[4],cut[6]-1:comm.ticks-1}
    for st in range(cut[6]):
        target=want[0]+int((comm.ticks-1-want[0])*sum(times[:st+1])/sum(times))
        target=max(target,need.get(st,0))
        if target>done: at[st]=(done,target-done); done=target
    def ticks():
        for st,(lo,n) in at.items():
            @pl.when(j==st)
            def _(lo=lo,n=n): comm.run(lo,n)
    @pl.when(j==0)
    def _():
        own_ref[...]=jnp.zeros_like(own_ref)
        for at_,ref in ((Rows.gain,gain_in),(Rows.shift,shift_in),(Rows.outer,outer_in),(Rows.packed,packed_in),(Rows.mixed,mixed_in),(Rows.taps,taps_in)):
            own_ref[at_:at_+ref.shape[0],:]=ref[...].astype(F32)
        k=inner_in.shape[1]//L
        for l in range(2):
            for i in range(k): own_ref[Rows.inner+l*k+i:Rows.inner+l*k+i+1,:]=inner_in[l:l+1,i*L:i*L+L].astype(F32)
        comm.i[0][...]=own_ref[...].astype(BF).reshape(comm.i[0].shape)
        comm.begin()
        comm.run(0,want[0])
        cp=pltpu.make_async_copy(small,land_ref,land_sem.at[0]); cp.start()
        column(fi0,0,0).start(); band(fo0,0,0).start()
        cp.wait()
        for s in range(S): vec_ref[:,s*L:s*L+L]=land_ref[s//2,s%2].reshape(Rows.count,L).astype(F32)
        for i in range(steps//QB): rel_ref[i]=tn(table_ref[...],pick_ref[i]).astype(BF)
        def body(r):
            xhat,_r=stats(tok_ref[r,:].astype(F32))
            hid0_ref[r,:]=(xhat*row(Rows.gain)+row(Rows.shift)).astype(BF)
        chunks(steps,body)
        acc_ref[...]=jnp.zeros_like(acc_ref)
        pad_ref[0:PAD,:]=jnp.zeros((PAD,width),F32)
    def feed_tile(i,tau,l,hid_ref,act_ref,dsl_ref,fi,fo):
        slot=lax.rem(tau,2); k=tile//L
        column(fi,i,slot).wait(); band(fo,i,lax.rem(i,2)).wait()
        @pl.when(i+1<F)
        def _(): column(fi,i+1,lax.rem(tau+1,2)).start(); band(fo,i+1,lax.rem(i+1,2)).start()
        bias=jnp.concatenate([vec_ref[Rows.inner+l*k+a:Rows.inner+l*k+a+1,pl.ds(al(i*L,L),L)] for a in range(k)],axis=1)
        pre=nn(hid_ref[...],wa(slot))+bias
        sg=sigmoid(pre)
        act_ref[...]=(pre*sg).astype(BF)
        dsl_ref[...]=(sg*(1.0+pre*(1.0-sg))).astype(BF)
        acc_ref[...]+=nn(act_ref[...],wb_ref[lax.rem(i,2)].reshape(tile,width))
    @pl.when(j<cut[1])
    def _(): feed_tile(j,j,0,hid0_ref,act0_ref,dsl0_ref,fi0,fo0)
    @pl.when(j==cut[1]-1)
    def _():
        def body(r):
            x=tok_ref[r,:].astype(F32)+0.5*(acc_ref[r,:]+row(Rows.outer))
            x1_ref[r,:]=x
            xhat,_r=stats(x)
            hid1_ref[r,:]=(xhat*row(Rows.gain+1)+row(Rows.shift+1)).astype(BF)
        chunks(steps,body)
    def stream(w,lo,n,tau0,use):
        @pl.when((j>=lo)&(j<lo+n))
        def _():
            i=j-lo; slot=lax.rem(tau0+i,2)
            column(w,i,slot).wait()
            @pl.when(i+1<n)
            def _(): column(w,i+1,lax.rem(tau0+i+1,2)).start()
            use(i,slot)
    def after(step,w,tau):
        @pl.when(j==step)
        def _(): column(w,0,lax.rem(tau,2)).start()
    def here(i): return pl.ds(al(i*tile,tile),tile)
    def pack(i,slot):
        v=nn(hid1_ref[...],wa(slot))
        per=width//tile
        @pl.when(i<per)
        def _(): packed_ref[:,here(i)]=(v+vec_ref[Rows.packed:Rows.packed+1,here(lax.rem(i,per))]).astype(BF)
        @pl.when((i>=per)&(i<2*per))
        def _(): packed_ref[:,here(i)]=v.astype(BF)
        @pl.when(i>=2*per)
        def _(): packed_ref[:,here(i)]=(v+vec_ref[Rows.packed+1:Rows.packed+2,here(lax.rem(i,per))]).astype(BF)
    stream(ai,cut[1],B,F,pack)
    @pl.when((j>=cut[2])&(j<cut[3]))
    def _():
        h=j-cut[2]
        for a in range(3): qkv_ref[a]=packed_ref[:,pl.ds(al(a*width+h*128,128),128)]
        scale=1.0/math.sqrt(size)
        sl=[slice(i*QB,(i+1)*QB) for i in range(steps//QB)]; outs=[]
        for hh in range(128//size):
            cols=slice(hh*size,(hh+1)*size)
            rels=[nn(qkv_ref[0,r,cols],rel_ref[i]) for i,r in enumerate(sl)]
            rels=[pltpu.roll(x,0,1,stride=1,stride_axis=0)[:,:steps] for x in rels]
            ss=[(nt(qkv_ref[0,r,cols],qkv_ref[1,:,cols])+x)*scale+mask_ref[0:1,:] for r,x in zip(sl,rels)]
            es=[jnp.exp(s-jnp.max(s,axis=1,keepdims=True)) for s in ss]
            ps=[(e*(1.0/jnp.sum(e,axis=1,keepdims=True))).astype(BF) for e in es]
            for r,p in zip(sl,ps): p_ref[hh,r,:]=p
            outs.append(jnp.concatenate([nn(p,qkv_ref[2,:,cols]).astype(BF) for p in ps],axis=0))
        mixed_ref[:,pl.ds(al(h*128,128),128)]=jnp.concatenate(outs,axis=1)
    def join(i,slot):
        x2_ref[:,here(i)]=x1_ref[:,here(i)]+nn(mixed_ref[...],wa(slot))+vec_ref[Rows.mixed:Rows.mixed+1,here(i)]
        @pl.when(i==M0-1)
        def _():
            def body(r):
                xhat,_r=stats(x2_ref[r,:])
                chid_ref[r,:]=(xhat*row(Rows.gain+2)+row(Rows.shift+2)).astype(BF)
            chunks(steps,body)
    stream(ao,cut[3],M0,F+B,join)
    def raise_(i,slot):
        wide_ref[:,here(i)]=nn(chid_ref[...],wa(slot))
        @pl.when(i==M1-1)
        def _():
            def gate(k,c):
                r=pl.ds(pl.multiple_of(k*CH,CH),CH)
                a=wide_ref[r,:width]; b=wide_ref[r,width:]
                up_ref[r,:width]=a.astype(BF); up_ref[r,width:]=b.astype(BF)
                pad_ref[pl.ds(pl.multiple_of(k*CH+PAD,PAD),CH),:]=a*sigmoid(b)*valid_ref[r,0:1]
                return c
            lax.fori_loop(0,steps//CH,gate,0)
            weights=vec_ref.at[Rows.taps:Rows.taps+32]
            def conv(cols):
                for t0 in range(0,steps,RC):
                    depth_ref[t0:t0+RC,cols]=slide(pad_ref,weights,lambda k:k+PAD-taps+1,taps,t0,cols)
            over_columns(width,conv)
            def body(r):
                xhat,_r=stats(depth_ref[r,:])
                z=xhat*row(Rows.gain+3)+row(Rows.shift+3)
                cact_ref[r,:]=(z*sigmoid(z)).astype(BF)
            chunks(steps,body)
    stream(pi,cut[4],M1,F+B+M0,raise_)
    def lower(i,slot):
        x3_ref[:,here(i)]=x2_ref[:,here(i)]+nn(cact_ref[...],wa(slot))
        @pl.when(i==M2-1)
        def _():
            def body(r):
                xhat,_r=stats(x3_ref[r,:])
                hid4_ref[r,:]=(xhat*row(Rows.gain+4)+row(Rows.shift+4)).astype(BF)
            chunks(steps,body)
            acc_ref[...]=jnp.zeros_like(acc_ref)
    stream(po,cut[5],M2,F+B+M0+M1,lower)
    ticks()
    tau=F+B+M0+M1+M2
    after(cut[1]-1,ai,F); after(cut[3]-1,ao,F+B); after(cut[4]-1,pi,F+B+M0); after(cut[5]-1,po,F+B+M0+M1)
    @pl.when(j==cut[6]-1)
    def _():
        comm.run(comm.ticks-1,1)
        column(fi1,0,tau%2).start(); band(fo1,0,0).start()
    @pl.when(j>=cut[6])
    def _(): feed_tile(j-cut[6],tau+j-cut[6],1,hid4_ref,act1_ref,dsl1_ref,fi1,fo1)
    @pl.when(j==cut[7]-1)
    def _():
        s5_ref[...]=jnp.zeros_like(s5_ref)
        def body(r):
            y=x3_ref[r,:]+0.5*(acc_ref[r,:]+row(Rows.outer+1))
            xhat,rstd=stats(y)
            ok=valid_ref[r,0:1]
            gain=row(Rows.gain+5)
            res_ref[r,:]=((xhat*gain+row(Rows.shift+5))*ok).astype(BF)
            dy=cot_ref[r,:].astype(F32)*ok
            dx4_ref[r,:]=norm_back(dy,gain,xhat,rstd)
            s5_ref[0]+=fold(dy*xhat)
            s5_ref[1]+=fold(dy)
        chunks(steps,body)

LAG=2; CUTS=[1,8,8,6,2,4,2,8,8]; MODES=['h','qhhqhhqh','hqhhqhhq','hhqhhq','hq','hhqh','hq','hhqhhqhh','qhhqhhqh']
def early(S,vectors,tokens,cot,valid,mask,table,pick,heads,weights,cid):
    steps,width=tokens.shape; tile=512; taps=vectors[-1].shape[0]; L=vectors[0].shape[1]
    comm=Gather(S,[(Rows.count,L)]+weights,cuts=CUTS,modes=MODES,lag=LAG)
    hidden=comm.shapes[1][1]; size=width//heads
    F,B,A=hidden//tile,comm.shapes[3][1]//tile,width//128
    M=[comm.shapes[i][1]//tile for i in (4,5,6)]
    assert comm.shapes[2][0]*S==hidden and tile==hidden//S
    cut=np.cumsum([0,F,B,A]+M+[F]).tolist()
    within=lambda lo,n:(lambda j:jnp.minimum(jnp.maximum(j-lo,0),n-1))
    f0,at,f1=within(0,F),within(cut[2],A),within(cut[6],F)
    ins=list(vectors)+[tokens,cot,valid,mask,table,pick]
    D=jax.ShapeDtypeStruct
    b=D((steps,width),BF); f=D((steps,width),F32); hid=D((steps,hidden),BF)
    outs=[b,hid,hid,f,b,D((steps,3*width),BF),b,D((heads,steps,steps),BF),f,b,D((steps,2*width),BF),f,b,f,b,hid,hid,f,b,D((2,8,width),F32),D((Rows.count,width),F32)]
    specs=[whole(o.shape) for o in outs]
    for i,t in ((1,f0),(2,f0),(15,f1),(16,f1)): specs[i]=pl.BlockSpec((steps,tile),lambda j,t=t:(0,t(j)))
    specs[7]=pl.BlockSpec((128//size,steps,steps),lambda j:(at(j),0,0))
    V=pltpu.VMEM; sem=lambda n: pltpu.SemaphoreType.DMA((n,))
    scratch=[V((Rows.count,L),F32),V(comm.out_shapes[0].shape,BF),sem(1),V((steps,width),F32),V((2,)+comm.out_shapes[1].shape[:-1]+(tile,),BF),V((2,)+comm.out_shapes[2].shape[2:],BF),sem(2),sem(2),
        V((steps//QB,size,steps+QB),BF),V((3,steps,128),BF),V((steps+PAD,width),F32),V((steps,2*width),F32)]
    out=call(functools.partial(early_kernel,heads,taps),'gather_and_forward',(cut[-1],),ins,[whole(a.shape) for a in ins],outs,specs,scratch,comm,cid)
    return out[0],[a.reshape(-1,a.shape[-1]) for a in out[1]]


def local(S,R,tokens,lengths,cotangent,norm_gain,norm_shift,feed_in,feed_in_bias,feed_out,feed_out_bias,attention_in,attention_in_bias,attention_out,attention_out_bias,relative_table,pointwise_in,depthwise,pointwise_out):
    steps,width=tokens.shape; taps=depthwise.shape[0]
    live=jnp.arange(steps,dtype=jnp.int32)<lengths[0]
    valid=jnp.broadcast_to(live.astype(F32)[:,None],(steps,128))
    mask=jnp.broadcast_to(jnp.where(live,0.0,-1e30).astype(F32)[None,:],(8,steps))
    rows=relative_table.shape[0]
    table=jnp.pad(relative_table,((0,128-rows),(0,0)))
    pick=jnp.asarray(picker_table(steps,QB).astype(np.float32)).astype(BF)
    vectors=[norm_gain,norm_shift,feed_in_bias,feed_out_bias,attention_in_bias,attention_out_bias.reshape(1,-1),depthwise]
    weights=[(feed_in,0),(feed_out,0),attention_in,attention_out,pointwise_in,pointwise_out,(feed_in,1),(feed_out,1)]
    outs,full=early(S,vectors,tokens,cotangent,valid,mask,table,pick,HEADS,weights,0)
    hid0,act0,dsl0,x1,hid1,packed,mixed,p,x2,chid,up,depth,cact,x3,hid4,act1,dsl1,dx4,result,s5,vec=outs
    fi0,fo0,ai,ao,pi,po,fi1,fo1=full[1:]
    shapes=[feed_in.shape,feed_out.shape]+[a.shape for a in (attention_in,attention_out,pointwise_in,pointwise_out)]+[SUB]
    rest=[dx4,x3,x2,x1,hid4,hid1,hid0,chid,cact,mixed,up,depth,act1,act0,dsl1,dsl0,fi1,fo1,ai,ao,pi,po,fi0,fo0]
    (dtok,),outs=backward(S,packed,p,table,pick,HEADS,vec,valid,tokens,s5,rest,taps,shapes,1)
    sums=list(outs[:7])+[outs[-1]]
    if R>4:
        groups=[[g*4+i for g in range(R//4)] for i in range(4)]
        sums=[lax.psum(a,'rep',axis_index_groups=groups) for a in sums]
    gfi,gfo,gai,gao,gpi,gpo,small,common=[a.astype(F32) for a in sums]
    L=norm_gain.shape[1]
    ggain,gshift,gbout,gpbias,gmbias=[small[a:b,:L] for a,b in ((0,6),(6,12),(12,14),(14,16),(16,17))]
    gbin=small[17:19]; gdw=small[32:32+taps,:L]
    gtab=common.reshape(-1,SUB[1])[:rows,:relative_table.shape[1]]
    return (result,dtok,ggain,gshift,gfi,gbin,gfo,gbout,gai,gpbias,gao,gmbias[0],gtab,gpi,gdw,gpo)

HEADS=16

def solution(mesh):
    R,S=mesh.shape['rep'],mesh.shape['shard']
    rows=P(('rep','shard'),None)
    last,mid,first=P(None,'shard'),P(None,'shard',None),P('shard',None)
    weights=(last,last,mid,last,mid,last,first,last,first,P('shard'),P(),first,last,first)
    return jax.shard_map(functools.partial(local,S,R),mesh=mesh,in_specs=(rows,P(('rep','shard')),rows)+weights,out_specs=(rows,rows)+weights,check_vma=False)
```
